32 devices in a mesh: narrow: 4 (over y, core), wide: 8 (over z, x).
Axes of the slice: x: 2, y: 2, z: 4, core: 2. Of those that a mesh axis runs over, the one named last changes fastest.
Arguments:
- tokens: bfloat16 [8192, 2048], P(('narrow', 'wide')), may hold values from -6 to 6
- attention_gain: bfloat16 [2048], replicated, may hold values from 0.099609375 to 1.8984375
- query_weight: bfloat16 [2048, 2048], P(None, 'wide'), may hold values from -0.125 to 0.125
- key_weight: bfloat16 [2048, 512], replicated, may hold values from -0.125 to 0.125
- value_weight: bfloat16 [2048, 512], replicated, may hold values from -0.125 to 0.125
- query_gain: bfloat16 [64], replicated, may hold values from 0.099609375 to 1.8984375
- key_gain: bfloat16 [64], replicated, may hold values from 0.099609375 to 1.8984375
- output_weight: bfloat16 [2048, 2048], P('wide'), may hold values from -0.75 to 0.75
- feedforward_gain: bfloat16 [2048], replicated, may hold values from 0.099609375 to 1.8984375
- gate_weight: bfloat16 [2048, 8192], P(None, 'wide'), may hold values from -0.125 to 0.125
- up_weight: bfloat16 [2048, 8192], P(None, 'wide'), may hold values from -0.125 to 0.125
- down_weight: bfloat16 [8192, 2048], P('wide'), may hold values from -0.0625 to 0.0625
- cotangent: bfloat16 [8192, 2048], P(('narrow', 'wide')), may hold values from -6 to 6
- corpus_tags: int32 [8192], P(('narrow', 'wide')), may hold values from 0 to 7, as said below
- segments: int32 [4, 2048], P('narrow'), may hold values from 0 to 7, never falling along the last dimension, each value on 1 to 1024 neighbouring positions
Outputs:
- block_output: bfloat16 [8192, 2048], P(('narrow', 'wide'))
- tokens_gradient: bfloat16 [8192, 2048], P(('narrow', 'wide'))
- attention_gain_gradient: float32 [2048], P('wide')
- query_weight_gradient: float32 [2048, 2048], P(None, 'wide')
- key_weight_gradient: float32 [2048, 512], P(None, 'wide')
- value_weight_gradient: float32 [2048, 512], P(None, 'wide')
- query_gain_gradient: float32 [64], P('wide')
- key_gain_gradient: float32 [64], P('wide')
- output_weight_gradient: float32 [2048, 2048], P('wide')
- feedforward_gain_gradient: float32 [2048], P('wide')
- gate_weight_gradient: float32 [2048, 8192], P(None, 'wide')
- up_weight_gradient: float32 [2048, 8192], P(None, 'wide')
- down_weight_gradient: float32 [8192, 2048], P('wide')
The draws below stay inside these ranges and needn't reach their ends.
Inputs may be any that keep to these rules, and one draw needn't show every extreme that they name: `corpus_tags`: every corpus has at least one token. `segments`: along each sequence the document number never falls; a document has at most 1024 positions.
All inputs are finite; a program needn't handle non-finite values.
Results may differ from the reference program's by a relative error of at most 0.025.
Values may be sent and summed in bfloat16 or wider, within the bound.
A program may use at most 512 MiB of HBM per device.

```python
import math
import jax
import jax.numpy as jnp
import numpy as np
from jax import lax

D = 2048
QH = 32
KVH = 8
HD = 64
FF = 8192
SEQ = 2048
CORPORA = 8
TOKENS = 8192
NSEQ = 4


def draw_corpus_tags(key, part):
    row_index = jnp.arange(TOKENS, dtype=jnp.int32)
    upper_bound = 1 + row_index * CORPORA // TOKENS
    raw_values = jax.random.randint(key, (TOKENS,), 0, 840000, dtype=jnp.int32)
    tagged = raw_values % upper_bound
    tail_start = TOKENS - CORPORA
    return jnp.where(row_index >= tail_start, row_index - tail_start, tagged).astype(jnp.int32)


def levels(own_key, shape, split, low, top_value):
    loudness, own = 1.0, jax.random.fold_in(own_key, 6)
    for position, blocks in split:
        steps = jnp.exp(jax.random.uniform(jax.random.fold_in(own, position), (blocks,), jnp.float32, low / len(split), top_value / len(split)))
        loudness = loudness * jnp.repeat(steps, shape[position] // blocks).reshape([-1 if axis == position else 1 for axis in range(len(shape))])
    return loudness


def profile(number_of, total, bound, skew):
    portions = [(1 << 20) // math.isqrt(grade ** skew) + 1 for grade in range(2, number_of + 1)]
    spare, holding = total - bound - (number_of - 1), [1] * (number_of - 1)
    while spare > 0:
        movable = [i for i in range(number_of - 1) if holding[i] < bound]
        whole, budget = sum([portions[i] for i in movable]), spare
        for i in movable:
            extra = min(bound - holding[i], max(1, budget * portions[i] // whole), spare)
            holding[i] = holding[i] + extra
            spare = spare - extra
    return np.array([bound] + holding)


def uneven(own_key, count, total, bound, slope):
    if count == 2:
        one = jax.random.randint(own_key, (), max(1, total - bound), min(bound, total - 1) + 1)
        return jnp.stack([one, total - one])
    tallies = jnp.asarray(profile(count, total, bound, slope), jnp.int32)
    couples = (count - 1) // 2
    source_of, receiver = tallies[1:1 + 2 * couples:2], tallies[2:2 + 2 * couples:2]
    room = jnp.minimum(source_of - 1, bound - receiver)
    moved = jax.random.randint(jax.random.fold_in(own_key, 1), (couples,), 0, 1 << 20) % (room + 1)
    tallies = tallies.at[1:1 + 2 * couples:2].set(source_of - moved).at[2:2 + 2 * couples:2].set(receiver + moved)
    return tallies[jax.random.permutation(jax.random.fold_in(own_key, 2), count)]


def normal_values(key, dims, scale, reach, pieces=(), kind=jnp.bfloat16):
    level = levels(key, dims, pieces, -0.22, 0.18) if pieces else 1.0
    values = jax.random.normal(key, dims, jnp.float32) * scale * level
    return jnp.minimum(jnp.maximum(values, -reach), reach).astype(kind)


def setup_inputs(seed: int = 0) -> dict:
    key_list = jax.random.split(jax.random.key(seed), 16)
    tokens = normal_values(key_list[0], (TOKENS, D), 1.0, 6.0, ((0, 32),))
    attention_gain = jnp.clip(1.0 + 0.18 * jax.random.normal(key_list[1], (D,), jnp.float32), 0.099609375, 1.8984375).astype(jnp.bfloat16)
    query_weight = normal_values(key_list[2], (D, QH * HD), D ** -0.5, 0.125, ((1, 8),))
    key_weight = normal_values(key_list[3], (D, KVH * HD), D ** -0.5, 0.125)
    value_weight = normal_values(key_list[4], (D, KVH * HD), D ** -0.5, 0.125)
    query_gain = jnp.clip(1.0 + 0.18 * jax.random.normal(key_list[5], (HD,), jnp.float32), 0.099609375, 1.8984375).astype(jnp.bfloat16)
    key_gain = jnp.clip(1.0 + 0.18 * jax.random.normal(key_list[6], (HD,), jnp.float32), 0.099609375, 1.8984375).astype(jnp.bfloat16)
    output_weight = normal_values(key_list[7], (QH * HD, D), (QH * HD // 32) ** -0.5, 0.75, ((0, 8),))
    feedforward_gain = jnp.clip(1.0 + 0.18 * jax.random.normal(key_list[8], (D,), jnp.float32), 0.099609375, 1.8984375).astype(jnp.bfloat16)
    gate_weight = normal_values(key_list[9], (D, FF), D ** -0.5, 0.125, ((1, 8),))
    up_weight = normal_values(key_list[10], (D, FF), D ** -0.5, 0.125, ((1, 8),))
    down_weight = normal_values(key_list[11], (FF, D), FF ** -0.5, 0.0625, ((0, 8),))
    cotangent = normal_values(key_list[12], (TOKENS, D), 1.0, 6.0, ((0, 32),))
    corpus_tags = draw_corpus_tags(jax.random.fold_in(key_list[15], 71), 0)
    segments = jax.vmap(lambda own: jnp.searchsorted(jnp.cumsum(uneven(own, 8, SEQ, SEQ // 2, 2)), jnp.arange(SEQ), side="right"))(jax.random.split(key_list[14], NSEQ)).reshape((NSEQ, SEQ)).astype(jnp.int32)
    return dict(tokens=tokens, attention_gain=attention_gain, query_weight=query_weight, key_weight=key_weight, value_weight=value_weight, query_gain=query_gain, key_gain=key_gain, output_weight=output_weight, feedforward_gain=feedforward_gain, gate_weight=gate_weight, up_weight=up_weight, down_weight=down_weight, cotangent=cotangent, corpus_tags=corpus_tags, segments=segments)


@jax.custom_vjp
def low(v):
    return lax.optimization_barrier(v.astype(jnp.bfloat16)).astype(jnp.float32)

@jax.custom_vjp
def low_back(v):
    return v

def low_keep(v):
    return (low(v), None)

def low_pass(kept, grad):
    return (grad,)

def back_keep(v):
    return (v, None)

def back_low(kept, grad):
    return (low(grad),)
low.defvjp(low_keep, low_pass)
low_back.defvjp(back_keep, back_low)
epsilon = 1e-06
rope_base = 10000.0

def exact_product(left, right):
    return jnp.dot(left, right, precision=lax.Precision.HIGHEST, preferred_element_type=jnp.float32)

def norm_scale(values, scale_gain):
    return values * lax.rsqrt(lax.optimization_barrier(jnp.mean(values * values, axis=-1, keepdims=True)) + epsilon) * scale_gain

def rotary_tables(row_total, head_size):
    positions = (jnp.arange(row_total) % SEQ).astype(jnp.float32)
    exponents = jnp.arange(head_size // 2).astype(jnp.float32) * (2.0 / head_size)
    frequency = rope_base ** (-exponents)
    angles = positions[:, None] * frequency[None, :]
    return (jnp.cos(angles), jnp.sin(angles))

def rotate(values, cosine_table, sine_table):
    half_width = values.shape[-1] // 2
    table_shape = (values.shape[0],) + (1,) * (values.ndim - 2) + (half_width,)
    cosine_part = cosine_table.reshape(table_shape)
    sine_part = sine_table.reshape(table_shape)
    first_half = values[..., :half_width]
    second_half = values[..., half_width:]
    return jnp.concatenate([first_half * cosine_part - second_half * sine_part, second_half * cosine_part + first_half * sine_part], axis=-1)

def attend_one(query_rows, key_rows, value_rows, segment_row):
    scores = low_back(exact_product(query_rows, key_rows.T) * HD ** (-0.5))
    positions = jnp.arange(SEQ)
    allowed = (positions[None, :] <= positions[:, None]) & (segment_row[None, :] == segment_row[:, None])
    masked = jnp.where(allowed, scores, -1e+30)
    shifted = jnp.exp(masked - lax.optimization_barrier(jnp.max(masked, axis=-1, keepdims=True)))
    probability = shifted / lax.optimization_barrier(jnp.sum(shifted, axis=-1, keepdims=True))
    return exact_product(low(probability), value_rows)
attend_saved = jax.checkpoint(attend_one)

def by_head(values):
    return values.reshape(NSEQ, SEQ, QH, HD).transpose(0, 2, 1, 3).reshape(NSEQ * QH, SEQ, HD)

def make_forward(segments):

    def forward(tokens, attention_gain, query_weight, key_weight, value_weight, query_gain, key_gain, output_weight, feedforward_gain, gate_weight, up_weight, down_weight):
        row_total = tokens.shape[0]
        cosine_table, sine_table = rotary_tables(row_total, HD)
        group_size = QH // KVH
        hidden_one = low(norm_scale(tokens, attention_gain))
        queries = low_back(exact_product(hidden_one, query_weight).reshape(row_total, QH, HD))
        keys_raw = exact_product(hidden_one, key_weight).reshape(row_total, KVH, HD)
        values_raw = exact_product(hidden_one, value_weight).reshape(row_total, KVH, HD)
        keys_all = low_back(jnp.repeat(keys_raw, group_size, axis=1))
        values_all = low(low_back(jnp.repeat(values_raw, group_size, axis=1)))
        query_rot = low(rotate(norm_scale(queries, query_gain), cosine_table, sine_table))
        key_rot = low(rotate(norm_scale(keys_all, key_gain), cosine_table, sine_table))
        segment_rows = jnp.repeat(segments, QH, axis=0)
        attended = lax.map(lambda packed: attend_saved(*packed), (by_head(query_rot), by_head(key_rot), by_head(values_all), segment_rows))
        mixed_heads = attended.reshape(NSEQ, QH, SEQ, HD).transpose(0, 2, 1, 3).reshape(row_total, QH * HD)
        mixed_low = low(low_back(mixed_heads))
        branch = low_back(exact_product(mixed_low, output_weight))
        middle = tokens + branch
        hidden_two = low(norm_scale(middle, feedforward_gain))
        gate_values = low_back(exact_product(hidden_two, gate_weight))
        up_values = low_back(exact_product(hidden_two, up_weight))
        activated = low(gate_values * lax.logistic(gate_values) * up_values)
        return middle + low_back(exact_product(activated, down_weight))
    return forward

def reference(tokens, attention_gain, query_weight, key_weight, value_weight, query_gain, key_gain, output_weight, feedforward_gain, gate_weight, up_weight, down_weight, cotangent, corpus_tags, segments):
    tag_hits = corpus_tags[:, None] == jnp.arange(CORPORA, dtype=jnp.int32)[None, :]
    counts = lax.optimization_barrier(jnp.sum(tag_hits.astype(jnp.float32), axis=0))
    corpus_scale = jnp.sqrt(TOKENS / (CORPORA * counts))
    row_weight = lax.optimization_barrier(jnp.sum(jnp.where(tag_hits, corpus_scale[None, :], 0.0), axis=1))
    inputs = [array_in.astype(jnp.float32) for array_in in (tokens, attention_gain, query_weight, key_weight, value_weight, query_gain, key_gain, output_weight, feedforward_gain, gate_weight, up_weight, down_weight)]
    result, pullback = jax.vjp(make_forward(segments), *inputs)
    grads = pullback(cotangent.astype(jnp.float32) * row_weight[:, None])
    return (result.astype(jnp.bfloat16), grads[0].astype(jnp.bfloat16), grads[1], grads[2], grads[3], grads[4], grads[5], grads[6], grads[7], grads[8], grads[9], grads[10], grads[11])
```

```python
import numpy as np

import jax
import jax.numpy as jnp
from jax import lax
from jax.experimental import pallas as pl
from jax.experimental.pallas import tpu as pltpu
from jax.sharding import PartitionSpec as P

SEQ = 2048
epsilon = 1e-06
rope_base = 10000.0
BLOCK = 256
NEG = -1e30


def rope_tables(head_size):
    positions = np.arange(SEQ, dtype=np.float32)
    exponents = np.arange(head_size // 2, dtype=np.float32) * np.float32(2.0 / head_size)
    frequency = np.power(np.float32(rope_base), -exponents).astype(np.float32)
    angles = (positions[:, None] * frequency[None, :]).astype(np.float32)
    cosine, sine = np.cos(angles).astype(np.float32), np.sin(angles).astype(np.float32)
    return (
        np.concatenate([cosine, cosine], axis=1),
        np.concatenate([-sine, sine], axis=1),
    )


def dot_nn(left, right):
    return jnp.dot(left, right, preferred_element_type=jnp.float32)


def dot_nt(left, right):
    return lax.dot_general(
        left, right, (((1,), (1,)), ((), ())), preferred_element_type=jnp.float32
    )


def lane_ids(shape):
    return lax.broadcasted_iota(jnp.int32, shape, 1)


def group_ones(width, head_size):
    rows = lax.broadcasted_iota(jnp.int32, (width, width), 0) // head_size
    columns = lax.broadcasted_iota(jnp.int32, (width, width), 1) // head_size
    return jnp.where(rows == columns, 1.0, 0.0).astype(jnp.bfloat16)


def group_sum(values, ones):
    top = values.astype(jnp.bfloat16)
    rest = (values - top.astype(jnp.float32)).astype(jnp.bfloat16)
    return dot_nn(top, ones) + dot_nn(rest, ones)


def swap_halves(values, head_size):
    width, half = values.shape[1], head_size // 2
    if width == head_size:
        return jnp.concatenate([values[:, half:], values[:, :half]], axis=1)
    ahead = pltpu.roll(values, width - half, 1)
    behind = pltpu.roll(values, half, 1)
    return jnp.where(lane_ids(values.shape) % head_size < half, ahead, behind)


def tiled(values, count):
    return jnp.concatenate([values] * count, axis=1) if count > 1 else values


def split_raw(raw, width, head_size, heads):
    query = raw[:, :width]
    key = tiled(raw[:, width : width + head_size], heads)
    value = tiled(raw[:, width + head_size :], heads)
    return query, key, value


def head_masks(block, width, head_size, heads):
    group = lane_ids((block, width)) // head_size
    return [group == h for h in range(heads)]


def attention_forward(raw, query_gain, key_gain, segments, first_block):
    head_size = query_gain.shape[0]
    rows = raw.shape[0]
    heads = raw.shape[1] // head_size - 2
    width = heads * head_size
    seqs, blocks, block = rows // SEQ, SEQ // BLOCK, BLOCK
    scale = head_size ** (-0.5)

    def kernel(
        first_ref, raw_ref, qg_ref, kg_ref, cos_ref, sin_ref, segq_ref, segk_ref,
        mixed_ref, lse_ref, query_ref, key_ref, value_ref, keyt_ref,
        keys, values_t, masked, top, total, acc,
    ):
        s, i = pl.program_id(0), pl.program_id(1)
        cosine, sine = tiled(cos_ref[...], heads), tiled(sin_ref[...], heads)
        ones = group_ones(width, head_size)
        query, key, value = split_raw(raw_ref[...], width, head_size, heads)

        def norm_rope(x, gain):
            x = x * lax.rsqrt(group_sum(x * x, ones) * (1.0 / head_size) + epsilon) * gain
            return x * cosine + swap_halves(x, head_size) * sine

        query_low = norm_rope(query, qg_ref[...]).astype(jnp.bfloat16)
        key_rot = norm_rope(key, kg_ref[...])
        key_low = key_rot.astype(jnp.bfloat16)
        query_ref[...] = query_low
        key_ref[...] = key_low
        value_ref[...] = value.astype(jnp.bfloat16)
        keyt_ref[0] = jnp.transpose(key_rot)[:head_size].astype(jnp.bfloat16)
        keys[pl.ds(pl.multiple_of(i * block, block), block), :] = key_low
        values_t[i] = jnp.transpose(value)[:head_size].astype(jnp.bfloat16)
        scaled = query_low * jnp.bfloat16(scale)
        zero = jnp.zeros_like(scaled)
        for h, mask in enumerate(head_masks(block, width, head_size, heads)):
            masked[h] = jnp.where(mask, scaled, zero)
        top[...] = jnp.full_like(top, NEG)
        total[...] = jnp.zeros_like(total)
        acc[...] = jnp.zeros_like(acc)
        query_pos = i * block + lax.broadcasted_iota(jnp.int32, (block, block), 1)
        segment_query = segq_ref[0]

        def step(j, carry):
            at = pl.multiple_of(j * block, block)
            key_pos = at + lax.broadcasted_iota(jnp.int32, (block, block), 0)
            allowed = (key_pos <= query_pos) & (segk_ref[pl.ds(at, block), :] == segment_query)
            bias = jnp.where(allowed, 0.0, NEG)
            key_block = keys[pl.ds(at, block), :]
            value_t = values_t[j]
            for h in range(heads):
                scores = dot_nt(key_block, masked[h]) + bias
                before = top[h : h + 1, :]
                now = jnp.maximum(before, jnp.max(scores, axis=0, keepdims=True))
                shifted = jnp.exp(scores - now)
                fade = jnp.exp(before - now)
                top[h : h + 1, :] = now
                total[h : h + 1, :] = fade * total[h : h + 1, :] + jnp.sum(
                    shifted, axis=0, keepdims=True
                )
                span = slice(h * head_size, (h + 1) * head_size)
                acc[span, :] = fade * acc[span, :] + dot_nn(value_t, shifted.astype(jnp.bfloat16))
            return carry

        lax.fori_loop(first_ref[s, i], i + 1, step, 0)
        for h in range(heads):
            span = slice(h * head_size, (h + 1) * head_size)
            acc[span, :] = acc[span, :] / total[h : h + 1, :]
        mixed_ref[...] = jnp.transpose(acc[...]).astype(jnp.bfloat16)
        lse_ref[...] = top[...] + jnp.log(jnp.maximum(total[...], 1e-30))

    cosine, sine = rope_tables(head_size)
    at_rows = lambda s, i, first: (s * blocks + i, 0)
    fixed = lambda s, i, first: (0, 0)
    at_lanes = lambda s, i, first: (0, s * blocks + i)
    low = jnp.bfloat16
    pairs = blocks * (blocks + 1) // 2 * seqs * heads
    return pl.pallas_call(
        kernel,
        grid_spec=pltpu.PrefetchScalarGridSpec(
            num_scalar_prefetch=1,
            grid=(seqs, blocks),
            in_specs=[
                pl.BlockSpec((block, raw.shape[1]), at_rows),
                pl.BlockSpec((1, width), fixed),
                pl.BlockSpec((1, width), fixed),
                pl.BlockSpec((block, head_size), lambda s, i, first: (i, 0)),
                pl.BlockSpec((block, head_size), lambda s, i, first: (i, 0)),
                pl.BlockSpec((1, 1, block), lambda s, i, first: (s, 0, i)),
                pl.BlockSpec((SEQ, 1), lambda s, i, first: (s, 0)),
            ],
            out_specs=[
                pl.BlockSpec((block, width), at_rows),
                pl.BlockSpec((8, block), at_lanes),
                pl.BlockSpec((block, width), at_rows),
                pl.BlockSpec((block, width), at_rows),
                pl.BlockSpec((block, width), at_rows),
                pl.BlockSpec((1, head_size, block), lambda s, i, first: (s * blocks + i, 0, 0)),
            ],
            scratch_shapes=[
                pltpu.VMEM((SEQ, width), low),
                pltpu.VMEM((blocks, head_size, block), low),
                pltpu.VMEM((heads, block, width), low),
                pltpu.VMEM((8, block), jnp.float32),
                pltpu.VMEM((8, block), jnp.float32),
                pltpu.VMEM((width, block), jnp.float32),
            ],
        ),
        out_shape=[
            jax.ShapeDtypeStruct((rows, width), low),
            jax.ShapeDtypeStruct((8, rows), jnp.float32),
            jax.ShapeDtypeStruct((rows, width), low),
            jax.ShapeDtypeStruct((rows, width), low),
            jax.ShapeDtypeStruct((rows, width), low),
            jax.ShapeDtypeStruct((rows // block, head_size, block), low),
        ],
        compiler_params=pltpu.CompilerParams(vmem_limit_bytes=40 << 20),
        cost_estimate=pl.CostEstimate(
            flops=pairs * block * block * head_size * 8,
            bytes_accessed=rows * width * 16,
            transcendentals=pairs * block * block,
        ),
        name="attention_forward",
    )(
        first_block, raw,
        tiled(query_gain.astype(jnp.float32)[None], heads),
        tiled(key_gain.astype(jnp.float32)[None], heads),
        cosine, sine, segments[:, None, :], segments.reshape(rows, 1),
    )


def attention_backward(
    raw, query_gain, key_gain, segments, first_block, saved, mixed_grad
):
    mixed, lse, query_low, key_low, value_low, key_t = saved
    head_size = query_gain.shape[0]
    rows, width = mixed.shape
    heads = width // head_size
    seqs, blocks, block = rows // SEQ, SEQ // BLOCK, BLOCK
    scale = head_size ** (-0.5)

    def kernel(
        first_ref, raw_ref, qg_ref, kg_ref, cos_ref, sin_ref, segq_ref, segk_ref,
        mixed_ref, lse_ref, query_ref, grad_ref, keys_ref, values_ref, keyt_ref,
        out_ref, qgg_ref, kgg_ref,
        masked, masked_grad, key_sums, value_sums, query_sums, deltas,
    ):
        s, i = pl.program_id(0), blocks - 1 - pl.program_id(1)

        @pl.when(pl.program_id(1) == 0)
        def _():
            key_sums[...] = jnp.zeros_like(key_sums)
            value_sums[...] = jnp.zeros_like(value_sums)

        @pl.when((pl.program_id(1) == 0) & (s == 0))
        def _():
            qgg_ref[...] = jnp.zeros_like(qgg_ref)
            kgg_ref[...] = jnp.zeros_like(kgg_ref)

        query_sums[...] = jnp.zeros_like(query_sums)
        grad = grad_ref[...]
        scaled = query_ref[...] * jnp.bfloat16(scale)
        zero = jnp.zeros_like(scaled)
        for h, mask in enumerate(head_masks(block, width, head_size, heads)):
            span = slice(h * block, (h + 1) * block)
            masked[span, :] = jnp.where(mask, scaled, zero)
            masked_grad[span, :] = jnp.where(mask, grad, zero)
        product = jnp.transpose(grad.astype(jnp.float32) * mixed_ref[...].astype(jnp.float32))
        for h in range(heads):
            deltas[h : h + 1, :] = jnp.sum(
                product[h * head_size : (h + 1) * head_size], axis=0, keepdims=True
            )
        query_pos = i * block + lax.broadcasted_iota(jnp.int32, (block, block), 1)
        segment_query = segq_ref[0]

        def step(j, carry):
            at = pl.multiple_of(j * block, block)
            key_pos = at + lax.broadcasted_iota(jnp.int32, (block, block), 0)
            allowed = (key_pos <= query_pos) & (segk_ref[pl.ds(at, block), :] == segment_query)
            bias = jnp.where(allowed, 0.0, NEG)
            key_block = keys_ref[pl.ds(at, block), :]
            value_block = values_ref[pl.ds(at, block), :]
            key_t = keyt_ref[j]
            lows, grads = [], []
            for h in range(heads):
                span = slice(h * block, (h + 1) * block)
                scores = dot_nt(key_block, masked[span, :]) + bias
                probability = jnp.exp(scores - lse_ref[h : h + 1, :])
                prob_grad = dot_nt(value_block, masked_grad[span, :])
                score_grad = (probability * (prob_grad - deltas[h : h + 1, :])).astype(jnp.bfloat16)
                lows.append(probability.astype(jnp.bfloat16))
                grads.append(score_grad)
                rows_h = slice(h * head_size, (h + 1) * head_size)
                query_sums[rows_h, :] += dot_nn(key_t, score_grad)
            value_sums[pl.ds(at, block), :] += dot_nn(
                jnp.concatenate(lows, axis=1), masked_grad[...]
            )
            key_sums[pl.ds(at, block), :] += dot_nn(jnp.concatenate(grads, axis=1), masked[...])
            return carry

        lax.fori_loop(first_ref[s, i], i + 1, step, 0)
        cosine, sine = tiled(cos_ref[...], heads), tiled(sin_ref[...], heads)
        ones = group_ones(width, head_size)
        query, key, _ = split_raw(raw_ref[...], width, head_size, heads)

        def all_heads(x):
            total = x
            for h in range(1, heads):
                total = total + pltpu.roll(x, h * head_size, 1)
            return total

        def norm_rope_back(x, up, gain):
            unrot = up * cosine - swap_halves(up, head_size) * sine
            inverse = lax.rsqrt(group_sum(x * x, ones) * (1.0 / head_size) + epsilon)
            gain_part = jnp.sum(unrot * x * inverse, axis=0, keepdims=True)
            scaled_up = unrot * gain
            mean = group_sum(scaled_up * x, ones) * (1.0 / head_size)
            return scaled_up * inverse - x * (mean * inverse * inverse * inverse), gain_part

        query_up = jnp.transpose(query_sums[...]) * scale
        query_grad, query_part = norm_rope_back(query, query_up, qg_ref[...])
        here = pl.ds(pl.multiple_of(i * block, block), block)
        key_up = all_heads(key_sums[here, :])
        key_grad, key_part = norm_rope_back(key, key_up, kg_ref[...])
        value_grad = all_heads(value_sums[here, :])
        out_ref[...] = jnp.concatenate(
            [query_grad, key_grad[:, :head_size], value_grad[:, :head_size]], axis=1
        ).astype(jnp.bfloat16)
        qgg_ref[...] += query_part
        kgg_ref[...] += key_part

    cosine, sine = rope_tables(head_size)
    at_rows = lambda s, i, first: (s * blocks + blocks - 1 - i, 0)
    fixed = lambda s, i, first: (0, 0)
    at_lanes = lambda s, i, first: (0, s * blocks + blocks - 1 - i)
    at_seq = lambda s, i, first: (s, 0)
    low = jnp.bfloat16
    pairs = blocks * (blocks + 1) // 2 * seqs * heads
    grads, query_part, key_part = pl.pallas_call(
        kernel,
        grid_spec=pltpu.PrefetchScalarGridSpec(
            num_scalar_prefetch=1,
            grid=(seqs, blocks),
            in_specs=[
                pl.BlockSpec((block, raw.shape[1]), at_rows),
                pl.BlockSpec((1, width), fixed),
                pl.BlockSpec((1, width), fixed),
                pl.BlockSpec((block, head_size), lambda s, i, first: (blocks - 1 - i, 0)),
                pl.BlockSpec((block, head_size), lambda s, i, first: (blocks - 1 - i, 0)),
                pl.BlockSpec((1, 1, block), lambda s, i, first: (s, 0, blocks - 1 - i)),
                pl.BlockSpec((SEQ, 1), at_seq),
                pl.BlockSpec((block, width), at_rows),
                pl.BlockSpec((8, block), at_lanes),
                pl.BlockSpec((block, width), at_rows),
                pl.BlockSpec((block, width), at_rows),
                pl.BlockSpec((SEQ, width), at_seq),
                pl.BlockSpec((SEQ, width), at_seq),
                pl.BlockSpec((blocks, head_size, block), lambda s, i, first: (s, 0, 0)),
            ],
            out_specs=[
                pl.BlockSpec((block, raw.shape[1]), at_rows),
                pl.BlockSpec((1, width), fixed),
                pl.BlockSpec((1, width), fixed),
            ],
            scratch_shapes=[
                pltpu.VMEM((heads * block, width), low),
                pltpu.VMEM((heads * block, width), low),
                pltpu.VMEM((SEQ, width), jnp.float32),
                pltpu.VMEM((SEQ, width), jnp.float32),
                pltpu.VMEM((width, block), jnp.float32),
                pltpu.VMEM((8, block), jnp.float32),
            ],
        ),
        out_shape=[
            jax.ShapeDtypeStruct(raw.shape, low),
            jax.ShapeDtypeStruct((1, width), jnp.float32),
            jax.ShapeDtypeStruct((1, width), jnp.float32),
        ],
        compiler_params=pltpu.CompilerParams(vmem_limit_bytes=48 << 20),
        cost_estimate=pl.CostEstimate(
            flops=pairs * block * block * head_size * 20,
            bytes_accessed=rows * width * 24,
            transcendentals=pairs * block * block,
        ),
        name="attention_backward",
    )(
        first_block, raw,
        tiled(query_gain.astype(jnp.float32)[None], heads),
        tiled(key_gain.astype(jnp.float32)[None], heads),
        cosine, sine, segments[:, None, :], segments.reshape(rows, 1),
        mixed, lse, query_low, mixed_grad, key_low, value_low, key_t,
    )
    return (
        grads,
        jnp.sum(query_part.reshape(heads, head_size), axis=0),
        key_part[0, :head_size],
    )


def first_blocks(segments):
    starts = segments[:, :: BLOCK]
    below = jnp.sum(segments[:, None, :] < starts[:, :, None], axis=-1, dtype=jnp.int32)
    return below // BLOCK

MESH = pl.DeviceIdType.MESH


class Lattice:
    def __init__(self, count):
        self.depth = count // 2
        me = lax.axis_index("wide")
        self.z, self.x = me // 2, me % 2
        self.below = jnp.minimum(self.z, self.depth - 1 - self.z)
        self.low_side = self.z > self.depth - 1 - self.z

    def at(self, z, x):
        return z * 2 + x

    def order(self, m):
        near = m <= 2 * self.below
        r = jnp.where(near, (m + 1) // 2, m - self.below)
        minus = jnp.where(near, m % 2 == 1, self.low_side)
        return jnp.where(minus, self.z - r, self.z + r), r


def greet(lat):
    barrier = pltpu.get_barrier_semaphore()
    last = lat.depth - 1

    def each(act):
        act(lat.at(lat.z, 1 - lat.x))

        @pl.when(lat.z > 0)
        def _():
            act(lat.at(lat.z - 1, lat.x))

        @pl.when(lat.z < last)
        def _():
            act(lat.at(lat.z + 1, lat.x))

    each(lambda who: pl.semaphore_signal(barrier, inc=1, device_id={"wide": who}, device_id_type=MESH))
    pl.semaphore_wait(barrier, 1 + jnp.minimum(lat.z, 1) + jnp.minimum(last - lat.z, 1))


def gather_chunks(lat, full, send_sems, recv_sems, compute):
    z, x, depth = lat.z, lat.x, lat.depth
    last = depth - 1

    def copy(chunk, way, slot, target):
        return pltpu.make_async_remote_copy(
            src_ref=full.at[chunk], dst_ref=full.at[chunk],
            send_sem=send_sems.at[way, slot], recv_sem=recv_sems.at[chunk],
            device_id={"wide": target}, device_id_type=MESH,
        )

    def up(zz):
        return copy(lat.at(zz, x), 0, zz, lat.at(z + 1, x))

    def down(zz):
        return copy(lat.at(zz, x), 1, zz, lat.at(z - 1, x))

    def across(zz):
        return copy(lat.at(zz, x), 2, zz, lat.at(z, 1 - x))

    def arrived(chunk):
        copy(chunk, 2, 0, lat.at(z, 1 - x)).wait_recv()

    @pl.when(z < last)
    def _():
        up(z).start()

    @pl.when(z > 0)
    def _():
        down(z).start()

    across(z).start()

    def step(m, carry):
        zz, r = lat.order(m)
        _, before = lat.order(m - 1)

        @pl.when((m >= 1) & (m < depth) & (r != before))
        def _():
            @pl.when(z - r >= 0)
            def _():
                arrived(lat.at(z - r, x))

                @pl.when(z < last)
                def _():
                    up(z - r).start()

                across(z - r).start()

            @pl.when(z + r <= last)
            def _():
                arrived(lat.at(z + r, x))

                @pl.when(z > 0)
                def _():
                    down(z + r).start()

                across(z + r).start()

        mirror = lat.order(jnp.maximum(m - 1, 0))[0]

        def part(p, carry):
            @pl.when((p == 0) & (m < depth))
            def _():
                pass

            @pl.when((p == 1) & (m >= 1))
            def _():
                arrived(lat.at(mirror, 1 - x))

            @pl.when(((p == 0) & (m < depth)) | ((p == 1) & (m >= 1)))
            def _():
                compute(jnp.where(p == 0, lat.at(zz, x), lat.at(mirror, 1 - x)))

            return carry

        return lax.fori_loop(0, 2, part, carry)

    lax.fori_loop(0, depth + 1, step, 0)

    def settle(zz, carry):
        @pl.when((z < last) & (zz <= z))
        def _():
            up(zz).wait_send()

        @pl.when((z > 0) & (zz >= z))
        def _():
            down(zz).wait_send()

        across(zz).wait_send()
        return carry

    lax.fori_loop(0, depth, settle, 0)


def project_gathered(local, weights, wide_count, collective_id):
    rows, model = local.shape
    columns = weights.shape[1]
    depth = wide_count // 2

    def kernel(local_ref, weights_ref, full_ref, out_ref, full, send_sems, recv_sems, load_sem, store_sems):
        lat = Lattice(wide_count)
        me = lat.at(lat.z, lat.x)
        load = pltpu.make_async_copy(local_ref, full.at[me], load_sem)
        load.start()
        greet(lat)
        load.wait()

        def keep(chunk):
            return pltpu.make_async_copy(full.at[chunk], full_ref.at[chunk], store_sems.at[chunk])

        def compute(chunk):
            keep(chunk).start()
            at = pl.multiple_of(chunk * rows, rows)
            out_ref[pl.ds(at, rows), :] = jnp.dot(
                full[chunk], weights_ref[...], preferred_element_type=jnp.float32
            )

        gather_chunks(lat, full, send_sems, recv_sems, compute)
        lax.fori_loop(0, wide_count, lambda c, carry: (keep(c).wait(), carry)[1], 0)

    full, out = pl.pallas_call(
        kernel,
        in_specs=[pl.BlockSpec(memory_space=pl.ANY), pl.BlockSpec(memory_space=pltpu.VMEM)],
        out_specs=[pl.BlockSpec(memory_space=pl.ANY), pl.BlockSpec(memory_space=pltpu.VMEM)],
        out_shape=[
            jax.ShapeDtypeStruct((wide_count, rows, model), local.dtype),
            jax.ShapeDtypeStruct((wide_count * rows, columns), jnp.float32),
        ],
        scratch_shapes=[
            pltpu.VMEM((wide_count, rows, model), local.dtype),
            pltpu.SemaphoreType.DMA((3, depth)),
            pltpu.SemaphoreType.DMA((wide_count,)),
            pltpu.SemaphoreType.DMA,
            pltpu.SemaphoreType.DMA((wide_count,)),
        ],
        compiler_params=pltpu.CompilerParams(
            collective_id=collective_id, has_side_effects=True, vmem_limit_bytes=32 << 20
        ),
        name="project_gathered",
    )(local, weights)
    return full.reshape(wide_count * rows, model), out


def nt(left, right):
    return lax.dot_general(
        left, right, (((1,), (1,)), ((), ())), preferred_element_type=jnp.float32
    )


def forward_gathered(local, gate_weight, up_weight, down_weight, wide_count, collective_id):
    rows, model = local.shape
    hidden = gate_weight.shape[1]
    depth = wide_count // 2
    tile = min(256, hidden)
    wide_tile = min(512, model)

    def kernel(
        local_ref, gate_ref, up_ref, down_ref, full_ref, gates_ref, ups_ref, acts_ref, downs_ref,
        full, gates, ups, acts, downs, send_sems, recv_sems, load_sem, store_sems,
    ):
        lat = Lattice(wide_count)
        me = lat.at(lat.z, lat.x)
        load = pltpu.make_async_copy(local_ref, full.at[me], load_sem)
        load.start()
        greet(lat)
        load.wait()
        kept = ((full, full_ref), (gates, gates_ref), (ups, ups_ref), (acts, acts_ref), (downs, downs_ref))

        def keep(which, chunk):
            source, target = kept[which]
            return pltpu.make_async_copy(source.at[chunk], target.at[chunk], store_sems.at[which, chunk])

        def compute(chunk):
            keep(0, chunk).start()
            rows_in = full[chunk]

            def inner(t, carry):
                at = pl.ds(pl.multiple_of(t * tile, tile), tile)
                gate = jnp.dot(rows_in, gate_ref[:, at], preferred_element_type=jnp.float32)
                up = jnp.dot(rows_in, up_ref[:, at], preferred_element_type=jnp.float32)
                gates[chunk, :, at] = gate
                ups[chunk, :, at] = up
                acts[chunk, :, at] = (gate * lax.logistic(gate) * up).astype(jnp.bfloat16)
                return carry

            lax.fori_loop(0, hidden // tile, inner, 0)
            for which in (1, 2, 3):
                keep(which, chunk).start()
            act = acts[chunk]

            def outer(t, carry):
                at = pl.ds(pl.multiple_of(t * wide_tile, wide_tile), wide_tile)
                downs[chunk, :, at] = jnp.dot(
                    act, down_ref[:, at], preferred_element_type=jnp.float32
                ).astype(jnp.bfloat16)
                return carry

            lax.fori_loop(0, model // wide_tile, outer, 0)
            keep(4, chunk).start()

        gather_chunks(lat, full, send_sems, recv_sems, compute)
        for which in range(5):
            lax.fori_loop(0, wide_count, lambda c, carry: (keep(which, c).wait(), carry)[1], 0)

    low = jnp.bfloat16
    outs = [
        ((wide_count, rows, model), low),
        ((wide_count, rows, hidden), jnp.float32),
        ((wide_count, rows, hidden), jnp.float32),
        ((wide_count, rows, hidden), low),
        ((wide_count, rows, model), low),
    ]
    vmem = pl.BlockSpec(memory_space=pltpu.VMEM)
    hbm = pl.BlockSpec(memory_space=pl.ANY)
    results = pl.pallas_call(
        kernel,
        in_specs=[hbm, vmem, vmem, vmem],
        out_specs=[hbm] * 5,
        out_shape=[jax.ShapeDtypeStruct(*o) for o in outs],
        scratch_shapes=[pltpu.VMEM(*o) for o in outs]
        + [
            pltpu.SemaphoreType.DMA((3, depth)),
            pltpu.SemaphoreType.DMA((wide_count,)),
            pltpu.SemaphoreType.DMA,
            pltpu.SemaphoreType.DMA((5, wide_count)),
        ],
        compiler_params=pltpu.CompilerParams(
            collective_id=collective_id, has_side_effects=True, vmem_limit_bytes=60 << 20
        ),
        name="forward_gathered",
    )(local, gate_weight, up_weight, down_weight)
    return [r.reshape(wide_count * rows, r.shape[2]) for r in results]


def backward_scattered(
    cot, gates, ups, gate_weight, up_weight, down_weight, wide_count, collective_id
):
    model = cot.shape[1]
    rows = cot.shape[0] // wide_count
    hidden = gate_weight.shape[1]
    depth = wide_count // 2
    tile = min(256, hidden)
    wide_tile = min(512, model)
    low = jnp.bfloat16

    def kernel(
        cot_ref, gates_ref, ups_ref, gate_ref, up_ref, down_ref, sum_ref, gate_low_ref, up_low_ref,
        cots, gate_in, up_in, gate_low, up_low, foreign, own, crossed, from_low, from_high,
        in_sems, out_sems, cross_send, cross_recv, chain_send, low_recv, high_recv,
    ):
        lat = Lattice(wide_count)
        z, x, last = lat.z, lat.x, depth - 1

        def place(e):
            zz = lat.order(depth - 1 - e % depth)[0]
            return zz, lat.at(zz, jnp.where(e < depth, 1 - x, x))

        def loads(e):
            slot = e % 2
            chunk = place(e)[1]
            return [
                pltpu.make_async_copy(source.at[chunk], target.at[slot], in_sems.at[k, slot])
                for k, (source, target) in enumerate(
                    ((cot_ref, cots), (gates_ref, gate_in), (ups_ref, up_in))
                )
            ]

        def stores(e):
            slot = e % 2
            chunk = place(e)[1]
            return [
                pltpu.make_async_copy(source.at[slot], target.at[chunk], out_sems.at[k, slot])
                for k, (source, target) in enumerate(((gate_low, gate_low_ref), (up_low, up_low_ref)))
            ]

        def cross(zz):
            return pltpu.make_async_remote_copy(
                src_ref=foreign.at[zz], dst_ref=crossed.at[zz],
                send_sem=cross_send.at[zz], recv_sem=cross_recv.at[zz],
                device_id={"wide": lat.at(z, 1 - x)}, device_id_type=MESH,
            )

        def rise(zz):
            return pltpu.make_async_remote_copy(
                src_ref=own.at[zz], dst_ref=from_low.at[zz],
                send_sem=chain_send.at[zz], recv_sem=low_recv.at[zz],
                device_id={"wide": lat.at(z + 1, x)}, device_id_type=MESH,
            )

        def sink(zz):
            return pltpu.make_async_remote_copy(
                src_ref=own.at[zz], dst_ref=from_high.at[zz],
                send_sem=chain_send.at[zz], recv_sem=high_recv.at[zz],
                device_id={"wide": lat.at(z - 1, x)}, device_id_type=MESH,
            )

        for copy in loads(0):
            copy.start()
        greet(lat)

        def partial(e, target, zz):
            slot = e % 2
            for copy in loads(e):
                copy.wait()

            @pl.when(e + 1 < 2 * depth)
            def _():
                for copy in loads(e + 1):
                    copy.start()

            @pl.when(e >= 2)
            def _():
                for copy in stores(e - 2):
                    copy.wait()

            cot_rows = cots[slot]

            def inner(t, carry):
                at = pl.ds(pl.multiple_of(t * tile, tile), tile)
                act_grad = nt(cot_rows, down_ref[at, :])
                gate, up = gate_in[slot, :, at], up_in[slot, :, at]
                sigmoid = lax.logistic(gate)
                gate_low[slot, :, at] = (
                    act_grad * up * sigmoid * (1.0 + gate * (1.0 - sigmoid))
                ).astype(low)
                up_low[slot, :, at] = (act_grad * gate * sigmoid).astype(low)
                return carry

            lax.fori_loop(0, hidden // tile, inner, 0)
            for copy in stores(e):
                copy.start()
            gate_rows, up_rows = gate_low[slot], up_low[slot]

            def outer(t, carry):
                at = pl.ds(pl.multiple_of(t * wide_tile, wide_tile), wide_tile)
                target[zz, :, at] = (
                    nt(gate_rows, gate_ref[at, :]) + nt(up_rows, up_ref[at, :])
                ).astype(low)
                return carry

            lax.fori_loop(0, model // wide_tile, outer, 0)

        def send_step(e, carry):
            zz, _ = place(e)
            partial(e, foreign, zz)
            cross(zz).start()
            return carry

        lax.fori_loop(0, depth, send_step, 0)

        def chain_step(e, carry):
            zz, _ = place(e)
            partial(e, own, zz)
            cross(zz).wait_recv()
            wide = jnp.float32

            @pl.when((zz > z) & (z > 0))
            def _():
                rise(zz).wait_recv()
                own[zz] = (own[zz].astype(wide) + crossed[zz].astype(wide) + from_low[zz].astype(wide)).astype(low)

            @pl.when((zz < z) & (z < last))
            def _():
                sink(zz).wait_recv()
                own[zz] = (own[zz].astype(wide) + crossed[zz].astype(wide) + from_high[zz].astype(wide)).astype(low)

            @pl.when(((zz > z) & (z == 0)) | ((zz < z) & (z == last)))
            def _():
                own[zz] = (own[zz].astype(wide) + crossed[zz].astype(wide)).astype(low)

            @pl.when(zz > z)
            def _():
                rise(zz).start()

            @pl.when(zz < z)
            def _():
                sink(zz).start()

            @pl.when(zz == z)
            def _():
                sum_ref[...] = own[zz].astype(wide) + crossed[zz].astype(wide)

                @pl.when(z > 0)
                def _():
                    rise(zz).wait_recv()
                    sum_ref[...] += from_low[zz].astype(wide)

                @pl.when(z < last)
                def _():
                    sink(zz).wait_recv()
                    sum_ref[...] += from_high[zz].astype(wide)

            return carry

        lax.fori_loop(depth, 2 * depth, chain_step, 0)
        for e in (2 * depth - 2, 2 * depth - 1):
            for copy in stores(e):
                copy.wait()

        def settle(zz, carry):
            cross(zz).wait_send()

            @pl.when(zz > z)
            def _():
                rise(zz).wait_send()

            @pl.when(zz < z)
            def _():
                sink(zz).wait_send()

            return carry

        lax.fori_loop(0, depth, settle, 0)

    vmem = pl.BlockSpec(memory_space=pltpu.VMEM)
    hbm = pl.BlockSpec(memory_space=pl.ANY)
    total, gate_low, up_low = pl.pallas_call(
        kernel,
        in_specs=[hbm, hbm, hbm, vmem, vmem, vmem],
        out_specs=[vmem, hbm, hbm],
        out_shape=[
            jax.ShapeDtypeStruct((rows, model), jnp.float32),
            jax.ShapeDtypeStruct((wide_count, rows, hidden), low),
            jax.ShapeDtypeStruct((wide_count, rows, hidden), low),
        ],
        scratch_shapes=[
            pltpu.VMEM((2, rows, model), low),
            pltpu.VMEM((2, rows, hidden), jnp.float32),
            pltpu.VMEM((2, rows, hidden), jnp.float32),
            pltpu.VMEM((2, rows, hidden), low),
            pltpu.VMEM((2, rows, hidden), low),
        ]
        + [pltpu.VMEM((depth, rows, model), low)] * 5
        + [
            pltpu.SemaphoreType.DMA((3, 2)),
            pltpu.SemaphoreType.DMA((2, 2)),
        ]
        + [pltpu.SemaphoreType.DMA((depth,))] * 5,
        compiler_params=pltpu.CompilerParams(
            collective_id=collective_id, has_side_effects=True, vmem_limit_bytes=58 << 20
        ),
        name="backward_scattered",
    )(
        cot.reshape(wide_count, rows, model),
        gates.reshape(wide_count, rows, hidden),
        ups.reshape(wide_count, rows, hidden),
        gate_weight, up_weight, down_weight,
    )
    flat = wide_count * rows
    return total, gate_low.reshape(flat, hidden), up_low.reshape(flat, hidden)


def sum_everywhere(values, counts, collective_id):
    axes = ("narrow", "wide")

    def kernel(in_ref, out_ref, mine, held, total, load_sem, send_sems, recv_sems, wide_send, wide_recv):
        here = [lax.axis_index(axis) for axis in axes]

        def peers(k, act):
            def one(step, carry):
                act((here[k] + step) % counts[k])
                return carry

            lax.fori_loop(1, counts[k], one, 0)

        barrier = pltpu.get_barrier_semaphore()
        for k, axis in enumerate(axes):
            peers(k, lambda who: pl.semaphore_signal(
                barrier, inc=1, device_id={axis: who}, device_id_type=MESH))
        load = pltpu.make_async_copy(in_ref, mine, load_sem)
        load.start()
        load.wait()
        pl.semaphore_wait(barrier, counts[0] + counts[1] - 2)

        def exchange(k, source, slots, sends, recvs, target):
            def copy(who):
                return pltpu.make_async_remote_copy(
                    src_ref=source, dst_ref=slots.at[here[k]],
                    send_sem=sends.at[who], recv_sem=recvs.at[here[k]],
                    device_id={axes[k]: who}, device_id_type=MESH,
                )

            def arrival(who):
                return pltpu.make_async_remote_copy(
                    src_ref=source, dst_ref=slots.at[who],
                    send_sem=sends.at[who], recv_sem=recvs.at[who],
                    device_id={axes[k]: who}, device_id_type=MESH,
                )

            peers(k, lambda who: copy(who).start())
            slots[here[k]] = source[...]
            peers(k, lambda who: arrival(who).wait_recv())
            sums = slots[0]
            for n in range(1, counts[k]):
                sums = sums + slots[n]
            target[...] = sums
            peers(k, lambda who: copy(who).wait_send())

        exchange(0, mine, held.at[0], send_sems, recv_sems, total)
        exchange(1, total, held.at[1], wide_send, wide_recv, out_ref)

    most = max(counts)
    shape = values.shape
    return pl.pallas_call(
        kernel,
        in_specs=[pl.BlockSpec(memory_space=pl.ANY)],
        out_specs=pl.BlockSpec(memory_space=pltpu.VMEM),
        out_shape=jax.ShapeDtypeStruct(shape, jnp.float32),
        scratch_shapes=[
            pltpu.VMEM(shape, jnp.float32),
            pltpu.VMEM((2, most) + shape, jnp.float32),
            pltpu.VMEM(shape, jnp.float32),
            pltpu.SemaphoreType.DMA,
            pltpu.SemaphoreType.DMA((counts[0],)),
            pltpu.SemaphoreType.DMA((counts[0],)),
            pltpu.SemaphoreType.DMA((counts[1],)),
            pltpu.SemaphoreType.DMA((counts[1],)),
        ],
        compiler_params=pltpu.CompilerParams(collective_id=collective_id, has_side_effects=True),
        name="sum_everywhere",
    )(values)

CORPORA = 8
GATHER_BYTES = 8 << 20


def norm_scale(values, scale_gain):
    return (
        values * lax.rsqrt(jnp.mean(values * values, axis=-1, keepdims=True) + epsilon) * scale_gain
    )


def contract_first(left, right):
    return lax.dot_general(
        left, right, (((0,), (0,)), ((), ())), preferred_element_type=jnp.float32
    )


def gather_wide(values):
    return lax.all_gather(values, "wide", axis=0, tiled=True)


def scatter_wide(values):
    return lax.psum_scatter(
        values.astype(jnp.bfloat16), "wide", scatter_dimension=0, tiled=True
    ).astype(jnp.float32)


def own_part(values, axis, index, count):
    size = values.shape[axis] // count
    return lax.dynamic_slice_in_dim(values, index * size, size, axis)


def sum_narrow(values):
    part = lax.psum_scatter(
        values.astype(jnp.bfloat16), "narrow", scatter_dimension=0, tiled=True
    )
    return lax.all_gather(part, "narrow", axis=0, tiled=True).astype(jnp.float32)


def swiglu_back(act_grad, gate_values, up_values):
    sigmoid_gate = lax.logistic(gate_values)
    gate_part = act_grad * up_values * sigmoid_gate * (1.0 + gate_values * (1.0 - sigmoid_gate))
    up_part = act_grad * gate_values * sigmoid_gate
    return (gate_part.astype(jnp.bfloat16), up_part.astype(jnp.bfloat16))


def shards(
    tokens,
    attention_gain,
    query_weight,
    key_weight,
    value_weight,
    query_gain,
    key_gain,
    output_weight,
    feedforward_gain,
    gate_weight,
    up_weight,
    down_weight,
    cotangent,
    corpus_tags,
    segments,
):
    low, wide_type = jnp.bfloat16, jnp.float32
    head_size = query_gain.shape[0]
    own_rows, model_width = tokens.shape
    wide_count, narrow_count = lax.axis_size("wide"), lax.axis_size("narrow")
    wide_index, narrow_index = lax.axis_index("wide"), lax.axis_index("narrow")
    key_total = key_weight.shape[1] // head_size
    width = query_weight.shape[1]
    key_head = wide_index * key_total // wide_count
    all_rows = own_rows * wide_count
    chained = wide_count % 2 == 0 and all_rows * model_width * 2 <= GATHER_BYTES

    tag_hits = corpus_tags[:, None] == jnp.arange(CORPORA, dtype=jnp.int32)[None, :]
    local_counts = jnp.sum(tag_hits.astype(wide_type), axis=0)
    corpus_counts = sum_everywhere(
        jnp.pad(local_counts[None], ((0, 7), (0, 128 - CORPORA))), (narrow_count, wide_count), 1
    )[0, :CORPORA]
    corpus_scale = jnp.sqrt(jnp.sum(corpus_counts) / (CORPORA * corpus_counts))
    row_weight = jnp.sum(jnp.where(tag_hits, corpus_scale[None, :], 0.0), axis=1)
    out_cot = cotangent.astype(wide_type) * row_weight[:, None]
    token_values = tokens.astype(wide_type)
    first_gain = attention_gain.astype(wide_type)
    second_gain = feedforward_gain.astype(wide_type)

    key_columns = lax.dynamic_slice_in_dim(key_weight, key_head * head_size, head_size, 1)
    value_columns = lax.dynamic_slice_in_dim(value_weight, key_head * head_size, head_size, 1)
    own_weights = jnp.concatenate([query_weight, key_columns, value_columns], axis=1)
    output_full = lax.all_gather(
        own_part(output_weight, 0, narrow_index, narrow_count), ("wide", "narrow"), axis=0, tiled=True
    )

    hidden_local = norm_scale(token_values, first_gain).astype(low)
    if chained:
        hidden_one, raw = project_gathered(hidden_local, own_weights, wide_count, 2)
    else:
        hidden_one = gather_wide(hidden_local)
        raw = dot_nn(hidden_one, own_weights)
    cot_local, raw = lax.optimization_barrier((out_cot.astype(low), raw))
    cot_low = gather_wide(cot_local)

    first_block = first_blocks(segments)
    saved = attention_forward(raw, query_gain, key_gain, segments, first_block)
    mixed = lax.all_to_all(saved[0], "wide", split_axis=0, concat_axis=1, tiled=True)
    middle = token_values + dot_nn(mixed, output_full)

    hidden_two_local = norm_scale(middle, second_gain).astype(low)
    if chained:
        hidden_two, gate_values, up_values, activated, down_part = forward_gathered(
            hidden_two_local, gate_weight, up_weight, down_weight, wide_count, 3
        )
        hidden_two_grad, gate_low, up_low = backward_scattered(
            cot_low, gate_values, up_values, gate_weight, up_weight, down_weight, wide_count, 4
        )
        down_part, hidden_two_grad = lax.optimization_barrier((down_part, hidden_two_grad))
    else:
        hidden_two = gather_wide(hidden_two_local)
        gate_values = dot_nn(hidden_two, gate_weight)
        up_values = dot_nn(hidden_two, up_weight)
        activated = (gate_values * lax.logistic(gate_values) * up_values).astype(low)
        down_part = dot_nn(activated, down_weight)
        gate_low, up_low = swiglu_back(dot_nt(cot_low, down_weight), gate_values, up_values)
        hidden_two_grad = scatter_wide(dot_nt(gate_low, gate_weight) + dot_nt(up_low, up_weight))
    result = (middle + scatter_wide(down_part)).astype(low)
    down_grad = sum_narrow(contract_first(activated, cot_low))
    gate_grad = sum_narrow(contract_first(hidden_two, gate_low))
    up_grad = sum_narrow(contract_first(hidden_two, up_low))

    _, second_pull = jax.vjp(norm_scale, middle, second_gain)
    middle_part, second_gain_grad = second_pull(hidden_two_grad)
    middle_grad = out_cot + middle_part
    middle_low = middle_grad.astype(low)
    output_grad = lax.all_gather(
        lax.psum_scatter(
            contract_first(mixed, middle_low).astype(low),
            ("wide", "narrow"),
            scatter_dimension=0,
            tiled=True,
        ),
        "narrow",
        axis=0,
        tiled=True,
    ).astype(wide_type)
    mixed_grad = lax.all_to_all(
        dot_nt(middle_low, output_full).astype(low), "wide", split_axis=1, concat_axis=0, tiled=True
    )
    grads, query_gain_grad, key_gain_grad = attention_backward(
        raw, query_gain, key_gain, segments, first_block, saved, mixed_grad
    )

    query_turned = lax.all_gather(
        jnp.transpose(own_part(query_weight, 1, narrow_index, narrow_count)),
        ("wide", "narrow"),
        axis=0,
        tiled=True,
    )
    sent = lax.all_to_all(grads, "wide", split_axis=0, concat_axis=1, tiled=True).reshape(
        own_rows, wide_count, width + 2 * head_size
    )
    shared = wide_count // key_total

    def key_side(start):
        part = sent[:, :, start : start + head_size]
        if shared > 1:
            part = jnp.sum(
                part.astype(wide_type).reshape(own_rows, key_total, shared, head_size), axis=2
            ).astype(low)
        return part.reshape(own_rows, key_total * head_size)

    hidden_one_grad = (
        dot_nn(sent[:, :, :width].reshape(own_rows, wide_count * width), query_turned)
        + dot_nt(key_side(width), key_weight)
        + dot_nt(key_side(width + head_size), value_weight)
    )
    _, first_pull = jax.vjp(norm_scale, token_values, first_gain)
    token_part, first_gain_grad = first_pull(hidden_one_grad)
    tokens_gradient = (middle_grad + token_part).astype(low)

    weight_grads = contract_first(hidden_one, grads)
    if shared == 1:
        weight_sums = sum_narrow(weight_grads)
        key_weight_grad = weight_sums[:, width : width + head_size]
        value_weight_grad = weight_sums[:, width + head_size :]
    else:
        weight_sums = sum_narrow(weight_grads[:, :width])

        def spread(part):
            whole = jnp.zeros((model_width, key_total * head_size), wide_type)
            whole = lax.dynamic_update_slice_in_dim(whole, part, key_head * head_size, 1)
            share = lax.psum_scatter(whole.astype(low), "wide", scatter_dimension=1, tiled=True)
            return lax.psum(share, "narrow").astype(wide_type)

        key_weight_grad = spread(weight_grads[:, width : width + head_size])
        value_weight_grad = spread(weight_grads[:, width + head_size :])

    gain_parts = jnp.concatenate([first_gain_grad, second_gain_grad, query_gain_grad, key_gain_grad])
    lines = -(-gain_parts.shape[0] // 1024) * 8
    gain_parts = jnp.pad(gain_parts, (0, lines * 128 - gain_parts.shape[0])).reshape(lines, 128)
    gains = sum_everywhere(gain_parts, (narrow_count, wide_count), 5).reshape(-1)
    starts = (0, model_width, 2 * model_width, 2 * model_width + head_size)
    sizes = (model_width, model_width, head_size, head_size)
    first_out, second_out, query_gain_out, key_gain_out = (
        own_part(gains[start : start + size], 0, wide_index, wide_count)
        for start, size in zip(starts, sizes)
    )
    return (
        result,
        tokens_gradient,
        first_out,
        weight_sums[:, :width],
        key_weight_grad,
        value_weight_grad,
        query_gain_out,
        key_gain_out,
        output_grad,
        second_out,
        gate_grad,
        up_grad,
        down_grad,
    )


def solution(mesh):
    rows = P(("narrow", "wide"), None)
    columns, first = P(None, "wide"), P("wide", None)
    return jax.shard_map(
        shards,
        mesh=mesh,
        in_specs=(
            rows, P(), columns, P(), P(), P(), P(), first, P(), columns, columns, first,
            rows, P(("narrow", "wide")), P("narrow", None),
        ),
        out_specs=(
            rows, rows, P("wide"), columns, columns, columns, P("wide"), P("wide"),
            first, P("wide"), columns, columns, first,
        ),
        check_vma=False,
    )
```

```python
import numpy as np

import jax
import jax.numpy as jnp
from jax import lax
from jax.experimental import pallas as pl
from jax.experimental.pallas import tpu as pltpu
from jax.sharding import PartitionSpec as P

SEQ = 2048
epsilon = 1e-06
rope_base = 10000.0
BLOCK = 256
NEG = -1e30


def rope_tables(head_size):
    positions = np.arange(SEQ, dtype=np.float32)
    exponents = np.arange(head_size // 2, dtype=np.float32) * np.float32(2.0 / head_size)
    frequency = np.power(np.float32(rope_base), -exponents).astype(np.float32)
    angles = (positions[:, None] * frequency[None, :]).astype(np.float32)
    cosine, sine = np.cos(angles).astype(np.float32), np.sin(angles).astype(np.float32)
    return (
        np.concatenate([cosine, cosine], axis=1),
        np.concatenate([-sine, sine], axis=1),
    )


def dot_nn(left, right):
    return jnp.dot(left, right, preferred_element_type=jnp.float32)


def dot_nt(left, right):
    return lax.dot_general(
        left, right, (((1,), (1,)), ((), ())), preferred_element_type=jnp.float32
    )


def lane_ids(shape):
    return lax.broadcasted_iota(jnp.int32, shape, 1)


def group_ones(width, head_size):
    rows = lax.broadcasted_iota(jnp.int32, (width, width), 0) // head_size
    columns = lax.broadcasted_iota(jnp.int32, (width, width), 1) // head_size
    return jnp.where(rows == columns, 1.0, 0.0).astype(jnp.bfloat16)


def group_sum(values, ones):
    top = values.astype(jnp.bfloat16)
    rest = (values - top.astype(jnp.float32)).astype(jnp.bfloat16)
    return dot_nn(top, ones) + dot_nn(rest, ones)


def swap_halves(values, head_size):
    width, half = values.shape[1], head_size // 2
    if width == head_size:
        return jnp.concatenate([values[:, half:], values[:, :half]], axis=1)
    ahead = pltpu.roll(values, width - half, 1)
    behind = pltpu.roll(values, half, 1)
    return jnp.where(lane_ids(values.shape) % head_size < half, ahead, behind)


def tiled(values, count):
    return jnp.concatenate([values] * count, axis=1) if count > 1 else values


def split_raw(raw, width, head_size, heads):
    query = raw[:, :width]
    key = tiled(raw[:, width : width + head_size], heads)
    value = tiled(raw[:, width + head_size :], heads)
    return query, key, value


def head_masks(block, width, head_size, heads):
    group = lane_ids((block, width)) // head_size
    return [group == h for h in range(heads)]


def attention_forward(raw, query_gain, key_gain, segments, first_block):
    head_size = query_gain.shape[0]
    rows = raw.shape[0]
    heads = raw.shape[1] // head_size - 2
    width = heads * head_size
    seqs, blocks, block = rows // SEQ, SEQ // BLOCK, BLOCK
    scale = head_size ** (-0.5)

    def kernel(
        first_ref, raw_ref, qg_ref, kg_ref, cos_ref, sin_ref, segq_ref, segk_ref,
        mixed_ref, lse_ref, query_ref, key_ref, value_ref, keyt_ref,
        keys, values_t, masked, top, total, acc,
    ):
        s, i = pl.program_id(0), pl.program_id(1)
        cosine, sine = tiled(cos_ref[...], heads), tiled(sin_ref[...], heads)
        ones = group_ones(width, head_size)
        query, key, value = split_raw(raw_ref[...], width, head_size, heads)

        def norm_rope(x, gain):
            x = x * lax.rsqrt(group_sum(x * x, ones) * (1.0 / head_size) + epsilon) * gain
            return x * cosine + swap_halves(x, head_size) * sine

        query_low = norm_rope(query, qg_ref[...]).astype(jnp.bfloat16)
        key_rot = norm_rope(key, kg_ref[...])
        key_low = key_rot.astype(jnp.bfloat16)
        query_ref[...] = query_low
        key_ref[...] = key_low
        value_ref[...] = value.astype(jnp.bfloat16)
        keyt_ref[0] = jnp.transpose(key_rot)[:head_size].astype(jnp.bfloat16)
        keys[pl.ds(pl.multiple_of(i * block, block), block), :] = key_low
        values_t[i] = jnp.transpose(value)[:head_size].astype(jnp.bfloat16)
        scaled = query_low * jnp.bfloat16(scale)
        zero = jnp.zeros_like(scaled)
        for h, mask in enumerate(head_masks(block, width, head_size, heads)):
            masked[h] = jnp.where(mask, scaled, zero)
        top[...] = jnp.full_like(top, NEG)
        total[...] = jnp.zeros_like(total)
        acc[...] = jnp.zeros_like(acc)
        query_pos = i * block + lax.broadcasted_iota(jnp.int32, (block, block), 1)
        segment_query = segq_ref[0]

        def step(j, carry):
            at = pl.multiple_of(j * block, block)
            key_pos = at + lax.broadcasted_iota(jnp.int32, (block, block), 0)
            allowed = (key_pos <= query_pos) & (segk_ref[pl.ds(at, block), :] == segment_query)
            bias = jnp.where(allowed, 0.0, NEG)
            key_block = keys[pl.ds(at, block), :]
            value_t = values_t[j]
            for h in range(heads):
                scores = dot_nt(key_block, masked[h]) + bias
                before = top[h : h + 1, :]
                now = jnp.maximum(before, jnp.max(scores, axis=0, keepdims=True))
                shifted = jnp.exp(scores - now)
                fade = jnp.exp(before - now)
                top[h : h + 1, :] = now
                total[h : h + 1, :] = fade * total[h : h + 1, :] + jnp.sum(
                    shifted, axis=0, keepdims=True
                )
                span = slice(h * head_size, (h + 1) * head_size)
                acc[span, :] = fade * acc[span, :] + dot_nn(value_t, shifted.astype(jnp.bfloat16))
            return carry

        lax.fori_loop(first_ref[s, i], i + 1, step, 0)
        for h in range(heads):
            span = slice(h * head_size, (h + 1) * head_size)
            acc[span, :] = acc[span, :] / total[h : h + 1, :]
        mixed_ref[...] = jnp.transpose(acc[...]).astype(jnp.bfloat16)
        lse_ref[...] = top[...] + jnp.log(jnp.maximum(total[...], 1e-30))

    cosine, sine = rope_tables(head_size)
    at_rows = lambda s, i, first: (s * blocks + i, 0)
    fixed = lambda s, i, first: (0, 0)
    at_lanes = lambda s, i, first: (0, s * blocks + i)
    low = jnp.bfloat16
    pairs = blocks * (blocks + 1) // 2 * seqs * heads
    return pl.pallas_call(
        kernel,
        grid_spec=pltpu.PrefetchScalarGridSpec(
            num_scalar_prefetch=1,
            grid=(seqs, blocks),
            in_specs=[
                pl.BlockSpec((block, raw.shape[1]), at_rows),
                pl.BlockSpec((1, width), fixed),
                pl.BlockSpec((1, width), fixed),
                pl.BlockSpec((block, head_size), lambda s, i, first: (i, 0)),
                pl.BlockSpec((block, head_size), lambda s, i, first: (i, 0)),
                pl.BlockSpec((1, 1, block), lambda s, i, first: (s, 0, i)),
                pl.BlockSpec((SEQ, 1), lambda s, i, first: (s, 0)),
            ],
            out_specs=[
                pl.BlockSpec((block, width), at_rows),
                pl.BlockSpec((8, block), at_lanes),
                pl.BlockSpec((block, width), at_rows),
                pl.BlockSpec((block, width), at_rows),
                pl.BlockSpec((block, width), at_rows),
                pl.BlockSpec((1, head_size, block), lambda s, i, first: (s * blocks + i, 0, 0)),
            ],
            scratch_shapes=[
                pltpu.VMEM((SEQ, width), low),
                pltpu.VMEM((blocks, head_size, block), low),
                pltpu.VMEM((heads, block, width), low),
                pltpu.VMEM((8, block), jnp.float32),
                pltpu.VMEM((8, block), jnp.float32),
                pltpu.VMEM((width, block), jnp.float32),
            ],
        ),
        out_shape=[
            jax.ShapeDtypeStruct((rows, width), low),
            jax.ShapeDtypeStruct((8, rows), jnp.float32),
            jax.ShapeDtypeStruct((rows, width), low),
            jax.ShapeDtypeStruct((rows, width), low),
            jax.ShapeDtypeStruct((rows, width), low),
            jax.ShapeDtypeStruct((rows // block, head_size, block), low),
        ],
        compiler_params=pltpu.CompilerParams(vmem_limit_bytes=40 << 20),
        cost_estimate=pl.CostEstimate(flops=0, bytes_accessed=0, transcendentals=0),
        name="attention_forward",
    )(
        first_block, raw,
        tiled(query_gain.astype(jnp.float32)[None], heads),
        tiled(key_gain.astype(jnp.float32)[None], heads),
        cosine, sine, segments[:, None, :], segments.reshape(rows, 1),
    )


def attention_backward(
    raw, query_gain, key_gain, segments, first_block, saved, mixed_grad
):
    mixed, lse, query_low, key_low, value_low, key_t = saved
    head_size = query_gain.shape[0]
    rows, width = mixed.shape
    heads = width // head_size
    seqs, blocks, block = rows // SEQ, SEQ // BLOCK, BLOCK
    scale = head_size ** (-0.5)

    def kernel(
        first_ref, raw_ref, qg_ref, kg_ref, cos_ref, sin_ref, segq_ref, segk_ref,
        mixed_ref, lse_ref, query_ref, grad_ref, keys_ref, values_ref, keyt_ref,
        out_ref, qgg_ref, kgg_ref,
        masked, masked_grad, key_sums, value_sums, query_sums, deltas,
    ):
        s, i = pl.program_id(0), blocks - 1 - pl.program_id(1)

        @pl.when(pl.program_id(1) == 0)
        def _():
            key_sums[...] = jnp.zeros_like(key_sums)
            value_sums[...] = jnp.zeros_like(value_sums)

        @pl.when((pl.program_id(1) == 0) & (s == 0))
        def _():
            qgg_ref[...] = jnp.zeros_like(qgg_ref)
            kgg_ref[...] = jnp.zeros_like(kgg_ref)

        query_sums[...] = jnp.zeros_like(query_sums)
        grad = grad_ref[...]
        scaled = query_ref[...] * jnp.bfloat16(scale)
        zero = jnp.zeros_like(scaled)
        for h, mask in enumerate(head_masks(block, width, head_size, heads)):
            span = slice(h * block, (h + 1) * block)
            masked[span, :] = jnp.where(mask, scaled, zero)
            masked_grad[span, :] = jnp.where(mask, grad, zero)
        product = jnp.transpose(grad.astype(jnp.float32) * mixed_ref[...].astype(jnp.float32))
        for h in range(heads):
            deltas[h : h + 1, :] = jnp.sum(
                product[h * head_size : (h + 1) * head_size], axis=0, keepdims=True
            )
        query_pos = i * block + lax.broadcasted_iota(jnp.int32, (block, block), 1)
        segment_query = segq_ref[0]

        def step(j, carry):
            at = pl.multiple_of(j * block, block)
            key_pos = at + lax.broadcasted_iota(jnp.int32, (block, block), 0)
            allowed = (key_pos <= query_pos) & (segk_ref[pl.ds(at, block), :] == segment_query)
            bias = jnp.where(allowed, 0.0, NEG)
            key_block = keys_ref[pl.ds(at, block), :]
            value_block = values_ref[pl.ds(at, block), :]
            key_t = keyt_ref[j]
            lows, grads = [], []
            for h in range(heads):
                span = slice(h * block, (h + 1) * block)
                scores = dot_nt(key_block, masked[span, :]) + bias
                probability = jnp.exp(scores - lse_ref[h : h + 1, :])
                prob_grad = dot_nt(value_block, masked_grad[span, :])
                score_grad = (probability * (prob_grad - deltas[h : h + 1, :])).astype(jnp.bfloat16)
                lows.append(probability.astype(jnp.bfloat16))
                grads.append(score_grad)
                rows_h = slice(h * head_size, (h + 1) * head_size)
                query_sums[rows_h, :] += dot_nn(key_t, score_grad)
            value_sums[pl.ds(at, block), :] += dot_nn(
                jnp.concatenate(lows, axis=1), masked_grad[...]
            )
            key_sums[pl.ds(at, block), :] += dot_nn(jnp.concatenate(grads, axis=1), masked[...])
            return carry

        lax.fori_loop(first_ref[s, i], i + 1, step, 0)
        cosine, sine = tiled(cos_ref[...], heads), tiled(sin_ref[...], heads)
        ones = group_ones(width, head_size)
        query, key, _ = split_raw(raw_ref[...], width, head_size, heads)

        def all_heads(x):
            total = x
            for h in range(1, heads):
                total = total + pltpu.roll(x, h * head_size, 1)
            return total

        def norm_rope_back(x, up, gain):
            unrot = up * cosine - swap_halves(up, head_size) * sine
            inverse = lax.rsqrt(group_sum(x * x, ones) * (1.0 / head_size) + epsilon)
            gain_part = jnp.sum(unrot * x * inverse, axis=0, keepdims=True)
            scaled_up = unrot * gain
            mean = group_sum(scaled_up * x, ones) * (1.0 / head_size)
            return scaled_up * inverse - x * (mean * inverse * inverse * inverse), gain_part

        query_up = jnp.transpose(query_sums[...]) * scale
        query_grad, query_part = norm_rope_back(query, query_up, qg_ref[...])
        here = pl.ds(pl.multiple_of(i * block, block), block)
        key_up = all_heads(key_sums[here, :])
        key_grad, key_part = norm_rope_back(key, key_up, kg_ref[...])
        value_grad = all_heads(value_sums[here, :])
        out_ref[...] = jnp.concatenate(
            [query_grad, key_grad[:, :head_size], value_grad[:, :head_size]], axis=1
        ).astype(jnp.bfloat16)
        qgg_ref[...] += query_part
        kgg_ref[...] += key_part

    cosine, sine = rope_tables(head_size)
    at_rows = lambda s, i, first: (s * blocks + blocks - 1 - i, 0)
    fixed = lambda s, i, first: (0, 0)
    at_lanes = lambda s, i, first: (0, s * blocks + blocks - 1 - i)
    at_seq = lambda s, i, first: (s, 0)
    low = jnp.bfloat16
    pairs = blocks * (blocks + 1) // 2 * seqs * heads
    grads, query_part, key_part = pl.pallas_call(
        kernel,
        grid_spec=pltpu.PrefetchScalarGridSpec(
            num_scalar_prefetch=1,
            grid=(seqs, blocks),
            in_specs=[
                pl.BlockSpec((block, raw.shape[1]), at_rows),
                pl.BlockSpec((1, width), fixed),
                pl.BlockSpec((1, width), fixed),
                pl.BlockSpec((block, head_size), lambda s, i, first: (blocks - 1 - i, 0)),
                pl.BlockSpec((block, head_size), lambda s, i, first: (blocks - 1 - i, 0)),
                pl.BlockSpec((1, 1, block), lambda s, i, first: (s, 0, blocks - 1 - i)),
                pl.BlockSpec((SEQ, 1), at_seq),
                pl.BlockSpec((block, width), at_rows),
                pl.BlockSpec((8, block), at_lanes),
                pl.BlockSpec((block, width), at_rows),
                pl.BlockSpec((block, width), at_rows),
                pl.BlockSpec((SEQ, width), at_seq),
                pl.BlockSpec((SEQ, width), at_seq),
                pl.BlockSpec((blocks, head_size, block), lambda s, i, first: (s, 0, 0)),
            ],
            out_specs=[
                pl.BlockSpec((block, raw.shape[1]), at_rows),
                pl.BlockSpec((1, width), fixed),
                pl.BlockSpec((1, width), fixed),
            ],
            scratch_shapes=[
                pltpu.VMEM((heads * block, width), low),
                pltpu.VMEM((heads * block, width), low),
                pltpu.VMEM((SEQ, width), jnp.float32),
                pltpu.VMEM((SEQ, width), jnp.float32),
                pltpu.VMEM((width, block), jnp.float32),
                pltpu.VMEM((8, block), jnp.float32),
            ],
        ),
        out_shape=[
            jax.ShapeDtypeStruct(raw.shape, low),
            jax.ShapeDtypeStruct((1, width), jnp.float32),
            jax.ShapeDtypeStruct((1, width), jnp.float32),
        ],
        compiler_params=pltpu.CompilerParams(vmem_limit_bytes=48 << 20),
        cost_estimate=pl.CostEstimate(flops=0, bytes_accessed=0, transcendentals=0),
        name="attention_backward",
    )(
        first_block, raw,
        tiled(query_gain.astype(jnp.float32)[None], heads),
        tiled(key_gain.astype(jnp.float32)[None], heads),
        cosine, sine, segments[:, None, :], segments.reshape(rows, 1),
        mixed, lse, query_low, mixed_grad, key_low, value_low, key_t,
    )
    return (
        grads,
        jnp.sum(query_part.reshape(heads, head_size), axis=0),
        key_part[0, :head_size],
    )


def first_blocks(segments):
    starts = segments[:, :: BLOCK]
    below = jnp.sum(segments[:, None, :] < starts[:, :, None], axis=-1, dtype=jnp.int32)
    return below // BLOCK

MESH = pl.DeviceIdType.MESH


class Lattice:
    def __init__(self, count):
        self.depth = count // 2
        me = lax.axis_index("wide")
        self.z, self.x = me // 2, me % 2
        self.below = jnp.minimum(self.z, self.depth - 1 - self.z)
        self.low_side = self.z > self.depth - 1 - self.z

    def at(self, z, x):
        return z * 2 + x

    def order(self, m):
        near = m <= 2 * self.below
        r = jnp.where(near, (m + 1) // 2, m - self.below)
        minus = jnp.where(near, m % 2 == 1, self.low_side)
        return jnp.where(minus, self.z - r, self.z + r), r


def greet(lat, partners=()):
    barrier = pltpu.get_barrier_semaphore()
    last = lat.depth - 1
    for partner in partners:
        pl.semaphore_signal(
            barrier, inc=1, device_id={"narrow": partner}, device_id_type=MESH
        )

    def each(act):
        act(lat.at(lat.z, 1 - lat.x))

        @pl.when(lat.z > 0)
        def _():
            act(lat.at(lat.z - 1, lat.x))

        @pl.when(lat.z < last)
        def _():
            act(lat.at(lat.z + 1, lat.x))

    each(lambda who: pl.semaphore_signal(barrier, inc=1, device_id={"wide": who}, device_id_type=MESH))
    own = 1 + len(partners)
    pl.semaphore_wait(barrier, own + jnp.minimum(lat.z, 1) + jnp.minimum(last - lat.z, 1))


def gather_chunks(lat, buffers, send_sems, recv_sems, compute, meanwhile=None, landed=None):
    z, x, depth = lat.z, lat.x, lat.depth
    last = depth - 1
    every = range(len(buffers))

    def copy(k, chunk, way, slot, target):
        return pltpu.make_async_remote_copy(
            src_ref=buffers[k].at[chunk], dst_ref=buffers[k].at[chunk],
            send_sem=send_sems.at[k, way, slot], recv_sem=recv_sems.at[k, chunk],
            device_id={"wide": target}, device_id_type=MESH,
        )

    def up(k, zz):
        return copy(k, lat.at(zz, x), 0, zz, lat.at(z + 1, x))

    def down(k, zz):
        return copy(k, lat.at(zz, x), 1, zz, lat.at(z - 1, x))

    def across(k, zz):
        return copy(k, lat.at(zz, x), 2, zz, lat.at(z, 1 - x))

    def arrived(k, chunk):
        copy(k, chunk, 2, 0, lat.at(z, 1 - x)).wait_recv()
        if landed is not None:
            landed(k, chunk)

    for k in every:
        @pl.when(z < last)
        def _():
            up(k, z).start()

        @pl.when(z > 0)
        def _():
            down(k, z).start()

        across(k, z).start()
    if meanwhile is not None:
        meanwhile()

    def step(m, carry):
        zz, r = lat.order(m)
        _, before = lat.order(m - 1)

        @pl.when((m >= 1) & (m < depth) & (r != before))
        def _():
            for k in every:
                @pl.when(z - r >= 0)
                def _():
                    arrived(k, lat.at(z - r, x))

                    @pl.when(z < last)
                    def _():
                        up(k, z - r).start()

                    across(k, z - r).start()

                @pl.when(z + r <= last)
                def _():
                    arrived(k, lat.at(z + r, x))

                    @pl.when(z > 0)
                    def _():
                        down(k, z + r).start()

                    across(k, z + r).start()

        mirror = lat.order(jnp.maximum(m - 1, 0))[0]

        def part(p, carry):
            @pl.when((p == 1) & (m >= 1))
            def _():
                for k in every:
                    arrived(k, lat.at(mirror, 1 - x))

            @pl.when(((p == 0) & (m < depth)) | ((p == 1) & (m >= 1)))
            def _():
                compute(jnp.where(p == 0, lat.at(zz, x), lat.at(mirror, 1 - x)))

            return carry

        return lax.fori_loop(0, 2, part, carry)

    lax.fori_loop(0, depth + 1, step, 0)

    def settle(zz, carry):
        for k in every:
            @pl.when((z < last) & (zz <= z))
            def _():
                up(k, zz).wait_send()

            @pl.when((z > 0) & (zz >= z))
            def _():
                down(k, zz).wait_send()

            across(k, zz).wait_send()
        return carry

    lax.fori_loop(0, depth, settle, 0)


def project_gathered(local, weights, values, strips, counts, collective_id):
    rows, model = local.shape
    columns = weights.shape[1]
    narrow_count, wide_count = counts
    depth = wide_count // 2
    strip = strips[0].shape[0]
    tall = strip * len(strips)

    def kernel(
        local_ref, weights_ref, values_ref, *refs
    ):
        strip_refs, refs = refs[: len(strips)], refs[len(strips) :]
        full_ref, out_ref, sum_ref, refs = refs[0], refs[1], refs[2], refs[3:]
        spread_refs, refs = refs[: len(strips)], refs[len(strips) :]
        (full, spread, send_sems, recv_sems, own_sems, store_sems, spread_sems, y_send, core_send, spread_recv,
         mine, held, total, load_sem, *sems) = refs
        lat = Lattice(wide_count)
        me = lat.at(lat.z, lat.x)
        narrow_me = lax.axis_index("narrow")
        core_side, y_side = narrow_me + 1 - 2 * (narrow_me % 2), (narrow_me + 2) % 4
        corner = y_side + 1 - 2 * (y_side % 2)
        loads = [
            pltpu.make_async_copy(local_ref, full.at[me], own_sems.at[0]),
            pltpu.make_async_copy(values_ref, mine, load_sem),
        ] + [
            pltpu.make_async_copy(
                ref, spread.at[narrow_me, me, pl.ds(k * strip, strip)], own_sems.at[1 + k]
            )
            for k, ref in enumerate(strip_refs)
        ]
        for load in loads:
            load.start()
        arrive = greet_all(counts)
        for load in loads:
            load.wait()
        arrive()
        narrow, wide = exchange_pair(counts, mine, held, total, *sems)

        def to_side(n, chunk, target, send_sem):
            return pltpu.make_async_remote_copy(
                src_ref=spread.at[n, chunk], dst_ref=spread.at[n, chunk],
                send_sem=send_sem, recv_sem=spread_recv.at[n, chunk],
                device_id={"narrow": target}, device_id_type=MESH,
            )

        def to_y(chunk):
            return to_side(narrow_me, chunk, y_side, y_send.at[chunk])

        def to_core(n, chunk):
            return to_side(n, chunk, core_side, core_send.at[n // 2, chunk])

        def spread_out(chunk):
            to_y(chunk).start()
            to_core(narrow_me, chunk).start()

        def landed(k, chunk):
            if k == 0:
                spread_out(chunk)

        def meanwhile():
            spread_out(me)
            narrow.start()
            total[...] = narrow.total()
            wide.start()

        def keep(chunk):
            return pltpu.make_async_copy(full.at[chunk], full_ref.at[chunk], store_sems.at[chunk])

        def keep_strip(n, chunk, k):
            return pltpu.make_async_copy(
                spread.at[n, chunk, pl.ds(k * strip, strip)], spread_refs[k].at[n, chunk],
                spread_sems.at[k, n, chunk],
            )

        def keep_strips(n, chunk):
            for k in range(len(strips)):
                keep_strip(n, chunk, k).start()

        def compute(chunk):
            keep(chunk).start()
            keep_strips(narrow_me, chunk)
            at = pl.multiple_of(chunk * rows, rows)
            out_ref[pl.ds(at, rows), :] = jnp.dot(
                full[chunk], weights_ref[...], preferred_element_type=jnp.float32
            )

        gather_chunks(
            lat, [spread.at[narrow_me], full], send_sems, recv_sems, compute, meanwhile, landed
        )

        def event(e):
            zz = lat.order(e // 2)[0]
            return lat.at(zz, jnp.where(e % 2 == 0, lat.x, 1 - lat.x))

        def pass_on(e, carry):
            chunk = event(e)
            to_side(y_side, chunk, y_side, y_send.at[chunk]).wait_recv()
            to_core(y_side, chunk).start()
            keep_strips(y_side, chunk)
            return carry

        def take(e, carry):
            chunk = event(e)
            for n in (core_side, corner):
                to_side(n, chunk, core_side, core_send.at[0, chunk]).wait_recv()
                keep_strips(n, chunk)
            return carry

        lax.fori_loop(0, wide_count, pass_on, 0)
        lax.fori_loop(0, wide_count, take, 0)
        sum_ref[...] = wide.total()
        narrow.settle()
        wide.settle()

        def settle(c, carry):
            keep(c).wait()
            to_y(c).wait_send()
            to_core(narrow_me, c).wait_send()
            to_core(y_side, c).wait_send()
            for k in range(len(strips)):
                for n in range(narrow_count):
                    keep_strip(n, c, k).wait()
            return carry

        lax.fori_loop(0, wide_count, settle, 0)

    vmem = pl.BlockSpec(memory_space=pltpu.VMEM)
    hbm = pl.BlockSpec(memory_space=pl.ANY)
    low = local.dtype
    full, out, sums, *gathered = pl.pallas_call(
        kernel,
        in_specs=[hbm, vmem, hbm] + [hbm] * len(strips),
        out_specs=[hbm, vmem, vmem] + [hbm] * len(strips),
        out_shape=[
            jax.ShapeDtypeStruct((wide_count, rows, model), low),
            jax.ShapeDtypeStruct((wide_count * rows, columns), jnp.float32),
            jax.ShapeDtypeStruct(values.shape, jnp.float32),
        ]
        + [jax.ShapeDtypeStruct((narrow_count, wide_count, strip, model), low)] * len(strips),
        scratch_shapes=[
            pltpu.VMEM((wide_count, rows, model), low),
            pltpu.VMEM((narrow_count, wide_count, tall, model), low),
            pltpu.SemaphoreType.DMA((2, 3, depth)),
            pltpu.SemaphoreType.DMA((2, wide_count)),
            pltpu.SemaphoreType.DMA((1 + len(strips),)),
            pltpu.SemaphoreType.DMA((wide_count,)),
            pltpu.SemaphoreType.DMA((len(strips), narrow_count, wide_count)),
            pltpu.SemaphoreType.DMA((wide_count,)),
            pltpu.SemaphoreType.DMA((2, wide_count)),
            pltpu.SemaphoreType.DMA((narrow_count, wide_count)),
        ]
        + exchange_scratch(values.shape, counts),
        compiler_params=pltpu.CompilerParams(
            collective_id=collective_id, has_side_effects=True, vmem_limit_bytes=48 << 20
        ),
        name="project_gathered",
    )(local, weights, values, *strips)
    flat = narrow_count * wide_count * strip
    return full.reshape(wide_count * rows, model), out, sums, [g.reshape(flat, model) for g in gathered]


def nt(left, right):
    return lax.dot_general(
        left, right, (((1,), (1,)), ((), ())), preferred_element_type=jnp.float32
    )


def forward_gathered(local, gate_weight, up_weight, down_weight, wide_count, collective_id):
    rows, model = local.shape
    hidden = gate_weight.shape[1]
    depth = wide_count // 2
    tile = min(256, hidden)
    wide_tile = min(512, model)

    def kernel(
        local_ref, gate_ref, up_ref, down_ref, full_ref, gates_ref, ups_ref, acts_ref, downs_ref,
        full, gates, ups, acts, downs, send_sems, recv_sems, load_sem, store_sems,
    ):
        lat = Lattice(wide_count)
        me = lat.at(lat.z, lat.x)
        load = pltpu.make_async_copy(local_ref, full.at[me], load_sem)
        load.start()
        greet(lat)
        load.wait()
        kept = ((full, full_ref), (gates, gates_ref), (ups, ups_ref), (acts, acts_ref), (downs, downs_ref))

        def keep(which, chunk):
            source, target = kept[which]
            return pltpu.make_async_copy(source.at[chunk], target.at[chunk], store_sems.at[which, chunk])

        def compute(chunk):
            keep(0, chunk).start()
            rows_in = full[chunk]

            def inner(t, carry):
                at = pl.ds(pl.multiple_of(t * tile, tile), tile)
                gate = jnp.dot(rows_in, gate_ref[:, at], preferred_element_type=jnp.float32)
                up = jnp.dot(rows_in, up_ref[:, at], preferred_element_type=jnp.float32)
                gates[chunk, :, at] = gate
                ups[chunk, :, at] = up
                acts[chunk, :, at] = (gate * lax.logistic(gate) * up).astype(jnp.bfloat16)
                return carry

            lax.fori_loop(0, hidden // tile, inner, 0)
            for which in (1, 2, 3):
                keep(which, chunk).start()
            act = acts[chunk]

            def outer(t, carry):
                at = pl.ds(pl.multiple_of(t * wide_tile, wide_tile), wide_tile)
                downs[chunk, :, at] = jnp.dot(
                    act, down_ref[:, at], preferred_element_type=jnp.float32
                ).astype(jnp.bfloat16)
                return carry

            lax.fori_loop(0, model // wide_tile, outer, 0)
            keep(4, chunk).start()

        gather_chunks(lat, [full], send_sems, recv_sems, compute)
        for which in range(5):
            lax.fori_loop(0, wide_count, lambda c, carry: (keep(which, c).wait(), carry)[1], 0)

    low = jnp.bfloat16
    outs = [
        ((wide_count, rows, model), low),
        ((wide_count, rows, hidden), jnp.float32),
        ((wide_count, rows, hidden), jnp.float32),
        ((wide_count, rows, hidden), low),
        ((wide_count, rows, model), low),
    ]
    vmem = pl.BlockSpec(memory_space=pltpu.VMEM)
    hbm = pl.BlockSpec(memory_space=pl.ANY)
    results = pl.pallas_call(
        kernel,
        in_specs=[hbm, vmem, vmem, vmem],
        out_specs=[hbm] * 5,
        out_shape=[jax.ShapeDtypeStruct(*o) for o in outs],
        scratch_shapes=[pltpu.VMEM(*o) for o in outs]
        + [
            pltpu.SemaphoreType.DMA((1, 3, depth)),
            pltpu.SemaphoreType.DMA((1, wide_count)),
            pltpu.SemaphoreType.DMA,
            pltpu.SemaphoreType.DMA((5, wide_count)),
        ],
        compiler_params=pltpu.CompilerParams(
            collective_id=collective_id, has_side_effects=True, vmem_limit_bytes=60 << 20
        ),
        name="forward_gathered",
    )(local, gate_weight, up_weight, down_weight)
    return [r.reshape(wide_count * rows, r.shape[2]) for r in results]


def tn(left, right):
    return lax.dot_general(
        left, right, (((0,), (0,)), ((), ())), preferred_element_type=jnp.float32
    )


def backward_scattered(
    cot, gates, ups, hidden_rows, carried, gate_weight, up_weight, down_weight, wide_count, collective_id
):
    model = cot.shape[1]
    rows = cot.shape[0] // wide_count
    hidden = gate_weight.shape[1]
    depth = wide_count // 2
    tile = min(256, hidden)
    wide_tile = min(512, model)
    low = jnp.bfloat16

    half = model // 2
    slab = min(256, half)
    per = half // slab

    def kernel(
        cot_ref, gates_ref, ups_ref, hidden_ref, carried_ref, gate_ref, up_ref, down_ref,
        sum_ref, gate_half_ref, up_half_ref, swapped_ref,
        cots, gate_in, up_in, gate_low, up_low, foreign, own, crossed, from_low, from_high,
        columns, given, taken, kept,
        in_sems, cross_send, cross_recv, chain_send, low_recv, high_recv,
        column_sems, give_send, give_recv, kept_sems, carry_sems,
    ):
        lat = Lattice(wide_count)
        z, x, last = lat.z, lat.x, depth - 1
        narrow = lax.axis_index("narrow")
        core = narrow % 2
        partner = narrow + 1 - 2 * core
        across = (narrow + 2) % 4

        def place(e):
            zz = lat.order(depth - 1 - e % depth)[0]
            return zz, lat.at(zz, jnp.where(e < depth, 1 - x, x))

        def loads(e):
            slot = e % 2
            chunk = place(e)[1]
            return [
                pltpu.make_async_copy(source.at[chunk], target.at[slot], in_sems.at[k, slot])
                for k, (source, target) in enumerate(
                    ((cot_ref, cots), (gates_ref, gate_in), (ups_ref, up_in))
                )
            ]

        def cross(zz):
            return pltpu.make_async_remote_copy(
                src_ref=foreign.at[zz], dst_ref=crossed.at[zz],
                send_sem=cross_send.at[zz], recv_sem=cross_recv.at[zz],
                device_id={"wide": lat.at(z, 1 - x)}, device_id_type=MESH,
            )

        def rise(zz):
            return pltpu.make_async_remote_copy(
                src_ref=own.at[zz], dst_ref=from_low.at[zz],
                send_sem=chain_send.at[zz], recv_sem=low_recv.at[zz],
                device_id={"wide": lat.at(z + 1, x)}, device_id_type=MESH,
            )

        def sink(zz):
            return pltpu.make_async_remote_copy(
                src_ref=own.at[zz], dst_ref=from_high.at[zz],
                send_sem=chain_send.at[zz], recv_sem=high_recv.at[zz],
                device_id={"wide": lat.at(z - 1, x)}, device_id_type=MESH,
            )

        def slab_of(e):
            side = jnp.where(e < 2 * per, 1 - core, core)
            return e // per % 2, e % per, side * per + e % per

        def column_load(e):
            at = pl.ds(pl.multiple_of(slab_of(e)[2] * slab, slab), slab)
            return pltpu.make_async_copy(
                hidden_ref.at[:, :, at], columns.at[e % 2], column_sems.at[e % 2]
            )

        def give(e):
            which, n, _ = slab_of(e)
            return pltpu.make_async_remote_copy(
                src_ref=given.at[e % 2], dst_ref=taken.at[which, n],
                send_sem=give_send.at[e % 2], recv_sem=give_recv.at[which, n],
                device_id={"narrow": partner}, device_id_type=MESH,
            )

        def keep(e, k):
            target = (gate_half_ref, up_half_ref)[k]
            return pltpu.make_async_copy(kept.at[e % 2], target.at[slab_of(e)[1]], kept_sems.at[e % 2])

        def weight_slab(e):
            which, n, _ = slab_of(e)
            column_load(e).wait()

            @pl.when(e + 1 < 4 * per)
            def _():
                column_load(e + 1).start()

            tokens = columns[e % 2].reshape(wide_count * rows, slab)

            @pl.when((e >= 2) & (e < 2 * per + 2))
            def _():
                give(e - 2).wait_send()

            @pl.when(e >= 2 * per + 2)
            def _():
                keep(e - 2, 0).wait()

            def product(k):
                source = (gate_low, up_low)[k]
                value = tn(tokens, source[...].reshape(wide_count * rows, hidden))

                @pl.when(e < 2 * per)
                def _():
                    given[e % 2] = value.astype(low)
                    give(e).start()

                @pl.when(e >= 2 * per)
                def _():
                    give(e).wait_recv()
                    kept[e % 2] = (value + taken[k, n].astype(jnp.float32)).astype(low)
                    keep(e, k).start()

            @pl.when(which == 0)
            def _():
                product(0)

            @pl.when(which == 1)
            def _():
                product(1)

        for copy in loads(0):
            copy.start()
        column_load(0).start()
        greet(lat, (partner, across))
        carry = pltpu.make_async_remote_copy(
            src_ref=carried_ref, dst_ref=swapped_ref,
            send_sem=carry_sems.at[0], recv_sem=carry_sems.at[1],
            device_id={"narrow": across}, device_id_type=MESH,
        )
        carry.start()

        def partial(e, target, zz):
            slot = e % 2
            for copy in loads(e):
                copy.wait()

            @pl.when(e + 1 < 2 * depth)
            def _():
                for copy in loads(e + 1):
                    copy.start()

            cot_rows = cots[slot]
            chunk = place(e)[1]

            def inner(t, carry):
                at = pl.ds(pl.multiple_of(t * tile, tile), tile)
                act_grad = nt(cot_rows, down_ref[at, :])
                gate, up = gate_in[slot, :, at], up_in[slot, :, at]
                sigmoid = lax.logistic(gate)
                gate_low[chunk, :, at] = (
                    act_grad * up * sigmoid * (1.0 + gate * (1.0 - sigmoid))
                ).astype(low)
                up_low[chunk, :, at] = (act_grad * gate * sigmoid).astype(low)
                return carry

            lax.fori_loop(0, hidden // tile, inner, 0)
            gate_rows, up_rows = gate_low[chunk], up_low[chunk]

            def outer(t, carry):
                at = pl.ds(pl.multiple_of(t * wide_tile, wide_tile), wide_tile)
                target[zz, :, at] = (
                    nt(gate_rows, gate_ref[at, :]) + nt(up_rows, up_ref[at, :])
                ).astype(low)
                return carry

            lax.fori_loop(0, model // wide_tile, outer, 0)

        def send_step(e, carry):
            zz, _ = place(e)
            partial(e, foreign, zz)
            cross(zz).start()
            return carry

        lax.fori_loop(0, depth, send_step, 0)

        def own_step(e, carry):
            zz, _ = place(e)
            partial(e, own, zz)

            @pl.when(e == depth)
            def _():
                chain(zz)

            return carry

        def chain(zz):
            cross(zz).wait_recv()
            wide = jnp.float32

            @pl.when((zz > z) & (z > 0))
            def _():
                rise(zz).wait_recv()
                own[zz] = (own[zz].astype(wide) + crossed[zz].astype(wide) + from_low[zz].astype(wide)).astype(low)

            @pl.when((zz < z) & (z < last))
            def _():
                sink(zz).wait_recv()
                own[zz] = (own[zz].astype(wide) + crossed[zz].astype(wide) + from_high[zz].astype(wide)).astype(low)

            @pl.when(((zz > z) & (z == 0)) | ((zz < z) & (z == last)))
            def _():
                own[zz] = (own[zz].astype(wide) + crossed[zz].astype(wide)).astype(low)

            @pl.when(zz > z)
            def _():
                rise(zz).start()

            @pl.when(zz < z)
            def _():
                sink(zz).start()

            @pl.when(zz == z)
            def _():
                sum_ref[...] = own[zz].astype(wide) + crossed[zz].astype(wide)

                @pl.when(z > 0)
                def _():
                    rise(zz).wait_recv()
                    sum_ref[...] += from_low[zz].astype(wide)

                @pl.when(z < last)
                def _():
                    sink(zz).wait_recv()
                    sum_ref[...] += from_high[zz].astype(wide)

        lax.fori_loop(depth, 2 * depth, own_step, 0)

        def slab_step(e, carry):
            for k in range(1, depth):
                @pl.when(e == 4 * per * (k - 1) // (depth - 2))
                def _():
                    chain(place(depth + k)[0])

            @pl.when(e < 4 * per)
            def _():
                weight_slab(e)

            return carry

        lax.fori_loop(0, 4 * per + 1, slab_step, 0)
        for e in (4 * per - 2, 4 * per - 1):
            keep(e, 1).wait()
        carry.wait()

        def settle(zz, carry):
            cross(zz).wait_send()

            @pl.when(zz > z)
            def _():
                rise(zz).wait_send()

            @pl.when(zz < z)
            def _():
                sink(zz).wait_send()

            return carry

        lax.fori_loop(0, depth, settle, 0)

    vmem = pl.BlockSpec(memory_space=pltpu.VMEM)
    hbm = pl.BlockSpec(memory_space=pl.ANY)
    total, gate_half, up_half, swapped = pl.pallas_call(
        kernel,
        in_specs=[hbm, hbm, hbm, hbm, hbm, vmem, vmem, vmem],
        out_specs=[vmem, hbm, hbm, hbm],
        out_shape=[
            jax.ShapeDtypeStruct((rows, model), jnp.float32),
            jax.ShapeDtypeStruct((per, slab, hidden), low),
            jax.ShapeDtypeStruct((per, slab, hidden), low),
            jax.ShapeDtypeStruct(carried.shape, low),
        ],
        scratch_shapes=[
            pltpu.VMEM((2, rows, model), low),
            pltpu.VMEM((2, rows, hidden), jnp.float32),
            pltpu.VMEM((2, rows, hidden), jnp.float32),
            pltpu.VMEM((wide_count, rows, hidden), low),
            pltpu.VMEM((wide_count, rows, hidden), low),
        ]
        + [pltpu.VMEM((depth, rows, model), low)] * 5
        + [
            pltpu.VMEM((2, wide_count, rows, slab), low),
            pltpu.VMEM((2, slab, hidden), low),
            pltpu.VMEM((2, per, slab, hidden), low),
            pltpu.VMEM((2, slab, hidden), low),
            pltpu.SemaphoreType.DMA((3, 2)),
        ]
        + [pltpu.SemaphoreType.DMA((depth,))] * 5
        + [
            pltpu.SemaphoreType.DMA((2,)),
            pltpu.SemaphoreType.DMA((2,)),
            pltpu.SemaphoreType.DMA((2, per)),
            pltpu.SemaphoreType.DMA((2,)),
            pltpu.SemaphoreType.DMA((2,)),
        ],
        compiler_params=pltpu.CompilerParams(
            collective_id=collective_id, has_side_effects=True, vmem_limit_bytes=67043328
        ),
        name="backward_scattered",
    )(
        cot.reshape(wide_count, rows, model),
        gates.reshape(wide_count, rows, hidden),
        ups.reshape(wide_count, rows, hidden),
        hidden_rows.reshape(wide_count, rows, model),
        carried,
        gate_weight, up_weight, down_weight,
    )
    return total, gate_half.reshape(half, hidden), up_half.reshape(half, hidden), swapped


AXES = ("narrow", "wide")


def peers(k, counts, act):
    here = lax.axis_index(AXES[k])

    def one(step, carry):
        act((here + step) % counts[k])
        return carry

    lax.fori_loop(1, counts[k], one, 0)


def greet_all(counts):
    barrier = pltpu.get_barrier_semaphore()
    for k, axis in enumerate(AXES):
        peers(k, counts, lambda who: pl.semaphore_signal(
            barrier, inc=1, device_id={axis: who}, device_id_type=MESH))
    return lambda: pl.semaphore_wait(barrier, counts[0] + counts[1] - 2)


class Exchange:
    def __init__(self, k, counts, source, slots, sends, recvs):
        self.k, self.counts, self.source = k, counts, source
        self.slots, self.sends, self.recvs = slots, sends, recvs
        self.here = lax.axis_index(AXES[k])

    def copy(self, who, slot):
        return pltpu.make_async_remote_copy(
            src_ref=self.source, dst_ref=self.slots.at[slot],
            send_sem=self.sends.at[who], recv_sem=self.recvs.at[slot],
            device_id={AXES[self.k]: who}, device_id_type=MESH,
        )

    def start(self):
        peers(self.k, self.counts, lambda who: self.copy(who, self.here).start())
        self.slots[self.here] = self.source[...]

    def total(self):
        peers(self.k, self.counts, lambda who: self.copy(who, who).wait_recv())
        sums = self.slots[0]
        for n in range(1, self.counts[self.k]):
            sums = sums + self.slots[n]
        return sums

    def settle(self):
        peers(self.k, self.counts, lambda who: self.copy(who, self.here).wait_send())


def exchange_scratch(shape, counts):
    return [
        pltpu.VMEM(shape, jnp.float32),
        pltpu.VMEM((2, max(counts)) + shape, jnp.float32),
        pltpu.VMEM(shape, jnp.float32),
        pltpu.SemaphoreType.DMA,
        pltpu.SemaphoreType.DMA((counts[0],)),
        pltpu.SemaphoreType.DMA((counts[0],)),
        pltpu.SemaphoreType.DMA((counts[1],)),
        pltpu.SemaphoreType.DMA((counts[1],)),
    ]


def exchange_pair(counts, mine, held, total, narrow_send, narrow_recv, wide_send, wide_recv):
    return (
        Exchange(0, counts, mine, held.at[0], narrow_send, narrow_recv),
        Exchange(1, counts, total, held.at[1], wide_send, wide_recv),
    )


def sum_everywhere(values, counts, collective_id):
    def kernel(in_ref, out_ref, mine, held, total, load_sem, *sems):
        load = pltpu.make_async_copy(in_ref, mine, load_sem)
        load.start()
        arrive = greet_all(counts)
        load.wait()
        arrive()
        narrow, wide = exchange_pair(counts, mine, held, total, *sems)
        narrow.start()
        total[...] = narrow.total()
        wide.start()
        out_ref[...] = wide.total()
        narrow.settle()
        wide.settle()

    return pl.pallas_call(
        kernel,
        in_specs=[pl.BlockSpec(memory_space=pl.ANY)],
        out_specs=pl.BlockSpec(memory_space=pltpu.VMEM),
        out_shape=jax.ShapeDtypeStruct(values.shape, jnp.float32),
        scratch_shapes=exchange_scratch(values.shape, counts),
        compiler_params=pltpu.CompilerParams(collective_id=collective_id, has_side_effects=True),
        name="sum_everywhere",
    )(values)

CORPORA = 8
GATHER_BYTES = 8 << 20


def norm_scale(values, scale_gain):
    return (
        values * lax.rsqrt(jnp.mean(values * values, axis=-1, keepdims=True) + epsilon) * scale_gain
    )


def contract_first(left, right):
    return lax.dot_general(
        left, right, (((0,), (0,)), ((), ())), preferred_element_type=jnp.float32
    )


def gather_wide(values):
    return lax.all_gather(values, "wide", axis=0, tiled=True)


def scatter_wide(values):
    return lax.psum_scatter(
        values.astype(jnp.bfloat16), "wide", scatter_dimension=0, tiled=True
    ).astype(jnp.float32)


def own_part(values, axis, index, count):
    size = values.shape[axis] // count
    return lax.dynamic_slice_in_dim(values, index * size, size, axis)


def swap_narrow(values, bit):
    count = lax.axis_size("narrow")
    return lax.ppermute(values, "narrow", [(i, i ^ bit) for i in range(count)])


def keep_half(values, axis, bit):
    side = lax.axis_index("narrow") // bit % 2
    mine = lax.dynamic_index_in_dim(values, side, axis, keepdims=False)
    other = lax.dynamic_index_in_dim(values, 1 - side, axis, keepdims=False)
    return add_low(mine, swap_narrow(other, bit))


def add_low(left, right):
    return (left.astype(jnp.float32) + right.astype(jnp.float32)).astype(jnp.bfloat16)


def core_half(values):
    rows, columns = values.shape
    return keep_half(values.astype(jnp.bfloat16).reshape(2, rows // 2, columns), 0, 1)


def sum_narrow(values):
    half = core_half(values)
    return hand_back(add_low(half, swap_narrow(half, 2)))


def hand_back(half):
    other = swap_narrow(half, 1)
    first = lax.axis_index("narrow") % 2 == 0
    return jnp.concatenate(
        [jnp.where(first, half, other), jnp.where(first, other, half)], axis=0
    ).astype(jnp.float32)


def swiglu_back(act_grad, gate_values, up_values):
    sigmoid_gate = lax.logistic(gate_values)
    gate_part = act_grad * up_values * sigmoid_gate * (1.0 + gate_values * (1.0 - sigmoid_gate))
    up_part = act_grad * gate_values * sigmoid_gate
    return (gate_part.astype(jnp.bfloat16), up_part.astype(jnp.bfloat16))


def shards(
    tokens,
    attention_gain,
    query_weight,
    key_weight,
    value_weight,
    query_gain,
    key_gain,
    output_weight,
    feedforward_gain,
    gate_weight,
    up_weight,
    down_weight,
    cotangent,
    corpus_tags,
    segments,
):
    low, wide_type = jnp.bfloat16, jnp.float32
    head_size = query_gain.shape[0]
    own_rows, model_width = tokens.shape
    wide_count, narrow_count = lax.axis_size("wide"), lax.axis_size("narrow")
    wide_index, narrow_index = lax.axis_index("wide"), lax.axis_index("narrow")
    key_total = key_weight.shape[1] // head_size
    width = query_weight.shape[1]
    key_head = wide_index * key_total // wide_count
    all_rows = own_rows * wide_count
    chained = wide_count % 2 == 0 and all_rows * model_width * 2 <= GATHER_BYTES

    tag_hits = corpus_tags[:, None] == jnp.arange(CORPORA, dtype=jnp.int32)[None, :]
    local_counts = jnp.sum(tag_hits.astype(wide_type), axis=0)
    local_counts = jnp.pad(local_counts[None], ((0, 7), (0, 128 - CORPORA)))
    token_values = tokens.astype(wide_type)
    first_gain = attention_gain.astype(wide_type)
    second_gain = feedforward_gain.astype(wide_type)

    key_columns = lax.dynamic_slice_in_dim(key_weight, key_head * head_size, head_size, 1)
    value_columns = lax.dynamic_slice_in_dim(value_weight, key_head * head_size, head_size, 1)
    own_weights = jnp.concatenate([query_weight, key_columns, value_columns], axis=1)
    strip = width // narrow_count

    def gather_strips(part):
        return lax.all_gather(gather_wide(part), "narrow", axis=0, tiled=True)

    def narrow_first(values):
        values = values.reshape(-1, wide_count, narrow_count, strip)
        return values.transpose(0, 2, 1, 3).reshape(-1, wide_count * width)

    def wide_first(values):
        values = values.reshape(-1, narrow_count, wide_count, strip)
        return values.transpose(0, 2, 1, 3).reshape(-1, wide_count * width)

    strips = [
        own_part(output_weight, 0, narrow_index, narrow_count),
        jnp.transpose(own_part(query_weight, 1, narrow_index, narrow_count)),
    ]
    hidden_local = norm_scale(token_values, first_gain).astype(low)
    if chained:
        hidden_one, raw, corpus_counts, gathered = project_gathered(
            hidden_local, own_weights, local_counts, strips, (narrow_count, wide_count), 2
        )
    else:
        hidden_one = gather_wide(hidden_local)
        raw = dot_nn(hidden_one, own_weights)
        corpus_counts = sum_everywhere(local_counts, (narrow_count, wide_count), 1)
        gathered = [gather_strips(part) for part in strips]
    output_full, query_turned = gathered
    corpus_counts = corpus_counts[0, :CORPORA]
    corpus_scale = jnp.sqrt(jnp.sum(corpus_counts) / (CORPORA * corpus_counts))
    row_weight = jnp.sum(jnp.where(tag_hits, corpus_scale[None, :], 0.0), axis=1)
    out_cot = cotangent.astype(wide_type) * row_weight[:, None]
    cot_low, raw = lax.optimization_barrier((out_cot.astype(low), raw))
    cot_low = gather_wide(cot_low)

    first_block = first_blocks(segments)
    saved = attention_forward(raw, query_gain, key_gain, segments, first_block)
    mixed = narrow_first(lax.all_to_all(saved[0], "wide", split_axis=0, concat_axis=1, tiled=True))
    middle = token_values + dot_nn(mixed, output_full)

    together = lax.optimization_barrier
    hidden_two_local = norm_scale(middle, second_gain).astype(low)
    if chained:
        hidden_two, gate_values, up_values, activated, down_part = forward_gathered(
            hidden_two_local, gate_weight, up_weight, down_weight, wide_count, 3
        )
        down_half = core_half(contract_first(activated, cot_low))
        hidden_two_grad, gate_half, up_half, down_other = backward_scattered(
            cot_low, gate_values, up_values, hidden_two, down_half, gate_weight, up_weight, down_weight,
            wide_count, 4,
        )
        down_part, hidden_two_grad = together((down_part, hidden_two_grad))
    else:
        hidden_two = gather_wide(hidden_two_local)
        gate_values = dot_nn(hidden_two, gate_weight)
        up_values = dot_nn(hidden_two, up_weight)
        activated = (gate_values * lax.logistic(gate_values) * up_values).astype(low)
        down_part = dot_nn(activated, down_weight)
        down_half = core_half(contract_first(activated, cot_low))
        gate_low, up_low = swiglu_back(dot_nt(cot_low, down_weight), gate_values, up_values)
        hidden_two_grad = scatter_wide(dot_nt(gate_low, gate_weight) + dot_nt(up_low, up_weight))
        gate_half = core_half(contract_first(hidden_two, gate_low))
        up_half = core_half(contract_first(hidden_two, up_low))
        down_other = swap_narrow(down_half, 2)
    down_half = add_low(down_half, down_other)
    hidden_two_grad, down_half = together((hidden_two_grad, down_half))
    down_sum = scatter_wide(down_part)

    _, second_pull = jax.vjp(norm_scale, middle, second_gain)
    middle_part, second_gain_grad = second_pull(hidden_two_grad)
    middle_grad = out_cot + middle_part
    middle_low = middle_grad.astype(low)
    mixed_grad = wide_first(dot_nt(middle_low, output_full).astype(low))
    mixed_grad, mixed, middle_low = together((mixed_grad, mixed, middle_low))
    mixed_grad = lax.all_to_all(mixed_grad, "wide", split_axis=1, concat_axis=0, tiled=True)
    output_part = contract_first(mixed, middle_low).astype(low)
    output_part = output_part.reshape(2, 2, wide_count * strip, model_width)
    output_part = keep_half(output_part, 1, 1)
    mixed_grad, output_part = together((mixed_grad, output_part))
    output_part = keep_half(output_part, 0, 2)
    gate_half = add_low(gate_half, swap_narrow(gate_half, 2))
    grads, query_gain_grad, key_gain_grad = attention_backward(
        raw, query_gain, key_gain, segments, first_block, saved, mixed_grad
    )
    grads, output_part, gate_half, up_half = together((grads, output_part, gate_half, up_half))
    up_half = add_low(up_half, swap_narrow(up_half, 2))
    sent = lax.all_to_all(grads, "wide", split_axis=0, concat_axis=1, tiled=True).reshape(
        own_rows, wide_count, width + 2 * head_size
    )
    sent, down_sum, output_part = together((sent, down_sum, output_part))
    output_part = output_part.reshape(wide_count, strip, model_width)
    output_part = lax.all_to_all(output_part, "wide", split_axis=0, concat_axis=0, tiled=True)
    output_part = jnp.sum(output_part.astype(wide_type), axis=0).astype(low)
    output_grad = lax.all_gather(output_part, "narrow", axis=0, tiled=True).astype(wide_type)
    down_grad, gate_grad, up_grad = (hand_back(h) for h in (down_half, gate_half, up_half))
    shared = wide_count // key_total

    def key_side(start):
        part = sent[:, :, start : start + head_size]
        if shared > 1:
            part = jnp.sum(
                part.astype(wide_type).reshape(own_rows, key_total, shared, head_size), axis=2
            ).astype(low)
        return part.reshape(own_rows, key_total * head_size)

    hidden_one_grad = (
        dot_nn(narrow_first(sent[:, :, :width]), query_turned)
        + dot_nt(key_side(width), key_weight)
        + dot_nt(key_side(width + head_size), value_weight)
    )
    _, first_pull = jax.vjp(norm_scale, token_values, first_gain)
    token_part, first_gain_grad = first_pull(hidden_one_grad)
    tokens_gradient = (middle_grad + token_part).astype(low)
    tokens_gradient, down_sum = lax.optimization_barrier((tokens_gradient, down_sum))
    result = (middle + down_sum).astype(low)

    weight_grads = contract_first(hidden_one, grads)
    if shared == 1:
        weight_sums = sum_narrow(weight_grads)
        key_weight_grad = weight_sums[:, width : width + head_size]
        value_weight_grad = weight_sums[:, width + head_size :]
    else:
        weight_sums = sum_narrow(weight_grads[:, :width])

        def spread(part):
            whole = jnp.zeros((model_width, key_total * head_size), wide_type)
            whole = lax.dynamic_update_slice_in_dim(whole, part, key_head * head_size, 1)
            share = lax.psum_scatter(whole.astype(low), "wide", scatter_dimension=1, tiled=True)
            return lax.psum(share, "narrow").astype(wide_type)

        key_weight_grad = spread(weight_grads[:, width : width + head_size])
        value_weight_grad = spread(weight_grads[:, width + head_size :])

    gain_parts = jnp.concatenate([first_gain_grad, second_gain_grad, query_gain_grad, key_gain_grad])
    lines = -(-gain_parts.shape[0] // 1024) * 8
    gain_parts = jnp.pad(gain_parts, (0, lines * 128 - gain_parts.shape[0])).reshape(lines, 128)
    gains = sum_everywhere(gain_parts, (narrow_count, wide_count), 5).reshape(-1)
    starts = (0, model_width, 2 * model_width, 2 * model_width + head_size)
    sizes = (model_width, model_width, head_size, head_size)
    first_out, second_out, query_gain_out, key_gain_out = (
        own_part(gains[start : start + size], 0, wide_index, wide_count)
        for start, size in zip(starts, sizes)
    )
    return (
        result,
        tokens_gradient,
        first_out,
        weight_sums[:, :width],
        key_weight_grad,
        value_weight_grad,
        query_gain_out,
        key_gain_out,
        output_grad,
        second_out,
        gate_grad,
        up_grad,
        down_grad,
    )


def solution(mesh):
    rows = P(("narrow", "wide"), None)
    columns, first = P(None, "wide"), P("wide", None)
    return jax.shard_map(
        shards,
        mesh=mesh,
        in_specs=(
            rows, P(), columns, P(), P(), P(), P(), first, P(), columns, columns, first,
            rows, P(("narrow", "wide")), P("narrow", None),
        ),
        out_specs=(
            rows, rows, P("wide"), columns, columns, columns, P("wide"), P("wide"),
            first, P("wide"), columns, columns, first,
        ),
        check_vma=False,
    )
```

```python
import numpy as np

import jax
import jax.numpy as jnp
from jax import lax
from jax.experimental import pallas as pl
from jax.experimental.pallas import tpu as pltpu
from jax.sharding import PartitionSpec as P

SEQ = 2048
epsilon = 1e-06
rope_base = 10000.0
BLOCK = 256
NEG = -1e30


def rope_tables(head_size):
    positions = np.arange(SEQ, dtype=np.float32)
    exponents = np.arange(head_size // 2, dtype=np.float32) * np.float32(2.0 / head_size)
    frequency = np.power(np.float32(rope_base), -exponents).astype(np.float32)
    angles = (positions[:, None] * frequency[None, :]).astype(np.float32)
    cosine, sine = np.cos(angles).astype(np.float32), np.sin(angles).astype(np.float32)
    return (
        np.concatenate([cosine, cosine], axis=1),
        np.concatenate([-sine, sine], axis=1),
    )


def dot_nn(left, right):
    return jnp.dot(left, right, preferred_element_type=jnp.float32)


def dot_nt(left, right):
    return lax.dot_general(
        left, right, (((1,), (1,)), ((), ())), preferred_element_type=jnp.float32
    )


def lane_ids(shape):
    return lax.broadcasted_iota(jnp.int32, shape, 1)


def group_ones(width, head_size):
    rows = lax.broadcasted_iota(jnp.int32, (width, width), 0) // head_size
    columns = lax.broadcasted_iota(jnp.int32, (width, width), 1) // head_size
    return jnp.where(rows == columns, 1.0, 0.0).astype(jnp.bfloat16)


def group_sum(values, ones):
    top = values.astype(jnp.bfloat16)
    rest = (values - top.astype(jnp.float32)).astype(jnp.bfloat16)
    return dot_nn(top, ones) + dot_nn(rest, ones)


def swap_halves(values, head_size):
    width, half = values.shape[1], head_size // 2
    if width == head_size:
        return jnp.concatenate([values[:, half:], values[:, :half]], axis=1)
    ahead = pltpu.roll(values, width - half, 1)
    behind = pltpu.roll(values, half, 1)
    return jnp.where(lane_ids(values.shape) % head_size < half, ahead, behind)


def tiled(values, count):
    return jnp.concatenate([values] * count, axis=1) if count > 1 else values


def split_raw(raw, width, head_size, heads):
    query = raw[:, :width]
    key = tiled(raw[:, width : width + head_size], heads)
    value = tiled(raw[:, width + head_size :], heads)
    return query, key, value


def head_masks(block, width, head_size, heads):
    group = lane_ids((block, width)) // head_size
    return [group == h for h in range(heads)]


def attention_forward(raw, query_gain, key_gain, segments, first_block):
    head_size = query_gain.shape[0]
    rows = raw.shape[0]
    heads = raw.shape[1] // head_size - 2
    width = heads * head_size
    seqs, blocks, block = rows // SEQ, SEQ // BLOCK, BLOCK
    scale = head_size ** (-0.5)

    def kernel(
        first_ref, raw_ref, qg_ref, kg_ref, cos_ref, sin_ref, segq_ref, segk_ref,
        mixed_ref, lse_ref, query_ref, key_ref, value_ref, keyt_ref,
        keys, values_t, masked, top, total, acc,
    ):
        s, i = pl.program_id(0), pl.program_id(1)
        cosine, sine = tiled(cos_ref[...], heads), tiled(sin_ref[...], heads)
        ones = group_ones(width, head_size)
        query, key, value = split_raw(raw_ref[...], width, head_size, heads)

        def norm_rope(x, gain):
            x = x * lax.rsqrt(group_sum(x * x, ones) * (1.0 / head_size) + epsilon) * gain
            return x * cosine + swap_halves(x, head_size) * sine

        query_low = norm_rope(query, qg_ref[...]).astype(jnp.bfloat16)
        key_rot = norm_rope(key, kg_ref[...])
        key_low = key_rot.astype(jnp.bfloat16)
        query_ref[...] = query_low
        key_ref[...] = key_low
        value_ref[...] = value.astype(jnp.bfloat16)
        keyt_ref[0] = jnp.transpose(key_rot)[:head_size].astype(jnp.bfloat16)
        keys[pl.ds(pl.multiple_of(i * block, block), block), :] = key_low
        values_t[i] = jnp.transpose(value)[:head_size].astype(jnp.bfloat16)
        scaled = query_low * jnp.bfloat16(scale)
        zero = jnp.zeros_like(scaled)
        for h, mask in enumerate(head_masks(block, width, head_size, heads)):
            masked[h] = jnp.where(mask, scaled, zero)
        top[...] = jnp.full_like(top, NEG)
        total[...] = jnp.zeros_like(total)
        acc[...] = jnp.zeros_like(acc)
        query_pos = i * block + lax.broadcasted_iota(jnp.int32, (block, block), 1)
        segment_query = segq_ref[0]

        def step(j, carry):
            at = pl.multiple_of(j * block, block)
            key_pos = at + lax.broadcasted_iota(jnp.int32, (block, block), 0)
            allowed = (key_pos <= query_pos) & (segk_ref[pl.ds(at, block), :] == segment_query)
            bias = jnp.where(allowed, 0.0, NEG)
            key_block = keys[pl.ds(at, block), :]
            value_t = values_t[j]
            for h in range(heads):
                scores = dot_nt(key_block, masked[h]) + bias
                before = top[h : h + 1, :]
                now = jnp.maximum(before, jnp.max(scores, axis=0, keepdims=True))
                shifted = jnp.exp(scores - now)
                fade = jnp.exp(before - now)
                top[h : h + 1, :] = now
                total[h : h + 1, :] = fade * total[h : h + 1, :] + jnp.sum(
                    shifted, axis=0, keepdims=True
                )
                span = slice(h * head_size, (h + 1) * head_size)
                acc[span, :] = fade * acc[span, :] + dot_nn(value_t, shifted.astype(jnp.bfloat16))
            return carry

        lax.fori_loop(first_ref[s, i], i + 1, step, 0)
        for h in range(heads):
            span = slice(h * head_size, (h + 1) * head_size)
            acc[span, :] = acc[span, :] / total[h : h + 1, :]
        mixed_ref[...] = jnp.transpose(acc[...]).astype(jnp.bfloat16)
        lse_ref[...] = top[...] + jnp.log(jnp.maximum(total[...], 1e-30))

    cosine, sine = rope_tables(head_size)
    at_rows = lambda s, i, first: (s * blocks + i, 0)
    fixed = lambda s, i, first: (0, 0)
    at_lanes = lambda s, i, first: (0, s * blocks + i)
    low = jnp.bfloat16
    pairs = blocks * (blocks + 1) // 2 * seqs * heads
    return pl.pallas_call(
        kernel,
        grid_spec=pltpu.PrefetchScalarGridSpec(
            num_scalar_prefetch=1,
            grid=(seqs, blocks),
            in_specs=[
                pl.BlockSpec((block, raw.shape[1]), at_rows),
                pl.BlockSpec((1, width), fixed),
                pl.BlockSpec((1, width), fixed),
                pl.BlockSpec((block, head_size), lambda s, i, first: (i, 0)),
                pl.BlockSpec((block, head_size), lambda s, i, first: (i, 0)),
                pl.BlockSpec((1, 1, block), lambda s, i, first: (s, 0, i)),
                pl.BlockSpec((SEQ, 1), lambda s, i, first: (s, 0)),
            ],
            out_specs=[
                pl.BlockSpec((block, width), at_rows),
                pl.BlockSpec((8, block), at_lanes),
                pl.BlockSpec((block, width), at_rows),
                pl.BlockSpec((block, width), at_rows),
                pl.BlockSpec((block, width), at_rows),
                pl.BlockSpec((1, head_size, block), lambda s, i, first: (s * blocks + i, 0, 0)),
            ],
            scratch_shapes=[
                pltpu.VMEM((SEQ, width), low),
                pltpu.VMEM((blocks, head_size, block), low),
                pltpu.VMEM((heads, block, width), low),
                pltpu.VMEM((8, block), jnp.float32),
                pltpu.VMEM((8, block), jnp.float32),
                pltpu.VMEM((width, block), jnp.float32),
            ],
        ),
        out_shape=[
            jax.ShapeDtypeStruct((rows, width), low),
            jax.ShapeDtypeStruct((8, rows), jnp.float32),
            jax.ShapeDtypeStruct((rows, width), low),
            jax.ShapeDtypeStruct((rows, width), low),
            jax.ShapeDtypeStruct((rows, width), low),
            jax.ShapeDtypeStruct((rows // block, head_size, block), low),
        ],
        compiler_params=pltpu.CompilerParams(vmem_limit_bytes=40 << 20),
        cost_estimate=pl.CostEstimate(flops=0, bytes_accessed=0, transcendentals=0),
        name="attention_forward",
    )(
        first_block, raw,
        tiled(query_gain.astype(jnp.float32)[None], heads),
        tiled(key_gain.astype(jnp.float32)[None], heads),
        cosine, sine, segments[:, None, :], segments.reshape(rows, 1),
    )


def attention_backward(
    raw, query_gain, key_gain, segments, first_block, saved, mixed_grad
):
    mixed, lse, query_low, key_low, value_low, key_t = saved
    head_size = query_gain.shape[0]
    rows, width = mixed.shape
    heads = width // head_size
    seqs, blocks, block = rows // SEQ, SEQ // BLOCK, BLOCK
    scale = head_size ** (-0.5)

    def kernel(
        first_ref, raw_ref, qg_ref, kg_ref, cos_ref, sin_ref, segq_ref, segk_ref,
        mixed_ref, lse_ref, query_ref, grad_ref, keys_ref, values_ref, keyt_ref,
        out_ref, qgg_ref, kgg_ref,
        masked, masked_grad, key_sums, value_sums, query_sums, deltas,
    ):
        s, i = pl.program_id(0), blocks - 1 - pl.program_id(1)

        @pl.when(pl.program_id(1) == 0)
        def _():
            key_sums[...] = jnp.zeros_like(key_sums)
            value_sums[...] = jnp.zeros_like(value_sums)

        @pl.when((pl.program_id(1) == 0) & (s == 0))
        def _():
            qgg_ref[...] = jnp.zeros_like(qgg_ref)
            kgg_ref[...] = jnp.zeros_like(kgg_ref)

        query_sums[...] = jnp.zeros_like(query_sums)
        grad = grad_ref[...]
        scaled = query_ref[...] * jnp.bfloat16(scale)
        zero = jnp.zeros_like(scaled)
        for h, mask in enumerate(head_masks(block, width, head_size, heads)):
            span = slice(h * block, (h + 1) * block)
            masked[span, :] = jnp.where(mask, scaled, zero)
            masked_grad[span, :] = jnp.where(mask, grad, zero)
        product = jnp.transpose(grad.astype(jnp.float32) * mixed_ref[...].astype(jnp.float32))
        for h in range(heads):
            deltas[h : h + 1, :] = jnp.sum(
                product[h * head_size : (h + 1) * head_size], axis=0, keepdims=True
            )
        query_pos = i * block + lax.broadcasted_iota(jnp.int32, (block, block), 1)
        segment_query = segq_ref[0]

        def step(j, carry):
            at = pl.multiple_of(j * block, block)
            key_pos = at + lax.broadcasted_iota(jnp.int32, (block, block), 0)
            allowed = (key_pos <= query_pos) & (segk_ref[pl.ds(at, block), :] == segment_query)
            bias = jnp.where(allowed, 0.0, NEG)
            key_block = keys_ref[pl.ds(at, block), :]
            value_block = values_ref[pl.ds(at, block), :]
            key_t = keyt_ref[j]
            lows, grads = [], []
            for h in range(heads):
                span = slice(h * block, (h + 1) * block)
                scores = dot_nt(key_block, masked[span, :]) + bias
                probability = jnp.exp(scores - lse_ref[h : h + 1, :])
                prob_grad = dot_nt(value_block, masked_grad[span, :])
                score_grad = (probability * (prob_grad - deltas[h : h + 1, :])).astype(jnp.bfloat16)
                lows.append(probability.astype(jnp.bfloat16))
                grads.append(score_grad)
                rows_h = slice(h * head_size, (h + 1) * head_size)
                query_sums[rows_h, :] += dot_nn(key_t, score_grad)
            value_sums[pl.ds(at, block), :] += dot_nn(
                jnp.concatenate(lows, axis=1), masked_grad[...]
            )
            key_sums[pl.ds(at, block), :] += dot_nn(jnp.concatenate(grads, axis=1), masked[...])
            return carry

        lax.fori_loop(first_ref[s, i], i + 1, step, 0)
        cosine, sine = tiled(cos_ref[...], heads), tiled(sin_ref[...], heads)
        ones = group_ones(width, head_size)
        query, key, _ = split_raw(raw_ref[...], width, head_size, heads)

        def all_heads(x):
            total = x
            for h in range(1, heads):
                total = total + pltpu.roll(x, h * head_size, 1)
            return total

        def norm_rope_back(x, up, gain):
            unrot = up * cosine - swap_halves(up, head_size) * sine
            inverse = lax.rsqrt(group_sum(x * x, ones) * (1.0 / head_size) + epsilon)
            gain_part = jnp.sum(unrot * x * inverse, axis=0, keepdims=True)
            scaled_up = unrot * gain
            mean = group_sum(scaled_up * x, ones) * (1.0 / head_size)
            return scaled_up * inverse - x * (mean * inverse * inverse * inverse), gain_part

        query_up = jnp.transpose(query_sums[...]) * scale
        query_grad, query_part = norm_rope_back(query, query_up, qg_ref[...])
        here = pl.ds(pl.multiple_of(i * block, block), block)
        key_up = all_heads(key_sums[here, :])
        key_grad, key_part = norm_rope_back(key, key_up, kg_ref[...])
        value_grad = all_heads(value_sums[here, :])
        out_ref[...] = jnp.concatenate(
            [query_grad, key_grad[:, :head_size], value_grad[:, :head_size]], axis=1
        ).astype(jnp.bfloat16)
        qgg_ref[...] += query_part
        kgg_ref[...] += key_part

    cosine, sine = rope_tables(head_size)
    at_rows = lambda s, i, first: (s * blocks + blocks - 1 - i, 0)
    fixed = lambda s, i, first: (0, 0)
    at_lanes = lambda s, i, first: (0, s * blocks + blocks - 1 - i)
    at_seq = lambda s, i, first: (s, 0)
    low = jnp.bfloat16
    pairs = blocks * (blocks + 1) // 2 * seqs * heads
    grads, query_part, key_part = pl.pallas_call(
        kernel,
        grid_spec=pltpu.PrefetchScalarGridSpec(
            num_scalar_prefetch=1,
            grid=(seqs, blocks),
            in_specs=[
                pl.BlockSpec((block, raw.shape[1]), at_rows),
                pl.BlockSpec((1, width), fixed),
                pl.BlockSpec((1, width), fixed),
                pl.BlockSpec((block, head_size), lambda s, i, first: (blocks - 1 - i, 0)),
                pl.BlockSpec((block, head_size), lambda s, i, first: (blocks - 1 - i, 0)),
                pl.BlockSpec((1, 1, block), lambda s, i, first: (s, 0, blocks - 1 - i)),
                pl.BlockSpec((SEQ, 1), at_seq),
                pl.BlockSpec((block, width), at_rows),
                pl.BlockSpec((8, block), at_lanes),
                pl.BlockSpec((block, width), at_rows),
                pl.BlockSpec((block, width), at_rows),
                pl.BlockSpec((SEQ, width), at_seq),
                pl.BlockSpec((SEQ, width), at_seq),
                pl.BlockSpec((blocks, head_size, block), lambda s, i, first: (s, 0, 0)),
            ],
            out_specs=[
                pl.BlockSpec((block, raw.shape[1]), at_rows),
                pl.BlockSpec((1, width), fixed),
                pl.BlockSpec((1, width), fixed),
            ],
            scratch_shapes=[
                pltpu.VMEM((heads * block, width), low),
                pltpu.VMEM((heads * block, width), low),
                pltpu.VMEM((SEQ, width), jnp.float32),
                pltpu.VMEM((SEQ, width), jnp.float32),
                pltpu.VMEM((width, block), jnp.float32),
                pltpu.VMEM((8, block), jnp.float32),
            ],
        ),
        out_shape=[
            jax.ShapeDtypeStruct(raw.shape, low),
            jax.ShapeDtypeStruct((1, width), jnp.float32),
            jax.ShapeDtypeStruct((1, width), jnp.float32),
        ],
        compiler_params=pltpu.CompilerParams(vmem_limit_bytes=48 << 20),
        cost_estimate=pl.CostEstimate(flops=0, bytes_accessed=0, transcendentals=0),
        name="attention_backward",
    )(
        first_block, raw,
        tiled(query_gain.astype(jnp.float32)[None], heads),
        tiled(key_gain.astype(jnp.float32)[None], heads),
        cosine, sine, segments[:, None, :], segments.reshape(rows, 1),
        mixed, lse, query_low, mixed_grad, key_low, value_low, key_t,
    )
    return (
        grads,
        jnp.sum(query_part.reshape(heads, head_size), axis=0),
        key_part[0, :head_size],
    )


def first_blocks(segments):
    starts = segments[:, :: BLOCK]
    below = jnp.sum(segments[:, None, :] < starts[:, :, None], axis=-1, dtype=jnp.int32)
    return below // BLOCK

MESH = pl.DeviceIdType.MESH


class Lattice:
    def __init__(self, count):
        self.depth = count // 2
        me = lax.axis_index("wide")
        self.z, self.x = me // 2, me % 2
        self.below = jnp.minimum(self.z, self.depth - 1 - self.z)
        self.low_side = self.z > self.depth - 1 - self.z

    def at(self, z, x):
        return z * 2 + x

    def order(self, m):
        near = m <= 2 * self.below
        r = jnp.where(near, (m + 1) // 2, m - self.below)
        minus = jnp.where(near, m % 2 == 1, self.low_side)
        return jnp.where(minus, self.z - r, self.z + r), r


def greet(lat, partners=()):
    barrier = pltpu.get_barrier_semaphore()
    last = lat.depth - 1
    for partner in partners:
        pl.semaphore_signal(
            barrier, inc=1, device_id={"narrow": partner}, device_id_type=MESH
        )

    def each(act):
        act(lat.at(lat.z, 1 - lat.x))

        @pl.when(lat.z > 0)
        def _():
            act(lat.at(lat.z - 1, lat.x))

        @pl.when(lat.z < last)
        def _():
            act(lat.at(lat.z + 1, lat.x))

    each(lambda who: pl.semaphore_signal(barrier, inc=1, device_id={"wide": who}, device_id_type=MESH))
    own = 1 + len(partners)
    pl.semaphore_wait(barrier, own + jnp.minimum(lat.z, 1) + jnp.minimum(last - lat.z, 1))


def gather_chunks(lat, buffers, send_sems, recv_sems, compute, meanwhile=None, landed=None):
    z, x, depth = lat.z, lat.x, lat.depth
    last = depth - 1
    every = range(len(buffers))

    def copy(k, chunk, way, slot, target):
        return pltpu.make_async_remote_copy(
            src_ref=buffers[k].at[chunk], dst_ref=buffers[k].at[chunk],
            send_sem=send_sems.at[k, way, slot], recv_sem=recv_sems.at[k, chunk],
            device_id={"wide": target}, device_id_type=MESH,
        )

    def up(k, zz):
        return copy(k, lat.at(zz, x), 0, zz, lat.at(z + 1, x))

    def down(k, zz):
        return copy(k, lat.at(zz, x), 1, zz, lat.at(z - 1, x))

    def across(k, zz):
        return copy(k, lat.at(zz, x), 2, zz, lat.at(z, 1 - x))

    def arrived(k, chunk):
        copy(k, chunk, 2, 0, lat.at(z, 1 - x)).wait_recv()
        if landed is not None:
            landed(k, chunk)

    for k in every:
        @pl.when(z < last)
        def _():
            up(k, z).start()

        @pl.when(z > 0)
        def _():
            down(k, z).start()

        across(k, z).start()
    if meanwhile is not None:
        meanwhile()

    def step(m, carry):
        zz, r = lat.order(m)
        _, before = lat.order(m - 1)

        @pl.when((m >= 1) & (m < depth) & (r != before))
        def _():
            for k in every:
                @pl.when(z - r >= 0)
                def _():
                    arrived(k, lat.at(z - r, x))

                    @pl.when(z < last)
                    def _():
                        up(k, z - r).start()

                    across(k, z - r).start()

                @pl.when(z + r <= last)
                def _():
                    arrived(k, lat.at(z + r, x))

                    @pl.when(z > 0)
                    def _():
                        down(k, z + r).start()

                    across(k, z + r).start()

        mirror = lat.order(jnp.maximum(m - 1, 0))[0]

        def part(p, carry):
            @pl.when((p == 1) & (m >= 1))
            def _():
                for k in every:
                    arrived(k, lat.at(mirror, 1 - x))

            @pl.when(((p == 0) & (m < depth)) | ((p == 1) & (m >= 1)))
            def _():
                compute(jnp.where(p == 0, lat.at(zz, x), lat.at(mirror, 1 - x)))

            return carry

        return lax.fori_loop(0, 2, part, carry)

    lax.fori_loop(0, depth + 1, step, 0)

    def settle(zz, carry):
        for k in every:
            @pl.when((z < last) & (zz <= z))
            def _():
                up(k, zz).wait_send()

            @pl.when((z > 0) & (zz >= z))
            def _():
                down(k, zz).wait_send()

            across(k, zz).wait_send()
        return carry

    lax.fori_loop(0, depth, settle, 0)


def project_gathered(local, weights, values, strips, counts, collective_id):
    rows, model = local.shape
    columns = weights.shape[1]
    narrow_count, wide_count = counts
    depth = wide_count // 2
    strip = strips[0].shape[0]
    tall = strip * len(strips)

    def kernel(
        local_ref, weights_ref, values_ref, *refs
    ):
        strip_refs, refs = refs[: len(strips)], refs[len(strips) :]
        full_ref, out_ref, sum_ref, refs = refs[0], refs[1], refs[2], refs[3:]
        spread_refs, refs = refs[: len(strips)], refs[len(strips) :]
        (full, spread, send_sems, recv_sems, own_sems, store_sems, spread_sems, y_send, core_send, spread_recv,
         mine, held, total, load_sem, *sems) = refs
        lat = Lattice(wide_count)
        me = lat.at(lat.z, lat.x)
        narrow_me = lax.axis_index("narrow")
        core_side, y_side = narrow_me + 1 - 2 * (narrow_me % 2), (narrow_me + 2) % 4
        corner = y_side + 1 - 2 * (y_side % 2)
        loads = [
            pltpu.make_async_copy(local_ref, full.at[me], own_sems.at[0]),
            pltpu.make_async_copy(values_ref, mine, load_sem),
        ] + [
            pltpu.make_async_copy(
                ref, spread.at[narrow_me, me, pl.ds(k * strip, strip)], own_sems.at[1 + k]
            )
            for k, ref in enumerate(strip_refs)
        ]
        for load in loads:
            load.start()
        arrive = greet_all(counts)
        for load in loads:
            load.wait()
        arrive()
        narrow, wide = exchange_pair(counts, mine, held, total, *sems)

        def to_side(n, chunk, target, send_sem):
            return pltpu.make_async_remote_copy(
                src_ref=spread.at[n, chunk], dst_ref=spread.at[n, chunk],
                send_sem=send_sem, recv_sem=spread_recv.at[n, chunk],
                device_id={"narrow": target}, device_id_type=MESH,
            )

        def to_y(chunk):
            return to_side(narrow_me, chunk, y_side, y_send.at[chunk])

        def to_core(n, chunk):
            return to_side(n, chunk, core_side, core_send.at[n // 2, chunk])

        def spread_out(chunk):
            to_y(chunk).start()
            to_core(narrow_me, chunk).start()

        def landed(k, chunk):
            if k == 0:
                spread_out(chunk)

        def meanwhile():
            spread_out(me)
            narrow.start()
            total[...] = narrow.total()
            wide.start()

        def keep(chunk):
            return pltpu.make_async_copy(full.at[chunk], full_ref.at[chunk], store_sems.at[chunk])

        def keep_strip(n, chunk, k):
            return pltpu.make_async_copy(
                spread.at[n, chunk, pl.ds(k * strip, strip)], spread_refs[k].at[chunk, n],
                spread_sems.at[k, n, chunk],
            )

        def keep_strips(n, chunk):
            for k in range(len(strips)):
                keep_strip(n, chunk, k).start()

        def compute(chunk):
            keep(chunk).start()
            keep_strips(narrow_me, chunk)
            at = pl.multiple_of(chunk * rows, rows)
            out_ref[pl.ds(at, rows), :] = jnp.dot(
                full[chunk], weights_ref[...], preferred_element_type=jnp.float32
            )

        gather_chunks(
            lat, [spread.at[narrow_me], full], send_sems, recv_sems, compute, meanwhile, landed
        )

        def event(e):
            zz = lat.order(e // 2)[0]
            return lat.at(zz, jnp.where(e % 2 == 0, lat.x, 1 - lat.x))

        def pass_on(e, carry):
            chunk = event(e)
            to_side(y_side, chunk, y_side, y_send.at[chunk]).wait_recv()
            to_core(y_side, chunk).start()
            keep_strips(y_side, chunk)
            return carry

        def take(e, carry):
            chunk = event(e)
            for n in (core_side, corner):
                to_side(n, chunk, core_side, core_send.at[0, chunk]).wait_recv()
                keep_strips(n, chunk)
            return carry

        lax.fori_loop(0, wide_count, pass_on, 0)
        lax.fori_loop(0, wide_count, take, 0)
        sum_ref[...] = wide.total()
        narrow.settle()
        wide.settle()

        def settle(c, carry):
            keep(c).wait()
            to_y(c).wait_send()
            to_core(narrow_me, c).wait_send()
            to_core(y_side, c).wait_send()
            for k in range(len(strips)):
                for n in range(narrow_count):
                    keep_strip(n, c, k).wait()
            return carry

        lax.fori_loop(0, wide_count, settle, 0)

    vmem = pl.BlockSpec(memory_space=pltpu.VMEM)
    hbm = pl.BlockSpec(memory_space=pl.ANY)
    low = local.dtype
    full, out, sums, *gathered = pl.pallas_call(
        kernel,
        in_specs=[hbm, vmem, hbm] + [hbm] * len(strips),
        out_specs=[hbm, vmem, vmem] + [hbm] * len(strips),
        out_shape=[
            jax.ShapeDtypeStruct((wide_count, rows, model), low),
            jax.ShapeDtypeStruct((wide_count * rows, columns), jnp.float32),
            jax.ShapeDtypeStruct(values.shape, jnp.float32),
        ]
        + [jax.ShapeDtypeStruct((wide_count, narrow_count, strip, model), low)] * len(strips),
        scratch_shapes=[
            pltpu.VMEM((wide_count, rows, model), low),
            pltpu.VMEM((narrow_count, wide_count, tall, model), low),
            pltpu.SemaphoreType.DMA((2, 3, depth)),
            pltpu.SemaphoreType.DMA((2, wide_count)),
            pltpu.SemaphoreType.DMA((1 + len(strips),)),
            pltpu.SemaphoreType.DMA((wide_count,)),
            pltpu.SemaphoreType.DMA((len(strips), narrow_count, wide_count)),
            pltpu.SemaphoreType.DMA((wide_count,)),
            pltpu.SemaphoreType.DMA((2, wide_count)),
            pltpu.SemaphoreType.DMA((narrow_count, wide_count)),
        ]
        + exchange_scratch(values.shape, counts),
        compiler_params=pltpu.CompilerParams(
            collective_id=collective_id, has_side_effects=True, vmem_limit_bytes=48 << 20
        ),
        name="project_gathered",
    )(local, weights, values, *strips)
    flat = narrow_count * wide_count * strip
    return full.reshape(wide_count * rows, model), out, sums, [g.reshape(flat, model) for g in gathered]


def nt(left, right):
    return lax.dot_general(
        left, right, (((1,), (1,)), ((), ())), preferred_element_type=jnp.float32
    )


def forward_gathered(local, gate_weight, up_weight, down_weight, wide_count, collective_id):
    rows, model = local.shape
    hidden = gate_weight.shape[1]
    depth = wide_count // 2
    tile = min(256, hidden)
    wide_tile = min(512, model)

    def kernel(
        local_ref, gate_ref, up_ref, down_ref, full_ref, gates_ref, ups_ref, acts_ref, downs_ref,
        full, gates, ups, acts, downs, send_sems, recv_sems, load_sem, store_sems,
    ):
        lat = Lattice(wide_count)
        me = lat.at(lat.z, lat.x)
        load = pltpu.make_async_copy(local_ref, full.at[me], load_sem)
        load.start()
        greet(lat)
        load.wait()
        kept = ((full, full_ref), (gates, gates_ref), (ups, ups_ref), (acts, acts_ref), (downs, downs_ref))

        def keep(which, chunk):
            source, target = kept[which]
            return pltpu.make_async_copy(source.at[chunk], target.at[chunk], store_sems.at[which, chunk])

        def compute(chunk):
            keep(0, chunk).start()
            rows_in = full[chunk]

            def inner(t, carry):
                at = pl.ds(pl.multiple_of(t * tile, tile), tile)
                gate = jnp.dot(rows_in, gate_ref[:, at], preferred_element_type=jnp.float32)
                up = jnp.dot(rows_in, up_ref[:, at], preferred_element_type=jnp.float32)
                gates[chunk, :, at] = gate
                ups[chunk, :, at] = up
                acts[chunk, :, at] = (gate * lax.logistic(gate) * up).astype(jnp.bfloat16)
                return carry

            lax.fori_loop(0, hidden // tile, inner, 0)
            for which in (1, 2, 3):
                keep(which, chunk).start()
            act = acts[chunk]

            def outer(t, carry):
                at = pl.ds(pl.multiple_of(t * wide_tile, wide_tile), wide_tile)
                downs[chunk, :, at] = jnp.dot(
                    act, down_ref[:, at], preferred_element_type=jnp.float32
                ).astype(jnp.bfloat16)
                return carry

            lax.fori_loop(0, model // wide_tile, outer, 0)
            keep(4, chunk).start()

        gather_chunks(lat, [full], send_sems, recv_sems, compute)
        for which in range(5):
            lax.fori_loop(0, wide_count, lambda c, carry: (keep(which, c).wait(), carry)[1], 0)

    low = jnp.bfloat16
    outs = [
        ((wide_count, rows, model), low),
        ((wide_count, rows, hidden), jnp.float32),
        ((wide_count, rows, hidden), jnp.float32),
        ((wide_count, rows, hidden), low),
        ((wide_count, rows, model), low),
    ]
    vmem = pl.BlockSpec(memory_space=pltpu.VMEM)
    hbm = pl.BlockSpec(memory_space=pl.ANY)
    results = pl.pallas_call(
        kernel,
        in_specs=[hbm, vmem, vmem, vmem],
        out_specs=[hbm] * 5,
        out_shape=[jax.ShapeDtypeStruct(*o) for o in outs],
        scratch_shapes=[pltpu.VMEM(*o) for o in outs]
        + [
            pltpu.SemaphoreType.DMA((1, 3, depth)),
            pltpu.SemaphoreType.DMA((1, wide_count)),
            pltpu.SemaphoreType.DMA,
            pltpu.SemaphoreType.DMA((5, wide_count)),
        ],
        compiler_params=pltpu.CompilerParams(
            collective_id=collective_id, has_side_effects=True, vmem_limit_bytes=60 << 20
        ),
        name="forward_gathered",
    )(local, gate_weight, up_weight, down_weight)
    return [r.reshape(wide_count * rows, r.shape[2]) for r in results]


def tn(left, right):
    return lax.dot_general(
        left, right, (((0,), (0,)), ((), ())), preferred_element_type=jnp.float32
    )


def backward_scattered(
    cot, gates, ups, hidden_rows, gate_weight, up_weight, down_weight, wide_count, collective_id
):
    model = cot.shape[1]
    rows = cot.shape[0] // wide_count
    hidden = gate_weight.shape[1]
    depth = wide_count // 2
    tile = min(256, hidden)
    wide_tile = min(512, model)
    low = jnp.bfloat16

    half = model // 2
    slab = min(256, half)
    per = half // slab

    def kernel(
        cot_ref, gates_ref, ups_ref, hidden_ref, gate_ref, up_ref, down_ref,
        sum_ref, gate_half_ref, up_half_ref,
        cots, gate_in, up_in, gate_low, up_low, foreign, own, crossed, from_low, from_high,
        columns, given, taken, kept,
        in_sems, cross_send, cross_recv, chain_send, low_recv, high_recv,
        column_sems, give_send, give_recv, kept_sems,
    ):
        lat = Lattice(wide_count)
        z, x, last = lat.z, lat.x, depth - 1
        narrow = lax.axis_index("narrow")
        core = narrow % 2
        partner = narrow + 1 - 2 * core

        def place(e):
            zz = lat.order(depth - 1 - e % depth)[0]
            return zz, lat.at(zz, jnp.where(e < depth, 1 - x, x))

        def loads(e):
            slot = e % 2
            chunk = place(e)[1]
            return [
                pltpu.make_async_copy(source.at[chunk], target.at[slot], in_sems.at[k, slot])
                for k, (source, target) in enumerate(
                    ((cot_ref, cots), (gates_ref, gate_in), (ups_ref, up_in))
                )
            ]

        def cross(zz):
            return pltpu.make_async_remote_copy(
                src_ref=foreign.at[zz], dst_ref=crossed.at[zz],
                send_sem=cross_send.at[zz], recv_sem=cross_recv.at[zz],
                device_id={"wide": lat.at(z, 1 - x)}, device_id_type=MESH,
            )

        def rise(zz):
            return pltpu.make_async_remote_copy(
                src_ref=own.at[zz], dst_ref=from_low.at[zz],
                send_sem=chain_send.at[zz], recv_sem=low_recv.at[zz],
                device_id={"wide": lat.at(z + 1, x)}, device_id_type=MESH,
            )

        def sink(zz):
            return pltpu.make_async_remote_copy(
                src_ref=own.at[zz], dst_ref=from_high.at[zz],
                send_sem=chain_send.at[zz], recv_sem=high_recv.at[zz],
                device_id={"wide": lat.at(z - 1, x)}, device_id_type=MESH,
            )

        def slab_of(e):
            side = jnp.where(e < 2 * per, 1 - core, core)
            return e // per % 2, e % per, side * per + e % per

        def column_load(e):
            at = pl.ds(pl.multiple_of(slab_of(e)[2] * slab, slab), slab)
            return pltpu.make_async_copy(
                hidden_ref.at[:, :, at], columns.at[e % 2], column_sems.at[e % 2]
            )

        def give(e):
            which, n, _ = slab_of(e)
            return pltpu.make_async_remote_copy(
                src_ref=given.at[e % 2], dst_ref=taken.at[which, n],
                send_sem=give_send.at[e % 2], recv_sem=give_recv.at[which, n],
                device_id={"narrow": partner}, device_id_type=MESH,
            )

        def keep(e, k):
            target = (gate_half_ref, up_half_ref)[k]
            return pltpu.make_async_copy(kept.at[e % 2], target.at[slab_of(e)[1]], kept_sems.at[e % 2])

        def weight_slab(e):
            which, n, _ = slab_of(e)
            column_load(e).wait()

            @pl.when(e + 1 < 4 * per)
            def _():
                column_load(e + 1).start()

            tokens = columns[e % 2].reshape(wide_count * rows, slab)

            @pl.when((e >= 2) & (e < 2 * per + 2))
            def _():
                give(e - 2).wait_send()

            @pl.when(e >= 2 * per + 2)
            def _():
                keep(e - 2, 0).wait()

            def product(k):
                source = (gate_low, up_low)[k]
                value = tn(tokens, source[...].reshape(wide_count * rows, hidden))

                @pl.when(e < 2 * per)
                def _():
                    given[e % 2] = value.astype(low)
                    give(e).start()

                @pl.when(e >= 2 * per)
                def _():
                    give(e).wait_recv()
                    kept[e % 2] = (value + taken[k, n].astype(jnp.float32)).astype(low)
                    keep(e, k).start()

            @pl.when(which == 0)
            def _():
                product(0)

            @pl.when(which == 1)
            def _():
                product(1)

        for copy in loads(0):
            copy.start()
        column_load(0).start()
        greet(lat, (partner,))

        def partial(e, target, zz):
            slot = e % 2
            for copy in loads(e):
                copy.wait()

            @pl.when(e + 1 < 2 * depth)
            def _():
                for copy in loads(e + 1):
                    copy.start()

            cot_rows = cots[slot]
            chunk = place(e)[1]

            def inner(t, carry):
                at = pl.ds(pl.multiple_of(t * tile, tile), tile)
                act_grad = nt(cot_rows, down_ref[at, :])
                gate, up = gate_in[slot, :, at], up_in[slot, :, at]
                sigmoid = lax.logistic(gate)
                gate_low[chunk, :, at] = (
                    act_grad * up * sigmoid * (1.0 + gate * (1.0 - sigmoid))
                ).astype(low)
                up_low[chunk, :, at] = (act_grad * gate * sigmoid).astype(low)
                return carry

            lax.fori_loop(0, hidden // tile, inner, 0)
            gate_rows, up_rows = gate_low[chunk], up_low[chunk]

            def outer(t, carry):
                at = pl.ds(pl.multiple_of(t * wide_tile, wide_tile), wide_tile)
                target[zz, :, at] = (
                    nt(gate_rows, gate_ref[at, :]) + nt(up_rows, up_ref[at, :])
                ).astype(low)
                return carry

            lax.fori_loop(0, model // wide_tile, outer, 0)

        def send_step(e, carry):
            zz, _ = place(e)
            partial(e, foreign, zz)
            cross(zz).start()
            return carry

        lax.fori_loop(0, depth, send_step, 0)

        def own_step(e, carry):
            zz, _ = place(e)
            partial(e, own, zz)

            @pl.when(e == depth)
            def _():
                chain(zz)

            return carry

        def chain(zz):
            cross(zz).wait_recv()
            wide = jnp.float32

            @pl.when((zz > z) & (z > 0))
            def _():
                rise(zz).wait_recv()
                own[zz] = (own[zz].astype(wide) + crossed[zz].astype(wide) + from_low[zz].astype(wide)).astype(low)

            @pl.when((zz < z) & (z < last))
            def _():
                sink(zz).wait_recv()
                own[zz] = (own[zz].astype(wide) + crossed[zz].astype(wide) + from_high[zz].astype(wide)).astype(low)

            @pl.when(((zz > z) & (z == 0)) | ((zz < z) & (z == last)))
            def _():
                own[zz] = (own[zz].astype(wide) + crossed[zz].astype(wide)).astype(low)

            @pl.when(zz > z)
            def _():
                rise(zz).start()

            @pl.when(zz < z)
            def _():
                sink(zz).start()

            @pl.when(zz == z)
            def _():
                sum_ref[...] = own[zz].astype(wide) + crossed[zz].astype(wide)

                @pl.when(z > 0)
                def _():
                    rise(zz).wait_recv()
                    sum_ref[...] += from_low[zz].astype(wide)

                @pl.when(z < last)
                def _():
                    sink(zz).wait_recv()
                    sum_ref[...] += from_high[zz].astype(wide)

        lax.fori_loop(depth, 2 * depth, own_step, 0)

        def slab_step(e, carry):
            for k in range(1, depth):
                @pl.when(e == 4 * per * (k - 1) // (depth - 2))
                def _():
                    chain(place(depth + k)[0])

            @pl.when(e < 4 * per)
            def _():
                weight_slab(e)

            return carry

        lax.fori_loop(0, 4 * per + 1, slab_step, 0)
        for e in (4 * per - 2, 4 * per - 1):
            keep(e, 1).wait()

        def settle(zz, carry):
            cross(zz).wait_send()

            @pl.when(zz > z)
            def _():
                rise(zz).wait_send()

            @pl.when(zz < z)
            def _():
                sink(zz).wait_send()

            return carry

        lax.fori_loop(0, depth, settle, 0)

    vmem = pl.BlockSpec(memory_space=pltpu.VMEM)
    hbm = pl.BlockSpec(memory_space=pl.ANY)
    total, gate_half, up_half = pl.pallas_call(
        kernel,
        in_specs=[hbm, hbm, hbm, hbm, vmem, vmem, vmem],
        out_specs=[vmem] + [hbm] * 2,
        out_shape=[
            jax.ShapeDtypeStruct((rows, model), jnp.float32),
            jax.ShapeDtypeStruct((per, slab, hidden), low),
            jax.ShapeDtypeStruct((per, slab, hidden), low),
        ],
        scratch_shapes=[
            pltpu.VMEM((2, rows, model), low),
            pltpu.VMEM((2, rows, hidden), jnp.float32),
            pltpu.VMEM((2, rows, hidden), jnp.float32),
            pltpu.VMEM((wide_count, rows, hidden), low),
            pltpu.VMEM((wide_count, rows, hidden), low),
        ]
        + [pltpu.VMEM((depth, rows, model), low)] * 5
        + [
            pltpu.VMEM((2, wide_count, rows, slab), low),
            pltpu.VMEM((2, slab, hidden), low),
            pltpu.VMEM((2, per, slab, hidden), low),
            pltpu.VMEM((2, slab, hidden), low),
            pltpu.SemaphoreType.DMA((3, 2)),
        ]
        + [pltpu.SemaphoreType.DMA((depth,))] * 5
        + [
            pltpu.SemaphoreType.DMA((2,)),
            pltpu.SemaphoreType.DMA((2,)),
            pltpu.SemaphoreType.DMA((2, per)),
            pltpu.SemaphoreType.DMA((2,)),
        ],
        compiler_params=pltpu.CompilerParams(
            collective_id=collective_id, has_side_effects=True, vmem_limit_bytes=67043328
        ),
        name="backward_scattered",
    )(
        cot.reshape(wide_count, rows, model),
        gates.reshape(wide_count, rows, hidden),
        ups.reshape(wide_count, rows, hidden),
        hidden_rows.reshape(wide_count, rows, model),
        gate_weight, up_weight, down_weight,
    )
    return total, gate_half.reshape(half, hidden), up_half.reshape(half, hidden)


AXES = ("narrow", "wide")


def peers(k, counts, act):
    here = lax.axis_index(AXES[k])

    def one(step, carry):
        act((here + step) % counts[k])
        return carry

    lax.fori_loop(1, counts[k], one, 0)


def greet_all(counts):
    barrier = pltpu.get_barrier_semaphore()
    for k, axis in enumerate(AXES):
        peers(k, counts, lambda who: pl.semaphore_signal(
            barrier, inc=1, device_id={axis: who}, device_id_type=MESH))
    return lambda: pl.semaphore_wait(barrier, counts[0] + counts[1] - 2)


class Exchange:
    def __init__(self, k, counts, source, slots, sends, recvs):
        self.k, self.counts, self.source = k, counts, source
        self.slots, self.sends, self.recvs = slots, sends, recvs
        self.here = lax.axis_index(AXES[k])

    def copy(self, who, slot):
        return pltpu.make_async_remote_copy(
            src_ref=self.source, dst_ref=self.slots.at[slot],
            send_sem=self.sends.at[who], recv_sem=self.recvs.at[slot],
            device_id={AXES[self.k]: who}, device_id_type=MESH,
        )

    def start(self):
        peers(self.k, self.counts, lambda who: self.copy(who, self.here).start())
        self.slots[self.here] = self.source[...]

    def total(self):
        peers(self.k, self.counts, lambda who: self.copy(who, who).wait_recv())
        sums = self.slots[0]
        for n in range(1, self.counts[self.k]):
            sums = sums + self.slots[n]
        return sums

    def settle(self):
        peers(self.k, self.counts, lambda who: self.copy(who, self.here).wait_send())


def exchange_scratch(shape, counts):
    return [
        pltpu.VMEM(shape, jnp.float32),
        pltpu.VMEM((2, max(counts)) + shape, jnp.float32),
        pltpu.VMEM(shape, jnp.float32),
        pltpu.SemaphoreType.DMA,
        pltpu.SemaphoreType.DMA((counts[0],)),
        pltpu.SemaphoreType.DMA((counts[0],)),
        pltpu.SemaphoreType.DMA((counts[1],)),
        pltpu.SemaphoreType.DMA((counts[1],)),
    ]


def exchange_pair(counts, mine, held, total, narrow_send, narrow_recv, wide_send, wide_recv):
    return (
        Exchange(0, counts, mine, held.at[0], narrow_send, narrow_recv),
        Exchange(1, counts, total, held.at[1], wide_send, wide_recv),
    )


def sum_everywhere(values, counts, collective_id):
    def kernel(in_ref, out_ref, mine, held, total, load_sem, *sems):
        load = pltpu.make_async_copy(in_ref, mine, load_sem)
        load.start()
        arrive = greet_all(counts)
        load.wait()
        arrive()
        narrow, wide = exchange_pair(counts, mine, held, total, *sems)
        narrow.start()
        total[...] = narrow.total()
        wide.start()
        out_ref[...] = wide.total()
        narrow.settle()
        wide.settle()

    return pl.pallas_call(
        kernel,
        in_specs=[pl.BlockSpec(memory_space=pl.ANY)],
        out_specs=pl.BlockSpec(memory_space=pltpu.VMEM),
        out_shape=jax.ShapeDtypeStruct(values.shape, jnp.float32),
        scratch_shapes=exchange_scratch(values.shape, counts),
        compiler_params=pltpu.CompilerParams(collective_id=collective_id, has_side_effects=True),
        name="sum_everywhere",
    )(values)


def greet_wide(counts, partners=()):
    barrier = pltpu.get_barrier_semaphore()
    peers(1, counts, lambda who: pl.semaphore_signal(
        barrier, inc=1, device_id={"wide": who}, device_id_type=MESH))
    for partner in partners:
        pl.semaphore_signal(
            barrier, inc=1, device_id={"narrow": partner}, device_id_type=MESH
        )
    pl.semaphore_wait(barrier, counts[1] - 1 + len(partners))


class Blocks:
    def __init__(self, counts, blocks, held, sends, recvs):
        self.counts, self.blocks, self.held = counts, blocks, held
        self.sends, self.recvs = sends, recvs
        self.me = lax.axis_index("wide")

    def copy(self, who, slot):
        return pltpu.make_async_remote_copy(
            src_ref=self.blocks.at[who], dst_ref=self.held.at[slot],
            send_sem=self.sends.at[who], recv_sem=self.recvs.at[slot],
            device_id={"wide": who}, device_id_type=MESH,
        )

    def start(self, who):
        self.copy(who, self.me).start()

    def each(self, act):
        peers(1, self.counts, act)

    def arrived(self, who):
        self.copy(who, who).wait_recv()

    def settle(self):
        self.each(lambda who: self.copy(who, self.me).wait_send())


def carry_over(source, target, sems):
    across = (lax.axis_index("narrow") + 2) % 4
    return pltpu.make_async_remote_copy(
        src_ref=source, dst_ref=target, send_sem=sems.at[0], recv_sem=sems.at[1],
        device_id={"narrow": across}, device_id_type=MESH,
    )


VMEM_SPEC = pl.BlockSpec(memory_space=pltpu.VMEM)
HBM_SPEC = pl.BlockSpec(memory_space=pl.ANY)


def mix_and_project(mixed, output_full, counts, collective_id):
    wide_count = counts[1]
    rows, width = mixed.shape[0] // wide_count, mixed.shape[1]
    model = output_full.shape[1]
    tile = min(512, model)

    def kernel(mixed_ref, weight_ref, out_ref, held_ref, sends, recvs):
        blocks = Blocks(counts, mixed_ref, held_ref, sends, recvs)
        greet_wide(counts)
        blocks.each(blocks.start)
        held_ref[blocks.me] = mixed_ref[blocks.me]

        def add(who, first):
            rows_in = held_ref[who]

            def one(t, carry):
                at = pl.ds(pl.multiple_of(t * tile, tile), tile)
                part = jnp.dot(
                    rows_in, weight_ref[pl.ds(pl.multiple_of(who * width, width), width), at],
                    preferred_element_type=jnp.float32,
                )
                out_ref[:, at] = part if first else out_ref[:, at] + part
                return carry

            lax.fori_loop(0, model // tile, one, 0)

        add(blocks.me, True)

        def later(who):
            blocks.arrived(who)
            add(who, False)

        blocks.each(later)
        blocks.settle()

    return pl.pallas_call(
        kernel,
        in_specs=[VMEM_SPEC, VMEM_SPEC],
        out_specs=[VMEM_SPEC, VMEM_SPEC],
        out_shape=[
            jax.ShapeDtypeStruct((rows, model), jnp.float32),
            jax.ShapeDtypeStruct((wide_count, rows, width), mixed.dtype),
        ],
        scratch_shapes=[pltpu.SemaphoreType.DMA((wide_count,))] * 2,
        compiler_params=pltpu.CompilerParams(
            collective_id=collective_id, has_side_effects=True, vmem_limit_bytes=32 << 20
        ),
        name="mix_and_project",
    )(mixed.reshape(wide_count, rows, width), output_full)


def unmix(middle_low, output_full, mixed_blocks, carried, counts, collective_id):
    wide_count = counts[1]
    rows, model = middle_low.shape
    width = mixed_blocks.shape[2]
    strip = width // 4
    low = jnp.bfloat16

    def kernel(
        middle_ref, weight_ref, mixed_ref, carried_ref, held_ref, half_ref, swapped_ref,
        made, product, own, given, taken, sends, recvs, give_send, give_recv, carry_sems,
    ):
        blocks = Blocks(counts, made, held_ref, sends, recvs)
        narrow = lax.axis_index("narrow")
        core = narrow % 2
        partner = narrow + 1 - 2 * core
        greet_wide(counts, (partner, (narrow + 2) % 4))
        carry = carry_over(carried_ref, swapped_ref, carry_sems)
        carry.start()

        def make(who):
            made[who] = nt(
                middle_ref[...], weight_ref[pl.ds(pl.multiple_of(who * width, width), width), :]
            ).astype(low)

        def make_and_start(who):
            make(who)
            blocks.start(who)

        blocks.each(make_and_start)
        make(blocks.me)
        held_ref[blocks.me] = made[blocks.me]

        def give(w):
            return pltpu.make_async_remote_copy(
                src_ref=given.at[w], dst_ref=taken.at[w],
                send_sem=give_send.at[w], recv_sem=give_recv.at[w],
                device_id={"narrow": partner}, device_id_type=MESH,
            )

        def multiply(w, state):
            product[...] = tn(mixed_ref[w], middle_ref[...])
            for y in range(2):
                at = pl.multiple_of((2 * y + 1 - core) * strip, strip)
                given[w, y] = product[pl.ds(at, strip), :].astype(low)
                at = pl.multiple_of((2 * y + core) * strip, strip)
                own[w, y] = product[pl.ds(at, strip), :]
            give(w).start()
            return state

        def collect(w, state):
            give(w).wait_recv()
            for y in range(2):
                half_ref[y, w] = (own[w, y] + taken[w, y].astype(jnp.float32)).astype(low)
            return state

        lax.fori_loop(0, wide_count, multiply, 0)
        lax.fori_loop(0, wide_count, collect, 0)
        blocks.each(blocks.arrived)
        blocks.settle()
        lax.fori_loop(0, wide_count, lambda w, state: (give(w).wait_send(), state)[1], 0)
        carry.wait()

    held, half, swapped = pl.pallas_call(
        kernel,
        in_specs=[VMEM_SPEC] * 3 + [HBM_SPEC],
        out_specs=[VMEM_SPEC] * 2 + [HBM_SPEC],
        out_shape=[
            jax.ShapeDtypeStruct((wide_count, rows, width), low),
            jax.ShapeDtypeStruct((2, wide_count, strip, model), low),
            jax.ShapeDtypeStruct(carried.shape, low),
        ],
        scratch_shapes=[
            pltpu.VMEM((wide_count, rows, width), low),
            pltpu.VMEM((width, model), jnp.float32),
            pltpu.VMEM((wide_count, 2, strip, model), jnp.float32),
            pltpu.VMEM((wide_count, 2, strip, model), low),
            pltpu.VMEM((wide_count, 2, strip, model), low),
        ]
        + [pltpu.SemaphoreType.DMA((wide_count,))] * 4
        + [pltpu.SemaphoreType.DMA((2,))],
        compiler_params=pltpu.CompilerParams(
            collective_id=collective_id, has_side_effects=True, vmem_limit_bytes=48 << 20
        ),
        name="unmix",
    )(middle_low, output_full, mixed_blocks, carried)
    return (
        held.reshape(wide_count * rows, width),
        half.reshape(2, wide_count * strip, model),
        swapped,
    )


def return_and_project(
    grads, hidden_rows, query_turned, key_weight, value_weight, carried, counts, collective_id
):
    wide_count = counts[1]
    rows, columns = grads.shape[0] // wide_count, grads.shape[1]
    model = query_turned.shape[1]
    width = query_turned.shape[0] // wide_count
    head = (columns - width) // 2
    tile = min(512, model)
    slab = min(256, model // 2)
    per = model // 2 // slab
    low = jnp.bfloat16

    def kernel(
        grads_ref, hidden_ref, query_ref, key_ref, value_ref, carried_ref,
        out_ref, weight_ref, swapped_ref,
        held, slabs, query_all, key_all, value_all, given, taken, halves, whole,
        sends, recvs, slab_sems, give_send, give_recv, half_sems, carry_sems,
    ):
        blocks = Blocks(counts, grads_ref, held, sends, recvs)
        narrow = lax.axis_index("narrow")
        core = narrow % 2
        partner, across = narrow + 1 - 2 * core, (narrow + 2) % 4

        def row_of(t):
            return pl.multiple_of((jnp.where(t < per, 1 - core, core) * per + t % per) * slab, slab)

        def load(t):
            at = pl.ds(row_of(t), slab)
            return pltpu.make_async_copy(hidden_ref.at[:, :, at], slabs.at[t % 2], slab_sems.at[t % 2])

        load(0).start()
        greet_wide(counts, (partner, across))
        blocks.each(blocks.start)
        carry = carry_over(carried_ref, swapped_ref, carry_sems)
        held[blocks.me] = grads_ref[blocks.me]

        def give(n):
            return pltpu.make_async_remote_copy(
                src_ref=given.at[n], dst_ref=taken.at[n],
                send_sem=give_send.at[n], recv_sem=give_recv.at[n],
                device_id={"narrow": partner}, device_id_type=MESH,
            )

        exchange = pltpu.make_async_remote_copy(
            src_ref=halves.at[0], dst_ref=halves.at[1],
            send_sem=half_sems.at[0], recv_sem=half_sems.at[1],
            device_id={"narrow": across}, device_id_type=MESH,
        )
        hand_over = pltpu.make_async_remote_copy(
            src_ref=whole.at[core], dst_ref=whole.at[core],
            send_sem=half_sems.at[2], recv_sem=half_sems.at[3],
            device_id={"narrow": partner}, device_id_type=MESH,
        )

        def weigh(t, state):
            load(t).wait()

            @pl.when(t + 1 < 2 * per)
            def _():
                load(t + 1).start()

            value = tn(
                slabs[t % 2].reshape(wide_count * rows, slab),
                grads_ref[...].reshape(wide_count * rows, columns),
            )
            n = t % per

            @pl.when(t < per)
            def _():
                given[n] = value.astype(low)
                give(n).start()

            @pl.when(t >= per)
            def _():
                give(n).wait_recv()
                halves[0, n] = (value + taken[n].astype(jnp.float32)).astype(low)

            return state

        lax.fori_loop(0, 2 * per, weigh, 0)
        exchange.start()
        carry.start()
        blocks.each(blocks.arrived)
        exchange.wait()
        whole[core] = (halves[0].astype(jnp.float32) + halves[1].astype(jnp.float32)).astype(low)
        hand_over.start()
        for w in range(wide_count):
            query_all[:, w * width : (w + 1) * width] = held[w, :, :width]
        key_all[...] = jnp.concatenate(
            [held[w, :, width : width + head] for w in range(wide_count)], axis=1
        )
        value_all[...] = jnp.concatenate(
            [held[w, :, width + head :] for w in range(wide_count)], axis=1
        )

        def one(t, state):
            at = pl.ds(pl.multiple_of(t * tile, tile), tile)
            out_ref[:, at] = (
                jnp.dot(query_all[...], query_ref[:, at], preferred_element_type=jnp.float32)
                + nt(key_all[...], key_ref[at, :])
                + nt(value_all[...], value_ref[at, :])
            )
            return state

        lax.fori_loop(0, model // tile, one, 0)
        hand_over.wait()
        weight_ref[...] = whole[...].reshape(model, columns).astype(jnp.float32)
        blocks.settle()
        lax.fori_loop(0, per, lambda n, state: (give(n).wait_send(), state)[1], 0)
        carry.wait()

    return pl.pallas_call(
        kernel,
        in_specs=[VMEM_SPEC, HBM_SPEC] + [VMEM_SPEC] * 3 + [HBM_SPEC],
        out_specs=[VMEM_SPEC] * 2 + [HBM_SPEC],
        out_shape=[
            jax.ShapeDtypeStruct((rows, model), jnp.float32),
            jax.ShapeDtypeStruct((model, columns), jnp.float32),
            jax.ShapeDtypeStruct(carried.shape, low),
        ],
        scratch_shapes=[
            pltpu.VMEM((wide_count, rows, columns), low),
            pltpu.VMEM((2, wide_count, rows, slab), low),
            pltpu.VMEM((rows, wide_count * width), low),
            pltpu.VMEM((rows, wide_count * head), low),
            pltpu.VMEM((rows, wide_count * head), low),
            pltpu.VMEM((per, slab, columns), low),
            pltpu.VMEM((per, slab, columns), low),
            pltpu.VMEM((2, per, slab, columns), low),
            pltpu.VMEM((2, per, slab, columns), low),
            pltpu.SemaphoreType.DMA((wide_count,)),
            pltpu.SemaphoreType.DMA((wide_count,)),
            pltpu.SemaphoreType.DMA((2,)),
            pltpu.SemaphoreType.DMA((per,)),
            pltpu.SemaphoreType.DMA((per,)),
            pltpu.SemaphoreType.DMA((4,)),
            pltpu.SemaphoreType.DMA((2,)),
        ],
        compiler_params=pltpu.CompilerParams(
            collective_id=collective_id, has_side_effects=True, vmem_limit_bytes=48 << 20
        ),
        name="return_and_project",
    )(
        grads.reshape(wide_count, rows, columns),
        hidden_rows.reshape(wide_count, rows, model),
        query_turned, key_weight, value_weight,
        carried,
    )

CORPORA = 8
GATHER_BYTES = 8 << 20


def norm_scale(values, scale_gain):
    return (
        values * lax.rsqrt(jnp.mean(values * values, axis=-1, keepdims=True) + epsilon) * scale_gain
    )


def contract_first(left, right):
    return lax.dot_general(
        left, right, (((0,), (0,)), ((), ())), preferred_element_type=jnp.float32
    )


def gather_wide(values):
    return lax.all_gather(values, "wide", axis=0, tiled=True)


def scatter_wide(values):
    return lax.psum_scatter(
        values.astype(jnp.bfloat16), "wide", scatter_dimension=0, tiled=True
    ).astype(jnp.float32)


def own_part(values, axis, index, count):
    size = values.shape[axis] // count
    return lax.dynamic_slice_in_dim(values, index * size, size, axis)


def swap_narrow(values, bit):
    count = lax.axis_size("narrow")
    return lax.ppermute(values, "narrow", [(i, i ^ bit) for i in range(count)])


def keep_half(values, axis, bit):
    side = lax.axis_index("narrow") // bit % 2
    mine = lax.dynamic_index_in_dim(values, side, axis, keepdims=False)
    other = lax.dynamic_index_in_dim(values, 1 - side, axis, keepdims=False)
    return add_low(mine, swap_narrow(other, bit))


def add_low(left, right):
    return (left.astype(jnp.float32) + right.astype(jnp.float32)).astype(jnp.bfloat16)


def core_half(values):
    rows, columns = values.shape
    return keep_half(values.astype(jnp.bfloat16).reshape(2, rows // 2, columns), 0, 1)


def sum_narrow(values):
    half = core_half(values)
    return hand_back(add_low(half, swap_narrow(half, 2)))


def hand_back(half):
    other = swap_narrow(half, 1)
    first = lax.axis_index("narrow") % 2 == 0
    return jnp.concatenate(
        [jnp.where(first, half, other), jnp.where(first, other, half)], axis=0
    ).astype(jnp.float32)


def swiglu_back(act_grad, gate_values, up_values):
    sigmoid_gate = lax.logistic(gate_values)
    gate_part = act_grad * up_values * sigmoid_gate * (1.0 + gate_values * (1.0 - sigmoid_gate))
    up_part = act_grad * gate_values * sigmoid_gate
    return (gate_part.astype(jnp.bfloat16), up_part.astype(jnp.bfloat16))


def shards(
    tokens,
    attention_gain,
    query_weight,
    key_weight,
    value_weight,
    query_gain,
    key_gain,
    output_weight,
    feedforward_gain,
    gate_weight,
    up_weight,
    down_weight,
    cotangent,
    corpus_tags,
    segments,
):
    low, wide_type = jnp.bfloat16, jnp.float32
    head_size = query_gain.shape[0]
    own_rows, model_width = tokens.shape
    wide_count, narrow_count = lax.axis_size("wide"), lax.axis_size("narrow")
    counts = (narrow_count, wide_count)
    wide_index, narrow_index = lax.axis_index("wide"), lax.axis_index("narrow")
    key_total = key_weight.shape[1] // head_size
    width = query_weight.shape[1]
    key_head = wide_index * key_total // wide_count
    all_rows = own_rows * wide_count
    chained = wide_count == key_total and narrow_count == 4 and all_rows * model_width * 2 <= GATHER_BYTES

    tag_hits = corpus_tags[:, None] == jnp.arange(CORPORA, dtype=jnp.int32)[None, :]
    local_counts = jnp.sum(tag_hits.astype(wide_type), axis=0)
    local_counts = jnp.pad(local_counts[None], ((0, 7), (0, 128 - CORPORA)))
    token_values = tokens.astype(wide_type)
    first_gain = attention_gain.astype(wide_type)
    second_gain = feedforward_gain.astype(wide_type)

    key_columns = lax.dynamic_slice_in_dim(key_weight, key_head * head_size, head_size, 1)
    value_columns = lax.dynamic_slice_in_dim(value_weight, key_head * head_size, head_size, 1)
    own_weights = jnp.concatenate([query_weight, key_columns, value_columns], axis=1)
    strip = width // narrow_count
    strips = [
        own_part(output_weight, 0, narrow_index, narrow_count),
        jnp.transpose(own_part(query_weight, 1, narrow_index, narrow_count)),
    ]
    hidden_local = norm_scale(token_values, first_gain).astype(low)
    if chained:
        hidden_one, raw, corpus_counts, gathered = project_gathered(
            hidden_local, own_weights, local_counts, strips, counts, 2
        )
    else:
        hidden_one = gather_wide(hidden_local)
        raw = dot_nn(hidden_one, own_weights)
        corpus_counts = sum_everywhere(local_counts, counts, 1)
        gathered = [lax.all_gather(part, ("wide", "narrow"), axis=0, tiled=True) for part in strips]
    output_full, query_turned = gathered
    corpus_counts = corpus_counts[0, :CORPORA]
    corpus_scale = jnp.sqrt(jnp.sum(corpus_counts) / (CORPORA * corpus_counts))
    row_weight = jnp.sum(jnp.where(tag_hits, corpus_scale[None, :], 0.0), axis=1)
    out_cot = cotangent.astype(wide_type) * row_weight[:, None]
    cot_low, raw = lax.optimization_barrier((out_cot.astype(low), raw))
    cot_low = gather_wide(cot_low)

    first_block = first_blocks(segments)
    saved = attention_forward(raw, query_gain, key_gain, segments, first_block)
    if chained:
        branch, mixed = mix_and_project(saved[0], output_full, counts, 6)
        middle = token_values + branch
    else:
        mixed = lax.all_to_all(saved[0], "wide", split_axis=0, concat_axis=1, tiled=True)
        middle = token_values + dot_nn(mixed, output_full)

    together = lax.optimization_barrier
    hidden_two_local = norm_scale(middle, second_gain).astype(low)
    if chained:
        hidden_two, gate_values, up_values, activated, down_part = forward_gathered(
            hidden_two_local, gate_weight, up_weight, down_weight, wide_count, 3
        )
        hidden_two_grad, gate_half, up_half = backward_scattered(
            cot_low, gate_values, up_values, hidden_two, gate_weight, up_weight, down_weight,
            wide_count, 4,
        )
        down_part, hidden_two_grad = together((down_part, hidden_two_grad))
    else:
        hidden_two = gather_wide(hidden_two_local)
        gate_values = dot_nn(hidden_two, gate_weight)
        up_values = dot_nn(hidden_two, up_weight)
        activated = (gate_values * lax.logistic(gate_values) * up_values).astype(low)
        down_part = dot_nn(activated, down_weight)
        gate_low, up_low = swiglu_back(dot_nt(cot_low, down_weight), gate_values, up_values)
        hidden_two_grad = scatter_wide(dot_nt(gate_low, gate_weight) + dot_nt(up_low, up_weight))
        gate_half = core_half(contract_first(hidden_two, gate_low))
        up_half = core_half(contract_first(hidden_two, up_low))
        gate_other = swap_narrow(gate_half, 2)
    down_sum = scatter_wide(down_part)

    _, second_pull = jax.vjp(norm_scale, middle, second_gain)
    middle_part, second_gain_grad = second_pull(hidden_two_grad)
    middle_grad = out_cot + middle_part
    middle_low = middle_grad.astype(low)
    if chained:
        mixed_grad, output_part, gate_other = unmix(
            middle_low, output_full, mixed, gate_half, counts, 7
        )
    else:
        mixed_grad = lax.all_to_all(
            dot_nt(middle_low, output_full).astype(low), "wide", split_axis=1, concat_axis=0, tiled=True
        )
        mixed = mixed.reshape(own_rows, wide_count, narrow_count, strip).transpose(0, 2, 1, 3)
        output_part = contract_first(mixed.reshape(own_rows, wide_count * width), middle_low)
        output_part = output_part.astype(low).reshape(2, 2, wide_count * strip, model_width)
        output_part = keep_half(output_part, 1, 1)
    mixed_grad, output_part, activated, up_half = together(
        (mixed_grad, output_part, activated, up_half)
    )
    output_part = keep_half(output_part, 0, 2)
    down_half = core_half(contract_first(activated, cot_low))
    mixed_grad, down_half = together((mixed_grad, down_half))
    up_half = add_low(up_half, swap_narrow(up_half, 2))
    gate_grad = hand_back(add_low(gate_half, gate_other))
    grads, query_gain_grad, key_gain_grad = attention_backward(
        raw, query_gain, key_gain, segments, first_block, saved, mixed_grad
    )
    grads, output_part, up_half, gate_grad, down_sum = together(
        (grads, output_part, up_half, gate_grad, down_sum)
    )
    output_part = lax.psum_scatter(output_part, "wide", scatter_dimension=0, tiled=True)
    shared = wide_count // key_total
    if chained:
        hidden_one_grad, weight_sums, down_other = return_and_project(
            grads, hidden_one, query_turned, key_weight, value_weight, down_half, counts, 8
        )
    else:
        down_other = swap_narrow(down_half, 2)
        weight_grads = contract_first(hidden_one, grads)
        sent = lax.all_to_all(grads, "wide", split_axis=0, concat_axis=1, tiled=True).reshape(
            own_rows, wide_count, width + 2 * head_size
        )

        def key_side(start):
            part = sent[:, :, start : start + head_size]
            if shared > 1:
                part = jnp.sum(
                    part.astype(wide_type).reshape(own_rows, key_total, shared, head_size), axis=2
                ).astype(low)
            return part.reshape(own_rows, key_total * head_size)

        hidden_one_grad = (
            dot_nn(sent[:, :, :width].reshape(own_rows, wide_count * width), query_turned)
            + dot_nt(key_side(width), key_weight)
            + dot_nt(key_side(width + head_size), value_weight)
        )
    hidden_one_grad, output_part = together((hidden_one_grad, output_part))
    output_grad = lax.all_gather(output_part, "narrow", axis=0, tiled=True).astype(wide_type)
    down_grad = hand_back(add_low(down_half, down_other))
    up_grad = hand_back(up_half)
    _, first_pull = jax.vjp(norm_scale, token_values, first_gain)
    token_part, first_gain_grad = first_pull(hidden_one_grad)
    tokens_gradient = (middle_grad + token_part).astype(low)
    tokens_gradient, down_sum = lax.optimization_barrier((tokens_gradient, down_sum))
    result = (middle + down_sum).astype(low)

    if shared == 1:
        if not chained:
            weight_sums = sum_narrow(weight_grads)
        key_weight_grad = weight_sums[:, width : width + head_size]
        value_weight_grad = weight_sums[:, width + head_size :]
    else:
        weight_sums = sum_narrow(weight_grads[:, :width])

        def spread(part):
            whole = jnp.zeros((model_width, key_total * head_size), wide_type)
            whole = lax.dynamic_update_slice_in_dim(whole, part, key_head * head_size, 1)
            share = lax.psum_scatter(whole.astype(low), "wide", scatter_dimension=1, tiled=True)
            return lax.psum(share, "narrow").astype(wide_type)

        key_weight_grad = spread(weight_grads[:, width : width + head_size])
        value_weight_grad = spread(weight_grads[:, width + head_size :])

    gain_parts = jnp.concatenate([first_gain_grad, second_gain_grad, query_gain_grad, key_gain_grad])
    lines = -(-gain_parts.shape[0] // 1024) * 8
    gain_parts = jnp.pad(gain_parts, (0, lines * 128 - gain_parts.shape[0])).reshape(lines, 128)
    gains = sum_everywhere(gain_parts, counts, 5).reshape(-1)
    starts = (0, model_width, 2 * model_width, 2 * model_width + head_size)
    sizes = (model_width, model_width, head_size, head_size)
    first_out, second_out, query_gain_out, key_gain_out = (
        own_part(gains[start : start + size], 0, wide_index, wide_count)
        for start, size in zip(starts, sizes)
    )
    return (
        result,
        tokens_gradient,
        first_out,
        weight_sums[:, :width],
        key_weight_grad,
        value_weight_grad,
        query_gain_out,
        key_gain_out,
        output_grad,
        second_out,
        gate_grad,
        up_grad,
        down_grad,
    )


def solution(mesh):
    rows = P(("narrow", "wide"), None)
    columns, first = P(None, "wide"), P("wide", None)
    return jax.shard_map(
        shards,
        mesh=mesh,
        in_specs=(
            rows, P(), columns, P(), P(), P(), P(), first, P(), columns, columns, first,
            rows, P(("narrow", "wide")), P("narrow", None),
        ),
        out_specs=(
            rows, rows, P("wide"), columns, columns, columns, P("wide"), P("wide"),
            first, P("wide"), columns, columns, first,
        ),
        check_vma=False,
    )
```

```python
import numpy as np

import jax
import jax.numpy as jnp
from jax import lax
from jax.experimental import pallas as pl
from jax.experimental.pallas import tpu as pltpu
from jax.sharding import PartitionSpec as P

SEQ = 2048
epsilon = 1e-06
rope_base = 10000.0
BLOCK = 256
NEG = -1e30


def rope_tables(head_size):
    positions = np.arange(SEQ, dtype=np.float32)
    exponents = np.arange(head_size // 2, dtype=np.float32) * np.float32(2.0 / head_size)
    frequency = np.power(np.float32(rope_base), -exponents).astype(np.float32)
    angles = (positions[:, None] * frequency[None, :]).astype(np.float32)
    cosine, sine = np.cos(angles).astype(np.float32), np.sin(angles).astype(np.float32)
    return (
        np.concatenate([cosine, cosine], axis=1),
        np.concatenate([-sine, sine], axis=1),
    )


def dot_nn(left, right):
    return jnp.dot(left, right, preferred_element_type=jnp.float32)


def dot_nt(left, right):
    return lax.dot_general(
        left, right, (((1,), (1,)), ((), ())), preferred_element_type=jnp.float32
    )


def lane_ids(shape):
    return lax.broadcasted_iota(jnp.int32, shape, 1)


def group_ones(width, head_size):
    rows = lax.broadcasted_iota(jnp.int32, (width, width), 0) // head_size
    columns = lax.broadcasted_iota(jnp.int32, (width, width), 1) // head_size
    return jnp.where(rows == columns, 1.0, 0.0).astype(jnp.bfloat16)


def group_sum(values, ones):
    top = values.astype(jnp.bfloat16)
    rest = (values - top.astype(jnp.float32)).astype(jnp.bfloat16)
    return dot_nn(top, ones) + dot_nn(rest, ones)


def swap_halves(values, head_size):
    width, half = values.shape[1], head_size // 2
    if width == head_size:
        return jnp.concatenate([values[:, half:], values[:, :half]], axis=1)
    ahead = pltpu.roll(values, width - half, 1)
    behind = pltpu.roll(values, half, 1)
    return jnp.where(lane_ids(values.shape) % head_size < half, ahead, behind)


def tiled(values, count):
    return jnp.concatenate([values] * count, axis=1) if count > 1 else values


def split_raw(raw, width, head_size, heads):
    query = raw[:, :width]
    key = tiled(raw[:, width : width + head_size], heads)
    value = tiled(raw[:, width + head_size :], heads)
    return query, key, value


def head_masks(block, width, head_size, heads):
    group = lane_ids((block, width)) // head_size
    return [group == h for h in range(heads)]


def attention_forward(raw, query_gain, key_gain, segments, first_block):
    head_size = query_gain.shape[0]
    rows = raw.shape[0]
    heads = raw.shape[1] // head_size - 2
    width = heads * head_size
    seqs, blocks, block = rows // SEQ, SEQ // BLOCK, BLOCK
    scale = head_size ** (-0.5)

    def kernel(
        first_ref, raw_ref, qg_ref, kg_ref, cos_ref, sin_ref, segq_ref, segk_ref,
        mixed_ref, lse_ref, query_ref, key_ref, value_ref, keyt_ref,
        keys, values_t, masked, top, total, acc,
    ):
        s, i = pl.program_id(0), pl.program_id(1)
        cosine, sine = tiled(cos_ref[...], heads), tiled(sin_ref[...], heads)
        ones = group_ones(width, head_size)
        query, key, value = split_raw(raw_ref[...], width, head_size, heads)

        def norm_rope(x, gain):
            x = x * lax.rsqrt(group_sum(x * x, ones) * (1.0 / head_size) + epsilon) * gain
            return x * cosine + swap_halves(x, head_size) * sine

        query_low = norm_rope(query, qg_ref[...]).astype(jnp.bfloat16)
        key_rot = norm_rope(key, kg_ref[...])
        key_low = key_rot.astype(jnp.bfloat16)
        query_ref[...] = query_low
        key_ref[...] = key_low
        value_ref[...] = value.astype(jnp.bfloat16)
        keyt_ref[0] = jnp.transpose(key_rot)[:head_size].astype(jnp.bfloat16)
        keys[pl.ds(pl.multiple_of(i * block, block), block), :] = key_low
        values_t[i] = jnp.transpose(value)[:head_size].astype(jnp.bfloat16)
        scaled = query_low * jnp.bfloat16(scale)
        zero = jnp.zeros_like(scaled)
        for h, mask in enumerate(head_masks(block, width, head_size, heads)):
            masked[h] = jnp.where(mask, scaled, zero)
        top[...] = jnp.full_like(top, NEG)
        total[...] = jnp.zeros_like(total)
        acc[...] = jnp.zeros_like(acc)
        query_pos = i * block + lax.broadcasted_iota(jnp.int32, (block, block), 1)
        segment_query = segq_ref[0]

        def step(j, carry):
            at = pl.multiple_of(j * block, block)
            key_pos = at + lax.broadcasted_iota(jnp.int32, (block, block), 0)
            allowed = (key_pos <= query_pos) & (segk_ref[pl.ds(at, block), :] == segment_query)
            bias = jnp.where(allowed, 0.0, NEG)
            key_block = keys[pl.ds(at, block), :]
            value_t = values_t[j]
            for h in range(heads):
                scores = dot_nt(key_block, masked[h]) + bias
                before = top[h : h + 1, :]
                now = jnp.maximum(before, jnp.max(scores, axis=0, keepdims=True))
                shifted = jnp.exp(scores - now)
                fade = jnp.exp(before - now)
                top[h : h + 1, :] = now
                total[h : h + 1, :] = fade * total[h : h + 1, :] + jnp.sum(
                    shifted, axis=0, keepdims=True
                )
                span = slice(h * head_size, (h + 1) * head_size)
                acc[span, :] = fade * acc[span, :] + dot_nn(value_t, shifted.astype(jnp.bfloat16))
            return carry

        lax.fori_loop(first_ref[s, i], i + 1, step, 0)
        for h in range(heads):
            span = slice(h * head_size, (h + 1) * head_size)
            acc[span, :] = acc[span, :] / total[h : h + 1, :]
        mixed_ref[...] = jnp.transpose(acc[...]).astype(jnp.bfloat16)
        lse_ref[...] = top[...] + jnp.log(jnp.maximum(total[...], 1e-30))

    cosine, sine = rope_tables(head_size)
    at_rows = lambda s, i, first: (s * blocks + i, 0)
    fixed = lambda s, i, first: (0, 0)
    at_lanes = lambda s, i, first: (0, s * blocks + i)
    low = jnp.bfloat16
    pairs = blocks * (blocks + 1) // 2 * seqs * heads
    return pl.pallas_call(
        kernel,
        grid_spec=pltpu.PrefetchScalarGridSpec(
            num_scalar_prefetch=1,
            grid=(seqs, blocks),
            in_specs=[
                pl.BlockSpec((block, raw.shape[1]), at_rows),
                pl.BlockSpec((1, width), fixed),
                pl.BlockSpec((1, width), fixed),
                pl.BlockSpec((block, head_size), lambda s, i, first: (i, 0)),
                pl.BlockSpec((block, head_size), lambda s, i, first: (i, 0)),
                pl.BlockSpec((1, 1, block), lambda s, i, first: (s, 0, i)),
                pl.BlockSpec((SEQ, 1), lambda s, i, first: (s, 0)),
            ],
            out_specs=[
                pl.BlockSpec((block, width), at_rows),
                pl.BlockSpec((8, block), at_lanes),
                pl.BlockSpec((block, width), at_rows),
                pl.BlockSpec((block, width), at_rows),
                pl.BlockSpec((block, width), at_rows),
                pl.BlockSpec((1, head_size, block), lambda s, i, first: (s * blocks + i, 0, 0)),
            ],
            scratch_shapes=[
                pltpu.VMEM((SEQ, width), low),
                pltpu.VMEM((blocks, head_size, block), low),
                pltpu.VMEM((heads, block, width), low),
                pltpu.VMEM((8, block), jnp.float32),
                pltpu.VMEM((8, block), jnp.float32),
                pltpu.VMEM((width, block), jnp.float32),
            ],
        ),
        out_shape=[
            jax.ShapeDtypeStruct((rows, width), low),
            jax.ShapeDtypeStruct((8, rows), jnp.float32),
            jax.ShapeDtypeStruct((rows, width), low),
            jax.ShapeDtypeStruct((rows, width), low),
            jax.ShapeDtypeStruct((rows, width), low),
            jax.ShapeDtypeStruct((rows // block, head_size, block), low),
        ],
        compiler_params=pltpu.CompilerParams(vmem_limit_bytes=40 << 20),
        cost_estimate=pl.CostEstimate(flops=0, bytes_accessed=0, transcendentals=0),
        name="attention_forward",
    )(
        first_block, raw,
        tiled(query_gain.astype(jnp.float32)[None], heads),
        tiled(key_gain.astype(jnp.float32)[None], heads),
        cosine, sine, segments[:, None, :], segments.reshape(rows, 1),
    )


def attention_backward(
    raw, query_gain, key_gain, segments, first_block, saved, mixed_grad
):
    mixed, lse, query_low, key_low, value_low, key_t = saved
    head_size = query_gain.shape[0]
    rows, width = mixed.shape
    heads = width // head_size
    seqs, blocks, block = rows // SEQ, SEQ // BLOCK, BLOCK
    scale = head_size ** (-0.5)

    def kernel(
        first_ref, raw_ref, qg_ref, kg_ref, cos_ref, sin_ref, segq_ref, segk_ref,
        mixed_ref, lse_ref, query_ref, grad_ref, keys_ref, values_ref, keyt_ref,
        out_ref, qgg_ref, kgg_ref,
        masked, masked_grad, key_sums, value_sums, query_sums, deltas,
    ):
        s, i = pl.program_id(0), blocks - 1 - pl.program_id(1)

        @pl.when(pl.program_id(1) == 0)
        def _():
            key_sums[...] = jnp.zeros_like(key_sums)
            value_sums[...] = jnp.zeros_like(value_sums)

        @pl.when((pl.program_id(1) == 0) & (s == 0))
        def _():
            qgg_ref[...] = jnp.zeros_like(qgg_ref)
            kgg_ref[...] = jnp.zeros_like(kgg_ref)

        query_sums[...] = jnp.zeros_like(query_sums)
        grad = grad_ref[...]
        scaled = query_ref[...] * jnp.bfloat16(scale)
        zero = jnp.zeros_like(scaled)
        for h, mask in enumerate(head_masks(block, width, head_size, heads)):
            span = slice(h * block, (h + 1) * block)
            masked[span, :] = jnp.where(mask, scaled, zero)
            masked_grad[span, :] = jnp.where(mask, grad, zero)
        product = jnp.transpose(grad.astype(jnp.float32) * mixed_ref[...].astype(jnp.float32))
        for h in range(heads):
            deltas[h : h + 1, :] = jnp.sum(
                product[h * head_size : (h + 1) * head_size], axis=0, keepdims=True
            )
        query_pos = i * block + lax.broadcasted_iota(jnp.int32, (block, block), 1)
        segment_query = segq_ref[0]

        def step(j, carry):
            at = pl.multiple_of(j * block, block)
            key_pos = at + lax.broadcasted_iota(jnp.int32, (block, block), 0)
            allowed = (key_pos <= query_pos) & (segk_ref[pl.ds(at, block), :] == segment_query)
            bias = jnp.where(allowed, 0.0, NEG)
            key_block = keys_ref[pl.ds(at, block), :]
            value_block = values_ref[pl.ds(at, block), :]
            key_t = keyt_ref[j]
            lows, grads = [], []
            for h in range(heads):
                span = slice(h * block, (h + 1) * block)
                scores = dot_nt(key_block, masked[span, :]) + bias
                probability = jnp.exp(scores - lse_ref[h : h + 1, :])
                prob_grad = dot_nt(value_block, masked_grad[span, :])
                score_grad = (probability * (prob_grad - deltas[h : h + 1, :])).astype(jnp.bfloat16)
                lows.append(probability.astype(jnp.bfloat16))
                grads.append(score_grad)
                rows_h = slice(h * head_size, (h + 1) * head_size)
                query_sums[rows_h, :] += dot_nn(key_t, score_grad)
            value_sums[pl.ds(at, block), :] += dot_nn(
                jnp.concatenate(lows, axis=1), masked_grad[...]
            )
            key_sums[pl.ds(at, block), :] += dot_nn(jnp.concatenate(grads, axis=1), masked[...])
            return carry

        lax.fori_loop(first_ref[s, i], i + 1, step, 0)
        cosine, sine = tiled(cos_ref[...], heads), tiled(sin_ref[...], heads)
        ones = group_ones(width, head_size)
        query, key, _ = split_raw(raw_ref[...], width, head_size, heads)

        def all_heads(x):
            total = x
            for h in range(1, heads):
                total = total + pltpu.roll(x, h * head_size, 1)
            return total

        def norm_rope_back(x, up, gain):
            unrot = up * cosine - swap_halves(up, head_size) * sine
            inverse = lax.rsqrt(group_sum(x * x, ones) * (1.0 / head_size) + epsilon)
            gain_part = jnp.sum(unrot * x * inverse, axis=0, keepdims=True)
            scaled_up = unrot * gain
            mean = group_sum(scaled_up * x, ones) * (1.0 / head_size)
            return scaled_up * inverse - x * (mean * inverse * inverse * inverse), gain_part

        query_up = jnp.transpose(query_sums[...]) * scale
        query_grad, query_part = norm_rope_back(query, query_up, qg_ref[...])
        here = pl.ds(pl.multiple_of(i * block, block), block)
        key_up = all_heads(key_sums[here, :])
        key_grad, key_part = norm_rope_back(key, key_up, kg_ref[...])
        value_grad = all_heads(value_sums[here, :])
        out_ref[...] = jnp.concatenate(
            [query_grad, key_grad[:, :head_size], value_grad[:, :head_size]], axis=1
        ).astype(jnp.bfloat16)
        qgg_ref[...] += query_part
        kgg_ref[...] += key_part

    cosine, sine = rope_tables(head_size)
    at_rows = lambda s, i, first: (s * blocks + blocks - 1 - i, 0)
    fixed = lambda s, i, first: (0, 0)
    at_lanes = lambda s, i, first: (0, s * blocks + blocks - 1 - i)
    at_seq = lambda s, i, first: (s, 0)
    low = jnp.bfloat16
    pairs = blocks * (blocks + 1) // 2 * seqs * heads
    grads, query_part, key_part = pl.pallas_call(
        kernel,
        grid_spec=pltpu.PrefetchScalarGridSpec(
            num_scalar_prefetch=1,
            grid=(seqs, blocks),
            in_specs=[
                pl.BlockSpec((block, raw.shape[1]), at_rows),
                pl.BlockSpec((1, width), fixed),
                pl.BlockSpec((1, width), fixed),
                pl.BlockSpec((block, head_size), lambda s, i, first: (blocks - 1 - i, 0)),
                pl.BlockSpec((block, head_size), lambda s, i, first: (blocks - 1 - i, 0)),
                pl.BlockSpec((1, 1, block), lambda s, i, first: (s, 0, blocks - 1 - i)),
                pl.BlockSpec((SEQ, 1), at_seq),
                pl.BlockSpec((block, width), at_rows),
                pl.BlockSpec((8, block), at_lanes),
                pl.BlockSpec((block, width), at_rows),
                pl.BlockSpec((block, width), at_rows),
                pl.BlockSpec((SEQ, width), at_seq),
                pl.BlockSpec((SEQ, width), at_seq),
                pl.BlockSpec((blocks, head_size, block), lambda s, i, first: (s, 0, 0)),
            ],
            out_specs=[
                pl.BlockSpec((block, raw.shape[1]), at_rows),
                pl.BlockSpec((1, width), fixed),
                pl.BlockSpec((1, width), fixed),
            ],
            scratch_shapes=[
                pltpu.VMEM((heads * block, width), low),
                pltpu.VMEM((heads * block, width), low),
                pltpu.VMEM((SEQ, width), jnp.float32),
                pltpu.VMEM((SEQ, width), jnp.float32),
                pltpu.VMEM((width, block), jnp.float32),
                pltpu.VMEM((8, block), jnp.float32),
            ],
        ),
        out_shape=[
            jax.ShapeDtypeStruct(raw.shape, low),
            jax.ShapeDtypeStruct((1, width), jnp.float32),
            jax.ShapeDtypeStruct((1, width), jnp.float32),
        ],
        compiler_params=pltpu.CompilerParams(vmem_limit_bytes=48 << 20),
        cost_estimate=pl.CostEstimate(flops=0, bytes_accessed=0, transcendentals=0),
        name="attention_backward",
    )(
        first_block, raw,
        tiled(query_gain.astype(jnp.float32)[None], heads),
        tiled(key_gain.astype(jnp.float32)[None], heads),
        cosine, sine, segments[:, None, :], segments.reshape(rows, 1),
        mixed, lse, query_low, mixed_grad, key_low, value_low, key_t,
    )
    return (
        grads,
        jnp.sum(query_part.reshape(heads, head_size), axis=0),
        key_part[0, :head_size],
    )


def first_blocks(segments):
    starts = segments[:, :: BLOCK]
    below = jnp.sum(segments[:, None, :] < starts[:, :, None], axis=-1, dtype=jnp.int32)
    return below // BLOCK

MESH = pl.DeviceIdType.MESH


class Lattice:
    def __init__(self, count):
        self.depth = count // 2
        me = lax.axis_index("wide")
        self.z, self.x = me // 2, me % 2
        self.below = jnp.minimum(self.z, self.depth - 1 - self.z)
        self.low_side = self.z > self.depth - 1 - self.z

    def at(self, z, x):
        return z * 2 + x

    def order(self, m):
        near = m <= 2 * self.below
        r = jnp.where(near, (m + 1) // 2, m - self.below)
        minus = jnp.where(near, m % 2 == 1, self.low_side)
        return jnp.where(minus, self.z - r, self.z + r), r


def greet(lat, partners=()):
    barrier = pltpu.get_barrier_semaphore()
    last = lat.depth - 1
    for partner in partners:
        pl.semaphore_signal(
            barrier, inc=1, device_id={"narrow": partner}, device_id_type=MESH
        )

    def each(act):
        act(lat.at(lat.z, 1 - lat.x))

        @pl.when(lat.z > 0)
        def _():
            act(lat.at(lat.z - 1, lat.x))

        @pl.when(lat.z < last)
        def _():
            act(lat.at(lat.z + 1, lat.x))

    each(lambda who: pl.semaphore_signal(barrier, inc=1, device_id={"wide": who}, device_id_type=MESH))
    own = 1 + len(partners)
    pl.semaphore_wait(barrier, own + jnp.minimum(lat.z, 1) + jnp.minimum(last - lat.z, 1))


def gather_chunks(lat, buffers, send_sems, recv_sems, compute, meanwhile=None, landed=None):
    z, x, depth = lat.z, lat.x, lat.depth
    last = depth - 1
    every = range(len(buffers))

    def copy(k, chunk, way, slot, target):
        return pltpu.make_async_remote_copy(
            src_ref=buffers[k].at[chunk], dst_ref=buffers[k].at[chunk],
            send_sem=send_sems.at[k, way, slot], recv_sem=recv_sems.at[k, chunk],
            device_id={"wide": target}, device_id_type=MESH,
        )

    def up(k, zz):
        return copy(k, lat.at(zz, x), 0, zz, lat.at(z + 1, x))

    def down(k, zz):
        return copy(k, lat.at(zz, x), 1, zz, lat.at(z - 1, x))

    def across(k, zz):
        return copy(k, lat.at(zz, x), 2, zz, lat.at(z, 1 - x))

    def arrived(k, chunk):
        copy(k, chunk, 2, 0, lat.at(z, 1 - x)).wait_recv()
        if landed is not None:
            landed(k, chunk)

    for k in every:
        @pl.when(z < last)
        def _():
            up(k, z).start()

        @pl.when(z > 0)
        def _():
            down(k, z).start()

        across(k, z).start()
    if meanwhile is not None:
        meanwhile()

    def step(m, carry):
        zz, r = lat.order(m)
        _, before = lat.order(m - 1)

        @pl.when((m >= 1) & (m < depth) & (r != before))
        def _():
            for k in every:
                @pl.when(z - r >= 0)
                def _():
                    arrived(k, lat.at(z - r, x))

                    @pl.when(z < last)
                    def _():
                        up(k, z - r).start()

                    across(k, z - r).start()

                @pl.when(z + r <= last)
                def _():
                    arrived(k, lat.at(z + r, x))

                    @pl.when(z > 0)
                    def _():
                        down(k, z + r).start()

                    across(k, z + r).start()

        mirror = lat.order(jnp.maximum(m - 1, 0))[0]

        def part(p, carry):
            @pl.when((p == 1) & (m >= 1))
            def _():
                for k in every:
                    arrived(k, lat.at(mirror, 1 - x))

            @pl.when(((p == 0) & (m < depth)) | ((p == 1) & (m >= 1)))
            def _():
                compute(jnp.where(p == 0, lat.at(zz, x), lat.at(mirror, 1 - x)))

            return carry

        return lax.fori_loop(0, 2, part, carry)

    lax.fori_loop(0, depth + 1, step, 0)

    def settle(zz, carry):
        for k in every:
            @pl.when((z < last) & (zz <= z))
            def _():
                up(k, zz).wait_send()

            @pl.when((z > 0) & (zz >= z))
            def _():
                down(k, zz).wait_send()

            across(k, zz).wait_send()
        return carry

    lax.fori_loop(0, depth, settle, 0)


def project_gathered(local, weights, values, strips, counts, collective_id):
    rows, model = local.shape
    columns = weights.shape[1]
    narrow_count, wide_count = counts
    depth = wide_count // 2
    strip = strips[0].shape[0]
    tall = strip * len(strips)

    def kernel(
        local_ref, weights_ref, values_ref, *refs
    ):
        strip_refs, refs = refs[: len(strips)], refs[len(strips) :]
        full_ref, out_ref, sum_ref, refs = refs[0], refs[1], refs[2], refs[3:]
        spread_refs, refs = refs[: len(strips)], refs[len(strips) :]
        (full, spread, send_sems, recv_sems, own_sems, store_sems, spread_sems, y_send, core_send, spread_recv,
         mine, held, total, load_sem, *sems) = refs
        lat = Lattice(wide_count)
        me = lat.at(lat.z, lat.x)
        narrow_me = lax.axis_index("narrow")
        core_side, y_side = narrow_me + 1 - 2 * (narrow_me % 2), (narrow_me + 2) % 4
        corner = y_side + 1 - 2 * (y_side % 2)
        loads = [
            pltpu.make_async_copy(local_ref, full.at[me], own_sems.at[0]),
            pltpu.make_async_copy(values_ref, mine, load_sem),
        ] + [
            pltpu.make_async_copy(
                ref, spread.at[narrow_me, me, pl.ds(k * strip, strip)], own_sems.at[1 + k]
            )
            for k, ref in enumerate(strip_refs)
        ]
        for load in loads:
            load.start()
        arrive = greet_all(counts)
        for load in loads:
            load.wait()
        arrive()
        narrow, wide = exchange_pair(counts, mine, held, total, *sems)

        def to_side(n, chunk, target, send_sem):
            return pltpu.make_async_remote_copy(
                src_ref=spread.at[n, chunk], dst_ref=spread.at[n, chunk],
                send_sem=send_sem, recv_sem=spread_recv.at[n, chunk],
                device_id={"narrow": target}, device_id_type=MESH,
            )

        def to_y(chunk):
            return to_side(narrow_me, chunk, y_side, y_send.at[chunk])

        def to_core(n, chunk):
            return to_side(n, chunk, core_side, core_send.at[n // 2, chunk])

        def spread_out(chunk):
            to_y(chunk).start()
            to_core(narrow_me, chunk).start()

        def landed(k, chunk):
            if k == 0:
                spread_out(chunk)

        def meanwhile():
            spread_out(me)
            narrow.start()
            total[...] = narrow.total()
            wide.start()

        def keep(chunk):
            return pltpu.make_async_copy(full.at[chunk], full_ref.at[chunk], store_sems.at[chunk])

        def keep_strip(n, chunk, k):
            return pltpu.make_async_copy(
                spread.at[n, chunk, pl.ds(k * strip, strip)], spread_refs[k].at[chunk, n],
                spread_sems.at[k, n, chunk],
            )

        def keep_strips(n, chunk):
            for k in range(len(strips)):
                keep_strip(n, chunk, k).start()

        def compute(chunk):
            keep(chunk).start()
            keep_strips(narrow_me, chunk)
            at = pl.multiple_of(chunk * rows, rows)
            out_ref[pl.ds(at, rows), :] = jnp.dot(
                full[chunk], weights_ref[...], preferred_element_type=jnp.float32
            )

        gather_chunks(
            lat, [spread.at[narrow_me], full], send_sems, recv_sems, compute, meanwhile, landed
        )

        def event(e):
            zz = lat.order(e // 2)[0]
            return lat.at(zz, jnp.where(e % 2 == 0, lat.x, 1 - lat.x))

        def pass_on(e, carry):
            chunk = event(e)
            to_side(y_side, chunk, y_side, y_send.at[chunk]).wait_recv()
            to_core(y_side, chunk).start()
            keep_strips(y_side, chunk)
            return carry

        def take(e, carry):
            chunk = event(e)
            for n in (core_side, corner):
                to_side(n, chunk, core_side, core_send.at[0, chunk]).wait_recv()
                keep_strips(n, chunk)
            return carry

        lax.fori_loop(0, wide_count, pass_on, 0)
        lax.fori_loop(0, wide_count, take, 0)
        sum_ref[...] = wide.total()
        narrow.settle()
        wide.settle()

        def settle(c, carry):
            keep(c).wait()
            to_y(c).wait_send()
            to_core(narrow_me, c).wait_send()
            to_core(y_side, c).wait_send()
            for k in range(len(strips)):
                for n in range(narrow_count):
                    keep_strip(n, c, k).wait()
            return carry

        lax.fori_loop(0, wide_count, settle, 0)

    vmem = pl.BlockSpec(memory_space=pltpu.VMEM)
    hbm = pl.BlockSpec(memory_space=pl.ANY)
    low = local.dtype
    full, out, sums, *gathered = pl.pallas_call(
        kernel,
        in_specs=[hbm, vmem, hbm] + [hbm] * len(strips),
        out_specs=[hbm, vmem, vmem] + [hbm] * len(strips),
        out_shape=[
            jax.ShapeDtypeStruct((wide_count, rows, model), low),
            jax.ShapeDtypeStruct((wide_count * rows, columns), jnp.float32),
            jax.ShapeDtypeStruct(values.shape, jnp.float32),
        ]
        + [jax.ShapeDtypeStruct((wide_count, narrow_count, strip, model), low)] * len(strips),
        scratch_shapes=[
            pltpu.VMEM((wide_count, rows, model), low),
            pltpu.VMEM((narrow_count, wide_count, tall, model), low),
            pltpu.SemaphoreType.DMA((2, 3, depth)),
            pltpu.SemaphoreType.DMA((2, wide_count)),
            pltpu.SemaphoreType.DMA((1 + len(strips),)),
            pltpu.SemaphoreType.DMA((wide_count,)),
            pltpu.SemaphoreType.DMA((len(strips), narrow_count, wide_count)),
            pltpu.SemaphoreType.DMA((wide_count,)),
            pltpu.SemaphoreType.DMA((2, wide_count)),
            pltpu.SemaphoreType.DMA((narrow_count, wide_count)),
        ]
        + exchange_scratch(values.shape, counts),
        compiler_params=pltpu.CompilerParams(
            collective_id=collective_id, has_side_effects=True, vmem_limit_bytes=48 << 20
        ),
        name="project_gathered",
    )(local, weights, values, *strips)
    flat = narrow_count * wide_count * strip
    return full.reshape(wide_count * rows, model), out, sums, [g.reshape(flat, model) for g in gathered]


def nt(left, right):
    return lax.dot_general(
        left, right, (((1,), (1,)), ((), ())), preferred_element_type=jnp.float32
    )


def forward_gathered(local, gate_weight, up_weight, down_weight, wide_count, collective_id):
    rows, model = local.shape
    hidden = gate_weight.shape[1]
    depth = wide_count // 2
    tile = min(256, hidden)
    wide_tile = min(512, model)

    def kernel(
        local_ref, gate_ref, up_ref, down_ref, full_ref, gates_ref, ups_ref, acts_ref, downs_ref,
        full, gates, ups, acts, downs, send_sems, recv_sems, load_sem, store_sems,
    ):
        lat = Lattice(wide_count)
        me = lat.at(lat.z, lat.x)
        load = pltpu.make_async_copy(local_ref, full.at[me], load_sem)
        load.start()
        greet(lat)
        load.wait()
        kept = ((full, full_ref), (gates, gates_ref), (ups, ups_ref), (acts, acts_ref), (downs, downs_ref))

        def keep(which, chunk):
            source, target = kept[which]
            return pltpu.make_async_copy(source.at[chunk], target.at[chunk], store_sems.at[which, chunk])

        def compute(chunk):
            keep(0, chunk).start()
            rows_in = full[chunk]

            def inner(t, carry):
                at = pl.ds(pl.multiple_of(t * tile, tile), tile)
                gate = jnp.dot(rows_in, gate_ref[:, at], preferred_element_type=jnp.float32)
                up = jnp.dot(rows_in, up_ref[:, at], preferred_element_type=jnp.float32)
                gates[chunk, :, at] = gate
                ups[chunk, :, at] = up
                acts[chunk, :, at] = (gate * lax.logistic(gate) * up).astype(jnp.bfloat16)
                return carry

            lax.fori_loop(0, hidden // tile, inner, 0)
            for which in (1, 2, 3):
                keep(which, chunk).start()
            act = acts[chunk]

            def outer(t, carry):
                at = pl.ds(pl.multiple_of(t * wide_tile, wide_tile), wide_tile)
                downs[chunk, :, at] = jnp.dot(
                    act, down_ref[:, at], preferred_element_type=jnp.float32
                ).astype(jnp.bfloat16)
                return carry

            lax.fori_loop(0, model // wide_tile, outer, 0)
            keep(4, chunk).start()

        gather_chunks(lat, [full], send_sems, recv_sems, compute)
        for which in range(5):
            lax.fori_loop(0, wide_count, lambda c, carry: (keep(which, c).wait(), carry)[1], 0)

    low = jnp.bfloat16
    outs = [
        ((wide_count, rows, model), low),
        ((wide_count, rows, hidden), jnp.float32),
        ((wide_count, rows, hidden), jnp.float32),
        ((wide_count, rows, hidden), low),
        ((wide_count, rows, model), low),
    ]
    vmem = pl.BlockSpec(memory_space=pltpu.VMEM)
    hbm = pl.BlockSpec(memory_space=pl.ANY)
    results = pl.pallas_call(
        kernel,
        in_specs=[hbm, vmem, vmem, vmem],
        out_specs=[hbm] * 5,
        out_shape=[jax.ShapeDtypeStruct(*o) for o in outs],
        scratch_shapes=[pltpu.VMEM(*o) for o in outs]
        + [
            pltpu.SemaphoreType.DMA((1, 3, depth)),
            pltpu.SemaphoreType.DMA((1, wide_count)),
            pltpu.SemaphoreType.DMA,
            pltpu.SemaphoreType.DMA((5, wide_count)),
        ],
        compiler_params=pltpu.CompilerParams(
            collective_id=collective_id, has_side_effects=True, vmem_limit_bytes=60 << 20
        ),
        name="forward_gathered",
    )(local, gate_weight, up_weight, down_weight)
    return [r.reshape(wide_count * rows, r.shape[2]) for r in results]


def tn(left, right):
    return lax.dot_general(
        left, right, (((0,), (0,)), ((), ())), preferred_element_type=jnp.float32
    )


def backward_scattered(
    cot, gates, ups, hidden_rows, gate_weight, up_weight, down_weight, wide_count, collective_id
):
    model = cot.shape[1]
    rows = cot.shape[0] // wide_count
    hidden = gate_weight.shape[1]
    depth = wide_count // 2
    tile = min(256, hidden)
    wide_tile = min(512, model)
    low = jnp.bfloat16

    half = model // 2
    slab = min(256, half)
    per = half // slab

    def kernel(
        cot_ref, gates_ref, ups_ref, hidden_ref, gate_ref, up_ref, down_ref,
        sum_ref, gate_half_ref, up_half_ref,
        cots, gate_in, up_in, gate_low, up_low, foreign, own, crossed, from_low, from_high,
        columns, given, taken, kept,
        in_sems, cross_send, cross_recv, chain_send, low_recv, high_recv,
        column_sems, give_send, give_recv, kept_sems,
    ):
        lat = Lattice(wide_count)
        z, x, last = lat.z, lat.x, depth - 1
        narrow = lax.axis_index("narrow")
        core = narrow % 2
        partner = narrow + 1 - 2 * core

        def place(e):
            zz = lat.order(depth - 1 - e % depth)[0]
            return zz, lat.at(zz, jnp.where(e < depth, 1 - x, x))

        def loads(e):
            slot = e % 2
            chunk = place(e)[1]
            return [
                pltpu.make_async_copy(source.at[chunk], target.at[slot], in_sems.at[k, slot])
                for k, (source, target) in enumerate(
                    ((cot_ref, cots), (gates_ref, gate_in), (ups_ref, up_in))
                )
            ]

        def cross(zz):
            return pltpu.make_async_remote_copy(
                src_ref=foreign.at[zz], dst_ref=crossed.at[zz],
                send_sem=cross_send.at[zz], recv_sem=cross_recv.at[zz],
                device_id={"wide": lat.at(z, 1 - x)}, device_id_type=MESH,
            )

        def rise(zz):
            return pltpu.make_async_remote_copy(
                src_ref=own.at[zz], dst_ref=from_low.at[zz],
                send_sem=chain_send.at[zz], recv_sem=low_recv.at[zz],
                device_id={"wide": lat.at(z + 1, x)}, device_id_type=MESH,
            )

        def sink(zz):
            return pltpu.make_async_remote_copy(
                src_ref=own.at[zz], dst_ref=from_high.at[zz],
                send_sem=chain_send.at[zz], recv_sem=high_recv.at[zz],
                device_id={"wide": lat.at(z - 1, x)}, device_id_type=MESH,
            )

        def slab_of(e):
            side = jnp.where(e < 2 * per, 1 - core, core)
            return e // per % 2, e % per, side * per + e % per

        def column_load(e):
            at = pl.ds(pl.multiple_of(slab_of(e)[2] * slab, slab), slab)
            return pltpu.make_async_copy(
                hidden_ref.at[:, :, at], columns.at[e % 2], column_sems.at[e % 2]
            )

        def give(e):
            which, n, _ = slab_of(e)
            return pltpu.make_async_remote_copy(
                src_ref=given.at[e % 2], dst_ref=taken.at[which, n],
                send_sem=give_send.at[e % 2], recv_sem=give_recv.at[which, n],
                device_id={"narrow": partner}, device_id_type=MESH,
            )

        def keep(e, k):
            target = (gate_half_ref, up_half_ref)[k]
            return pltpu.make_async_copy(kept.at[e % 2], target.at[slab_of(e)[1]], kept_sems.at[e % 2])

        def weight_slab(e):
            which, n, _ = slab_of(e)
            column_load(e).wait()

            @pl.when(e + 1 < 4 * per)
            def _():
                column_load(e + 1).start()

            tokens = columns[e % 2].reshape(wide_count * rows, slab)

            @pl.when((e >= 2) & (e < 2 * per + 2))
            def _():
                give(e - 2).wait_send()

            @pl.when(e >= 2 * per + 2)
            def _():
                keep(e - 2, 0).wait()

            def product(k):
                source = (gate_low, up_low)[k]
                value = tn(tokens, source[...].reshape(wide_count * rows, hidden))

                @pl.when(e < 2 * per)
                def _():
                    given[e % 2] = value.astype(low)
                    give(e).start()

                @pl.when(e >= 2 * per)
                def _():
                    give(e).wait_recv()
                    kept[e % 2] = (value + taken[k, n].astype(jnp.float32)).astype(low)
                    keep(e, k).start()

            @pl.when(which == 0)
            def _():
                product(0)

            @pl.when(which == 1)
            def _():
                product(1)

        for copy in loads(0):
            copy.start()
        column_load(0).start()
        greet(lat, (partner,))

        def partial(e, target, zz):
            slot = e % 2
            for copy in loads(e):
                copy.wait()

            @pl.when(e + 1 < 2 * depth)
            def _():
                for copy in loads(e + 1):
                    copy.start()

            cot_rows = cots[slot]
            chunk = place(e)[1]

            def inner(t, carry):
                at = pl.ds(pl.multiple_of(t * tile, tile), tile)
                act_grad = nt(cot_rows, down_ref[at, :])
                gate, up = gate_in[slot, :, at], up_in[slot, :, at]
                sigmoid = lax.logistic(gate)
                gate_low[chunk, :, at] = (
                    act_grad * up * sigmoid * (1.0 + gate * (1.0 - sigmoid))
                ).astype(low)
                up_low[chunk, :, at] = (act_grad * gate * sigmoid).astype(low)
                return carry

            lax.fori_loop(0, hidden // tile, inner, 0)
            gate_rows, up_rows = gate_low[chunk], up_low[chunk]

            def outer(t, carry):
                at = pl.ds(pl.multiple_of(t * wide_tile, wide_tile), wide_tile)
                target[zz, :, at] = (
                    nt(gate_rows, gate_ref[at, :]) + nt(up_rows, up_ref[at, :])
                ).astype(low)
                return carry

            lax.fori_loop(0, model // wide_tile, outer, 0)

        def send_step(e, carry):
            zz, _ = place(e)
            partial(e, foreign, zz)
            cross(zz).start()
            return carry

        lax.fori_loop(0, depth, send_step, 0)

        def own_step(e, carry):
            zz, _ = place(e)
            partial(e, own, zz)

            @pl.when(e == depth)
            def _():
                chain(zz)

            return carry

        def chain(zz):
            cross(zz).wait_recv()
            wide = jnp.float32

            @pl.when((zz > z) & (z > 0))
            def _():
                rise(zz).wait_recv()
                own[zz] = (own[zz].astype(wide) + crossed[zz].astype(wide) + from_low[zz].astype(wide)).astype(low)

            @pl.when((zz < z) & (z < last))
            def _():
                sink(zz).wait_recv()
                own[zz] = (own[zz].astype(wide) + crossed[zz].astype(wide) + from_high[zz].astype(wide)).astype(low)

            @pl.when(((zz > z) & (z == 0)) | ((zz < z) & (z == last)))
            def _():
                own[zz] = (own[zz].astype(wide) + crossed[zz].astype(wide)).astype(low)

            @pl.when(zz > z)
            def _():
                rise(zz).start()

            @pl.when(zz < z)
            def _():
                sink(zz).start()

            @pl.when(zz == z)
            def _():
                sum_ref[...] = own[zz].astype(wide) + crossed[zz].astype(wide)

                @pl.when(z > 0)
                def _():
                    rise(zz).wait_recv()
                    sum_ref[...] += from_low[zz].astype(wide)

                @pl.when(z < last)
                def _():
                    sink(zz).wait_recv()
                    sum_ref[...] += from_high[zz].astype(wide)

        lax.fori_loop(depth, 2 * depth, own_step, 0)

        def slab_step(e, carry):
            for k in range(1, depth):
                @pl.when(e == 4 * per * (k - 1) // (depth - 2))
                def _():
                    chain(place(depth + k)[0])

            @pl.when(e < 4 * per)
            def _():
                weight_slab(e)

            return carry

        lax.fori_loop(0, 4 * per + 1, slab_step, 0)
        for e in (4 * per - 2, 4 * per - 1):
            keep(e, 1).wait()

        def settle(zz, carry):
            cross(zz).wait_send()

            @pl.when(zz > z)
            def _():
                rise(zz).wait_send()

            @pl.when(zz < z)
            def _():
                sink(zz).wait_send()

            return carry

        lax.fori_loop(0, depth, settle, 0)

    vmem = pl.BlockSpec(memory_space=pltpu.VMEM)
    hbm = pl.BlockSpec(memory_space=pl.ANY)
    total, gate_half, up_half = pl.pallas_call(
        kernel,
        in_specs=[hbm, hbm, hbm, hbm, vmem, vmem, vmem],
        out_specs=[vmem] + [hbm] * 2,
        out_shape=[
            jax.ShapeDtypeStruct((rows, model), jnp.float32),
            jax.ShapeDtypeStruct((per, slab, hidden), low),
            jax.ShapeDtypeStruct((per, slab, hidden), low),
        ],
        scratch_shapes=[
            pltpu.VMEM((2, rows, model), low),
            pltpu.VMEM((2, rows, hidden), jnp.float32),
            pltpu.VMEM((2, rows, hidden), jnp.float32),
            pltpu.VMEM((wide_count, rows, hidden), low),
            pltpu.VMEM((wide_count, rows, hidden), low),
        ]
        + [pltpu.VMEM((depth, rows, model), low)] * 5
        + [
            pltpu.VMEM((2, wide_count, rows, slab), low),
            pltpu.VMEM((2, slab, hidden), low),
            pltpu.VMEM((2, per, slab, hidden), low),
            pltpu.VMEM((2, slab, hidden), low),
            pltpu.SemaphoreType.DMA((3, 2)),
        ]
        + [pltpu.SemaphoreType.DMA((depth,))] * 5
        + [
            pltpu.SemaphoreType.DMA((2,)),
            pltpu.SemaphoreType.DMA((2,)),
            pltpu.SemaphoreType.DMA((2, per)),
            pltpu.SemaphoreType.DMA((2,)),
        ],
        compiler_params=pltpu.CompilerParams(
            collective_id=collective_id, has_side_effects=True, vmem_limit_bytes=67043328
        ),
        name="backward_scattered",
    )(
        cot.reshape(wide_count, rows, model),
        gates.reshape(wide_count, rows, hidden),
        ups.reshape(wide_count, rows, hidden),
        hidden_rows.reshape(wide_count, rows, model),
        gate_weight, up_weight, down_weight,
    )
    return total, gate_half.reshape(half, hidden), up_half.reshape(half, hidden)


AXES = ("narrow", "wide")


def peers(k, counts, act):
    here = lax.axis_index(AXES[k])

    def one(step, carry):
        act((here + step) % counts[k])
        return carry

    lax.fori_loop(1, counts[k], one, 0)


def greet_all(counts):
    barrier = pltpu.get_barrier_semaphore()
    for k, axis in enumerate(AXES):
        peers(k, counts, lambda who: pl.semaphore_signal(
            barrier, inc=1, device_id={axis: who}, device_id_type=MESH))
    return lambda: pl.semaphore_wait(barrier, counts[0] + counts[1] - 2)


class Exchange:
    def __init__(self, k, counts, source, slots, sends, recvs):
        self.k, self.counts, self.source = k, counts, source
        self.slots, self.sends, self.recvs = slots, sends, recvs
        self.here = lax.axis_index(AXES[k])

    def copy(self, who, slot):
        return pltpu.make_async_remote_copy(
            src_ref=self.source, dst_ref=self.slots.at[slot],
            send_sem=self.sends.at[who], recv_sem=self.recvs.at[slot],
            device_id={AXES[self.k]: who}, device_id_type=MESH,
        )

    def start(self):
        peers(self.k, self.counts, lambda who: self.copy(who, self.here).start())
        self.slots[self.here] = self.source[...]

    def total(self):
        peers(self.k, self.counts, lambda who: self.copy(who, who).wait_recv())
        sums = self.slots[0]
        for n in range(1, self.counts[self.k]):
            sums = sums + self.slots[n]
        return sums

    def settle(self):
        peers(self.k, self.counts, lambda who: self.copy(who, self.here).wait_send())


def exchange_scratch(shape, counts):
    return [
        pltpu.VMEM(shape, jnp.float32),
        pltpu.VMEM((2, max(counts)) + shape, jnp.float32),
        pltpu.VMEM(shape, jnp.float32),
        pltpu.SemaphoreType.DMA,
        pltpu.SemaphoreType.DMA((counts[0],)),
        pltpu.SemaphoreType.DMA((counts[0],)),
        pltpu.SemaphoreType.DMA((counts[1],)),
        pltpu.SemaphoreType.DMA((counts[1],)),
    ]


def exchange_pair(counts, mine, held, total, narrow_send, narrow_recv, wide_send, wide_recv):
    return (
        Exchange(0, counts, mine, held.at[0], narrow_send, narrow_recv),
        Exchange(1, counts, total, held.at[1], wide_send, wide_recv),
    )


def sum_everywhere(values, counts, collective_id, strip=None):
    extra = [] if strip is None else [strip]

    def kernel(in_ref, *refs):
        strip_refs, refs = refs[: len(extra)], refs[len(extra) :]
        out_ref, refs = refs[0], refs[1:]
        gathered_refs, refs = refs[: len(extra)], refs[len(extra) :]
        mine, held, total, load_sem, narrow_send, narrow_recv, wide_send, wide_recv, *rest = refs
        load = pltpu.make_async_copy(in_ref, mine, load_sem)
        load.start()
        arrive = greet_all(counts)
        me = lax.axis_index("narrow")
        if extra:
            strips, strip_sem, strip_send, strip_recv = rest
            own = pltpu.make_async_copy(strip_refs[0], strips.at[me], strip_sem)
            own.start()
            own.wait()

        def strip_copy(who, slot):
            return pltpu.make_async_remote_copy(
                src_ref=strips.at[me], dst_ref=strips.at[slot],
                send_sem=strip_send.at[who], recv_sem=strip_recv.at[slot],
                device_id={"narrow": who}, device_id_type=MESH,
            )

        load.wait()
        arrive()
        narrow, wide = exchange_pair(
            counts, mine, held, total, narrow_send, narrow_recv, wide_send, wide_recv
        )
        narrow.start()
        if extra:
            peers(0, counts, lambda who: strip_copy(who, me).start())
        total[...] = narrow.total()
        wide.start()
        out_ref[...] = wide.total()
        narrow.settle()
        wide.settle()
        if extra:
            peers(0, counts, lambda who: strip_copy(who, who).wait_recv())
            gathered_refs[0][...] = strips[...]
            peers(0, counts, lambda who: strip_copy(who, me).wait_send())

    vmem, hbm = pl.BlockSpec(memory_space=pltpu.VMEM), pl.BlockSpec(memory_space=pl.ANY)
    out_shape = [jax.ShapeDtypeStruct(values.shape, jnp.float32)]
    scratch = exchange_scratch(values.shape, counts)
    if extra:
        whole = (counts[0],) + strip.shape
        out_shape += [jax.ShapeDtypeStruct(whole, strip.dtype)]
        scratch += [
            pltpu.VMEM(whole, strip.dtype),
            pltpu.SemaphoreType.DMA,
            pltpu.SemaphoreType.DMA((counts[0],)),
            pltpu.SemaphoreType.DMA((counts[0],)),
        ]
    results = pl.pallas_call(
        kernel,
        in_specs=[hbm] * (1 + len(extra)),
        out_specs=[vmem] * (1 + len(extra)),
        out_shape=out_shape,
        scratch_shapes=scratch,
        compiler_params=pltpu.CompilerParams(collective_id=collective_id, has_side_effects=True),
        name="sum_everywhere",
    )(values, *extra)
    if not extra:
        return results[0]
    return results[0], results[1].reshape(-1, strip.shape[1])


def greet_wide(counts, partners=()):
    barrier = pltpu.get_barrier_semaphore()
    peers(1, counts, lambda who: pl.semaphore_signal(
        barrier, inc=1, device_id={"wide": who}, device_id_type=MESH))
    for partner in partners:
        pl.semaphore_signal(
            barrier, inc=1, device_id={"narrow": partner}, device_id_type=MESH
        )
    pl.semaphore_wait(barrier, counts[1] - 1 + len(partners))


class Blocks:
    def __init__(self, counts, blocks, held, sends, recvs):
        self.counts, self.blocks, self.held = counts, blocks, held
        self.sends, self.recvs = sends, recvs
        self.me = lax.axis_index("wide")

    def copy(self, who, slot):
        return pltpu.make_async_remote_copy(
            src_ref=self.blocks.at[who], dst_ref=self.held.at[slot],
            send_sem=self.sends.at[who], recv_sem=self.recvs.at[slot],
            device_id={"wide": who}, device_id_type=MESH,
        )

    def start(self, who):
        self.copy(who, self.me).start()

    def each(self, act):
        peers(1, self.counts, act)

    def arrived(self, who):
        self.copy(who, who).wait_recv()

    def settle(self):
        self.each(lambda who: self.copy(who, self.me).wait_send())


def carry_over(source, target, sems):
    across = (lax.axis_index("narrow") + 2) % 4
    return pltpu.make_async_remote_copy(
        src_ref=source, dst_ref=target, send_sem=sems.at[0], recv_sem=sems.at[1],
        device_id={"narrow": across}, device_id_type=MESH,
    )


VMEM_SPEC = pl.BlockSpec(memory_space=pltpu.VMEM)
HBM_SPEC = pl.BlockSpec(memory_space=pl.ANY)


def mix_and_project(mixed, output_full, counts, collective_id):
    wide_count = counts[1]
    rows, width = mixed.shape[0] // wide_count, mixed.shape[1]
    model = output_full.shape[1]
    tile = min(512, model)

    def kernel(mixed_ref, weight_ref, out_ref, held_ref, sends, recvs):
        blocks = Blocks(counts, mixed_ref, held_ref, sends, recvs)
        greet_wide(counts)
        blocks.each(blocks.start)
        held_ref[blocks.me] = mixed_ref[blocks.me]

        def add(who, first):
            rows_in = held_ref[who]

            def one(t, carry):
                at = pl.ds(pl.multiple_of(t * tile, tile), tile)
                part = jnp.dot(
                    rows_in, weight_ref[pl.ds(pl.multiple_of(who * width, width), width), at],
                    preferred_element_type=jnp.float32,
                )
                out_ref[:, at] = part if first else out_ref[:, at] + part
                return carry

            lax.fori_loop(0, model // tile, one, 0)

        add(blocks.me, True)

        def later(who):
            blocks.arrived(who)
            add(who, False)

        blocks.each(later)
        blocks.settle()

    return pl.pallas_call(
        kernel,
        in_specs=[VMEM_SPEC, VMEM_SPEC],
        out_specs=[VMEM_SPEC, VMEM_SPEC],
        out_shape=[
            jax.ShapeDtypeStruct((rows, model), jnp.float32),
            jax.ShapeDtypeStruct((wide_count, rows, width), mixed.dtype),
        ],
        scratch_shapes=[pltpu.SemaphoreType.DMA((wide_count,))] * 2,
        compiler_params=pltpu.CompilerParams(
            collective_id=collective_id, has_side_effects=True, vmem_limit_bytes=32 << 20
        ),
        name="mix_and_project",
    )(mixed.reshape(wide_count, rows, width), output_full)


def unmix(middle_low, output_full, mixed_blocks, carried, counts, collective_id):
    wide_count = counts[1]
    rows, model = middle_low.shape
    width = mixed_blocks.shape[2]
    strip = width // 4
    low = jnp.bfloat16

    def kernel(
        middle_ref, weight_ref, mixed_ref, carried_ref, held_ref, half_ref, swapped_ref,
        made, product, own, given, taken, sends, recvs, give_send, give_recv, carry_sems,
    ):
        blocks = Blocks(counts, made, held_ref, sends, recvs)
        narrow = lax.axis_index("narrow")
        core = narrow % 2
        partner = narrow + 1 - 2 * core
        greet_wide(counts, (partner, (narrow + 2) % 4))
        carry = carry_over(carried_ref, swapped_ref, carry_sems)
        carry.start()

        def make(who):
            made[who] = nt(
                middle_ref[...], weight_ref[pl.ds(pl.multiple_of(who * width, width), width), :]
            ).astype(low)

        def make_and_start(who):
            make(who)
            blocks.start(who)

        blocks.each(make_and_start)
        make(blocks.me)
        held_ref[blocks.me] = made[blocks.me]

        def give(w):
            return pltpu.make_async_remote_copy(
                src_ref=given.at[w], dst_ref=taken.at[w],
                send_sem=give_send.at[w], recv_sem=give_recv.at[w],
                device_id={"narrow": partner}, device_id_type=MESH,
            )

        def multiply(w, state):
            product[...] = tn(mixed_ref[w], middle_ref[...])
            for y in range(2):
                at = pl.multiple_of((2 * y + 1 - core) * strip, strip)
                given[w, y] = product[pl.ds(at, strip), :].astype(low)
                at = pl.multiple_of((2 * y + core) * strip, strip)
                own[w, y] = product[pl.ds(at, strip), :]
            give(w).start()
            return state

        def collect(w, state):
            give(w).wait_recv()
            for y in range(2):
                half_ref[y, w] = (own[w, y] + taken[w, y].astype(jnp.float32)).astype(low)
            return state

        lax.fori_loop(0, wide_count, multiply, 0)
        lax.fori_loop(0, wide_count, collect, 0)
        blocks.each(blocks.arrived)
        blocks.settle()
        lax.fori_loop(0, wide_count, lambda w, state: (give(w).wait_send(), state)[1], 0)
        carry.wait()

    held, half, swapped = pl.pallas_call(
        kernel,
        in_specs=[VMEM_SPEC] * 3 + [HBM_SPEC],
        out_specs=[VMEM_SPEC] * 2 + [HBM_SPEC],
        out_shape=[
            jax.ShapeDtypeStruct((wide_count, rows, width), low),
            jax.ShapeDtypeStruct((2, wide_count, strip, model), low),
            jax.ShapeDtypeStruct(carried.shape, low),
        ],
        scratch_shapes=[
            pltpu.VMEM((wide_count, rows, width), low),
            pltpu.VMEM((width, model), jnp.float32),
            pltpu.VMEM((wide_count, 2, strip, model), jnp.float32),
            pltpu.VMEM((wide_count, 2, strip, model), low),
            pltpu.VMEM((wide_count, 2, strip, model), low),
        ]
        + [pltpu.SemaphoreType.DMA((wide_count,))] * 4
        + [pltpu.SemaphoreType.DMA((2,))],
        compiler_params=pltpu.CompilerParams(
            collective_id=collective_id, has_side_effects=True, vmem_limit_bytes=48 << 20
        ),
        name="unmix",
    )(middle_low, output_full, mixed_blocks, carried)
    return (
        held.reshape(wide_count * rows, width),
        half.reshape(2, wide_count * strip, model),
        swapped,
    )


def return_and_project(
    grads, hidden_rows, query_turned, key_weight, value_weight, carried, counts, collective_id
):
    wide_count = counts[1]
    rows, columns = grads.shape[0] // wide_count, grads.shape[1]
    model = query_turned.shape[1]
    width = query_turned.shape[0] // wide_count
    head = (columns - width) // 2
    tile = min(512, model)
    slab = min(256, model // 2)
    per = model // 2 // slab
    low = jnp.bfloat16

    def kernel(
        grads_ref, hidden_ref, query_ref, key_ref, value_ref, carried_ref,
        out_ref, weight_ref, swapped_ref,
        held, slabs, query_all, key_all, value_all, given, taken, halves, whole,
        sends, recvs, slab_sems, give_send, give_recv, half_sems, carry_sems,
    ):
        blocks = Blocks(counts, grads_ref, held, sends, recvs)
        narrow = lax.axis_index("narrow")
        core = narrow % 2
        partner, across = narrow + 1 - 2 * core, (narrow + 2) % 4

        def row_of(t):
            return pl.multiple_of((jnp.where(t < per, 1 - core, core) * per + t % per) * slab, slab)

        def load(t):
            at = pl.ds(row_of(t), slab)
            return pltpu.make_async_copy(hidden_ref.at[:, :, at], slabs.at[t % 2], slab_sems.at[t % 2])

        load(0).start()
        greet_wide(counts, (partner, across))
        blocks.each(blocks.start)
        carry = carry_over(carried_ref, swapped_ref, carry_sems)
        held[blocks.me] = grads_ref[blocks.me]

        def give(n):
            return pltpu.make_async_remote_copy(
                src_ref=given.at[n], dst_ref=taken.at[n],
                send_sem=give_send.at[n], recv_sem=give_recv.at[n],
                device_id={"narrow": partner}, device_id_type=MESH,
            )

        exchange = pltpu.make_async_remote_copy(
            src_ref=halves.at[0], dst_ref=halves.at[1],
            send_sem=half_sems.at[0], recv_sem=half_sems.at[1],
            device_id={"narrow": across}, device_id_type=MESH,
        )
        hand_over = pltpu.make_async_remote_copy(
            src_ref=whole.at[core], dst_ref=whole.at[core],
            send_sem=half_sems.at[2], recv_sem=half_sems.at[3],
            device_id={"narrow": partner}, device_id_type=MESH,
        )

        def weigh(t, state):
            load(t).wait()

            @pl.when(t + 1 < 2 * per)
            def _():
                load(t + 1).start()

            value = tn(
                slabs[t % 2].reshape(wide_count * rows, slab),
                grads_ref[...].reshape(wide_count * rows, columns),
            )
            n = t % per

            @pl.when(t < per)
            def _():
                given[n] = value.astype(low)
                give(n).start()

            @pl.when(t >= per)
            def _():
                give(n).wait_recv()
                halves[0, n] = (value + taken[n].astype(jnp.float32)).astype(low)

            return state

        lax.fori_loop(0, 2 * per, weigh, 0)
        exchange.start()
        carry.start()
        blocks.each(blocks.arrived)
        exchange.wait()
        whole[core] = (halves[0].astype(jnp.float32) + halves[1].astype(jnp.float32)).astype(low)
        hand_over.start()
        for w in range(wide_count):
            query_all[:, w * width : (w + 1) * width] = held[w, :, :width]
        key_all[...] = jnp.concatenate(
            [held[w, :, width : width + head] for w in range(wide_count)], axis=1
        )
        value_all[...] = jnp.concatenate(
            [held[w, :, width + head :] for w in range(wide_count)], axis=1
        )

        def one(t, state):
            at = pl.ds(pl.multiple_of(t * tile, tile), tile)
            out_ref[:, at] = (
                jnp.dot(query_all[...], query_ref[:, at], preferred_element_type=jnp.float32)
                + nt(key_all[...], key_ref[at, :])
                + nt(value_all[...], value_ref[at, :])
            )
            return state

        lax.fori_loop(0, model // tile, one, 0)
        hand_over.wait()
        weight_ref[...] = whole[...].reshape(model, columns).astype(jnp.float32)
        blocks.settle()
        lax.fori_loop(0, per, lambda n, state: (give(n).wait_send(), state)[1], 0)
        carry.wait()

    return pl.pallas_call(
        kernel,
        in_specs=[VMEM_SPEC, HBM_SPEC] + [VMEM_SPEC] * 3 + [HBM_SPEC],
        out_specs=[VMEM_SPEC] * 2 + [HBM_SPEC],
        out_shape=[
            jax.ShapeDtypeStruct((rows, model), jnp.float32),
            jax.ShapeDtypeStruct((model, columns), jnp.float32),
            jax.ShapeDtypeStruct(carried.shape, low),
        ],
        scratch_shapes=[
            pltpu.VMEM((wide_count, rows, columns), low),
            pltpu.VMEM((2, wide_count, rows, slab), low),
            pltpu.VMEM((rows, wide_count * width), low),
            pltpu.VMEM((rows, wide_count * head), low),
            pltpu.VMEM((rows, wide_count * head), low),
            pltpu.VMEM((per, slab, columns), low),
            pltpu.VMEM((per, slab, columns), low),
            pltpu.VMEM((2, per, slab, columns), low),
            pltpu.VMEM((2, per, slab, columns), low),
            pltpu.SemaphoreType.DMA((wide_count,)),
            pltpu.SemaphoreType.DMA((wide_count,)),
            pltpu.SemaphoreType.DMA((2,)),
            pltpu.SemaphoreType.DMA((per,)),
            pltpu.SemaphoreType.DMA((per,)),
            pltpu.SemaphoreType.DMA((4,)),
            pltpu.SemaphoreType.DMA((2,)),
        ],
        compiler_params=pltpu.CompilerParams(
            collective_id=collective_id, has_side_effects=True, vmem_limit_bytes=48 << 20
        ),
        name="return_and_project",
    )(
        grads.reshape(wide_count, rows, columns),
        hidden_rows.reshape(wide_count, rows, model),
        query_turned, key_weight, value_weight,
        carried,
    )

CORPORA = 8
GATHER_BYTES = 8 << 20


def norm_scale(values, scale_gain):
    return (
        values * lax.rsqrt(jnp.mean(values * values, axis=-1, keepdims=True) + epsilon) * scale_gain
    )


def contract_first(left, right):
    return lax.dot_general(
        left, right, (((0,), (0,)), ((), ())), preferred_element_type=jnp.float32
    )


def gather_wide(values):
    return lax.all_gather(values, "wide", axis=0, tiled=True)


def scatter_wide(values):
    return lax.psum_scatter(
        values.astype(jnp.bfloat16), "wide", scatter_dimension=0, tiled=True
    ).astype(jnp.float32)


def own_part(values, axis, index, count):
    size = values.shape[axis] // count
    return lax.dynamic_slice_in_dim(values, index * size, size, axis)


def swap_narrow(values, bit):
    count = lax.axis_size("narrow")
    return lax.ppermute(values, "narrow", [(i, i ^ bit) for i in range(count)])


def keep_half(values, axis, bit):
    side = lax.axis_index("narrow") // bit % 2
    mine = lax.dynamic_index_in_dim(values, side, axis, keepdims=False)
    other = lax.dynamic_index_in_dim(values, 1 - side, axis, keepdims=False)
    return add_low(mine, swap_narrow(other, bit))


def add_low(left, right):
    return (left.astype(jnp.float32) + right.astype(jnp.float32)).astype(jnp.bfloat16)


def core_half(values):
    rows, columns = values.shape
    return keep_half(values.astype(jnp.bfloat16).reshape(2, rows // 2, columns), 0, 1)


def sum_narrow(values):
    half = core_half(values)
    return hand_back(add_low(half, swap_narrow(half, 2)))


def hand_back(half):
    other = swap_narrow(half, 1)
    first = lax.axis_index("narrow") % 2 == 0
    return jnp.concatenate(
        [jnp.where(first, half, other), jnp.where(first, other, half)], axis=0
    ).astype(jnp.float32)


def swiglu_back(act_grad, gate_values, up_values):
    sigmoid_gate = lax.logistic(gate_values)
    gate_part = act_grad * up_values * sigmoid_gate * (1.0 + gate_values * (1.0 - sigmoid_gate))
    up_part = act_grad * gate_values * sigmoid_gate
    return (gate_part.astype(jnp.bfloat16), up_part.astype(jnp.bfloat16))


def shards(
    tokens,
    attention_gain,
    query_weight,
    key_weight,
    value_weight,
    query_gain,
    key_gain,
    output_weight,
    feedforward_gain,
    gate_weight,
    up_weight,
    down_weight,
    cotangent,
    corpus_tags,
    segments,
):
    low, wide_type = jnp.bfloat16, jnp.float32
    head_size = query_gain.shape[0]
    own_rows, model_width = tokens.shape
    wide_count, narrow_count = lax.axis_size("wide"), lax.axis_size("narrow")
    counts = (narrow_count, wide_count)
    wide_index, narrow_index = lax.axis_index("wide"), lax.axis_index("narrow")
    key_total = key_weight.shape[1] // head_size
    width = query_weight.shape[1]
    key_head = wide_index * key_total // wide_count
    all_rows = own_rows * wide_count
    chained = wide_count == key_total and narrow_count == 4 and all_rows * model_width * 2 <= GATHER_BYTES

    tag_hits = corpus_tags[:, None] == jnp.arange(CORPORA, dtype=jnp.int32)[None, :]
    local_counts = jnp.sum(tag_hits.astype(wide_type), axis=0)
    local_counts = jnp.pad(local_counts[None], ((0, 7), (0, 128 - CORPORA)))
    token_values = tokens.astype(wide_type)
    first_gain = attention_gain.astype(wide_type)
    second_gain = feedforward_gain.astype(wide_type)

    key_columns = lax.dynamic_slice_in_dim(key_weight, key_head * head_size, head_size, 1)
    value_columns = lax.dynamic_slice_in_dim(value_weight, key_head * head_size, head_size, 1)
    own_weights = jnp.concatenate([query_weight, key_columns, value_columns], axis=1)
    strip = width // narrow_count
    strips = [
        own_part(output_weight, 0, narrow_index, narrow_count),
        jnp.transpose(own_part(query_weight, 1, narrow_index, narrow_count)),
    ]
    hidden_local = norm_scale(token_values, first_gain).astype(low)
    if chained:
        hidden_one, raw, corpus_counts, gathered = project_gathered(
            hidden_local, own_weights, local_counts, strips, counts, 2
        )
    else:
        hidden_one = gather_wide(hidden_local)
        raw = dot_nn(hidden_one, own_weights)
        corpus_counts = sum_everywhere(local_counts, counts, 1)
        gathered = [lax.all_gather(part, ("wide", "narrow"), axis=0, tiled=True) for part in strips]
    output_full, query_turned = gathered
    corpus_counts = corpus_counts[0, :CORPORA]
    corpus_scale = jnp.sqrt(jnp.sum(corpus_counts) / (CORPORA * corpus_counts))
    row_weight = jnp.sum(jnp.where(tag_hits, corpus_scale[None, :], 0.0), axis=1)
    out_cot = cotangent.astype(wide_type) * row_weight[:, None]
    cot_low, raw = lax.optimization_barrier((out_cot.astype(low), raw))
    cot_low = gather_wide(cot_low)

    first_block = first_blocks(segments)
    saved = attention_forward(raw, query_gain, key_gain, segments, first_block)
    if chained:
        branch, mixed = mix_and_project(saved[0], output_full, counts, 6)
        middle = token_values + branch
    else:
        mixed = lax.all_to_all(saved[0], "wide", split_axis=0, concat_axis=1, tiled=True)
        middle = token_values + dot_nn(mixed, output_full)

    together = lax.optimization_barrier
    hidden_two_local = norm_scale(middle, second_gain).astype(low)
    if chained:
        hidden_two, gate_values, up_values, activated, down_part = forward_gathered(
            hidden_two_local, gate_weight, up_weight, down_weight, wide_count, 3
        )
        hidden_two_grad, gate_half, up_half = backward_scattered(
            cot_low, gate_values, up_values, hidden_two, gate_weight, up_weight, down_weight,
            wide_count, 4,
        )
        down_part, hidden_two_grad = together((down_part, hidden_two_grad))
    else:
        hidden_two = gather_wide(hidden_two_local)
        gate_values = dot_nn(hidden_two, gate_weight)
        up_values = dot_nn(hidden_two, up_weight)
        activated = (gate_values * lax.logistic(gate_values) * up_values).astype(low)
        down_part = dot_nn(activated, down_weight)
        gate_low, up_low = swiglu_back(dot_nt(cot_low, down_weight), gate_values, up_values)
        hidden_two_grad = scatter_wide(dot_nt(gate_low, gate_weight) + dot_nt(up_low, up_weight))
        gate_half = core_half(contract_first(hidden_two, gate_low))
        up_half = core_half(contract_first(hidden_two, up_low))
        gate_other = swap_narrow(gate_half, 2)
    down_sum = scatter_wide(down_part)

    _, second_pull = jax.vjp(norm_scale, middle, second_gain)
    middle_part, second_gain_grad = second_pull(hidden_two_grad)
    middle_grad = out_cot + middle_part
    middle_low = middle_grad.astype(low)
    if chained:
        mixed_grad, output_part, gate_other = unmix(
            middle_low, output_full, mixed, gate_half, counts, 7
        )
    else:
        mixed_grad = lax.all_to_all(
            dot_nt(middle_low, output_full).astype(low), "wide", split_axis=1, concat_axis=0, tiled=True
        )
        mixed = mixed.reshape(own_rows, wide_count, narrow_count, strip).transpose(0, 2, 1, 3)
        output_part = contract_first(mixed.reshape(own_rows, wide_count * width), middle_low)
        output_part = output_part.astype(low).reshape(2, 2, wide_count * strip, model_width)
        output_part = keep_half(output_part, 1, 1)
    mixed_grad, output_part, activated, up_half = together(
        (mixed_grad, output_part, activated, up_half)
    )
    output_part = keep_half(output_part, 0, 2)
    down_half = core_half(contract_first(activated, cot_low))
    mixed_grad, down_half = together((mixed_grad, down_half))
    up_half = add_low(up_half, swap_narrow(up_half, 2))
    gate_grad = hand_back(add_low(gate_half, gate_other))
    grads, query_gain_grad, key_gain_grad = attention_backward(
        raw, query_gain, key_gain, segments, first_block, saved, mixed_grad
    )
    grads, output_part, up_half, gate_grad, down_sum = together(
        (grads, output_part, up_half, gate_grad, down_sum)
    )
    output_part = lax.psum_scatter(output_part, "wide", scatter_dimension=0, tiled=True)
    shared = wide_count // key_total
    if chained:
        hidden_one_grad, weight_sums, down_other = return_and_project(
            grads, hidden_one, query_turned, key_weight, value_weight, down_half, counts, 8
        )
    else:
        down_other = swap_narrow(down_half, 2)
        weight_grads = contract_first(hidden_one, grads)
        sent = lax.all_to_all(grads, "wide", split_axis=0, concat_axis=1, tiled=True).reshape(
            own_rows, wide_count, width + 2 * head_size
        )

        def key_side(start):
            part = sent[:, :, start : start + head_size]
            if shared > 1:
                part = jnp.sum(
                    part.astype(wide_type).reshape(own_rows, key_total, shared, head_size), axis=2
                ).astype(low)
            return part.reshape(own_rows, key_total * head_size)

        hidden_one_grad = (
            dot_nn(sent[:, :, :width].reshape(own_rows, wide_count * width), query_turned)
            + dot_nt(key_side(width), key_weight)
            + dot_nt(key_side(width + head_size), value_weight)
        )
    hidden_one_grad, output_part = together((hidden_one_grad, output_part))
    down_grad = hand_back(add_low(down_half, down_other))
    up_grad = hand_back(up_half)
    _, first_pull = jax.vjp(norm_scale, token_values, first_gain)
    token_part, first_gain_grad = first_pull(hidden_one_grad)
    tokens_gradient = (middle_grad + token_part).astype(low)
    tokens_gradient, down_sum = lax.optimization_barrier((tokens_gradient, down_sum))
    result = (middle + down_sum).astype(low)

    if shared == 1:
        if not chained:
            weight_sums = sum_narrow(weight_grads)
        key_weight_grad = weight_sums[:, width : width + head_size]
        value_weight_grad = weight_sums[:, width + head_size :]
    else:
        weight_sums = sum_narrow(weight_grads[:, :width])

        def spread(part):
            whole = jnp.zeros((model_width, key_total * head_size), wide_type)
            whole = lax.dynamic_update_slice_in_dim(whole, part, key_head * head_size, 1)
            share = lax.psum_scatter(whole.astype(low), "wide", scatter_dimension=1, tiled=True)
            return lax.psum(share, "narrow").astype(wide_type)

        key_weight_grad = spread(weight_grads[:, width : width + head_size])
        value_weight_grad = spread(weight_grads[:, width + head_size :])

    gain_parts = jnp.concatenate([first_gain_grad, second_gain_grad, query_gain_grad, key_gain_grad])
    lines = -(-gain_parts.shape[0] // 1024) * 8
    gain_parts = jnp.pad(gain_parts, (0, lines * 128 - gain_parts.shape[0])).reshape(lines, 128)
    gains, output_grad = sum_everywhere(gain_parts, counts, 5, output_part)
    gains, output_grad = gains.reshape(-1), output_grad.astype(wide_type)
    starts = (0, model_width, 2 * model_width, 2 * model_width + head_size)
    sizes = (model_width, model_width, head_size, head_size)
    first_out, second_out, query_gain_out, key_gain_out = (
        own_part(gains[start : start + size], 0, wide_index, wide_count)
        for start, size in zip(starts, sizes)
    )
    return (
        result,
        tokens_gradient,
        first_out,
        weight_sums[:, :width],
        key_weight_grad,
        value_weight_grad,
        query_gain_out,
        key_gain_out,
        output_grad,
        second_out,
        gate_grad,
        up_grad,
        down_grad,
    )


def solution(mesh):
    rows = P(("narrow", "wide"), None)
    columns, first = P(None, "wide"), P("wide", None)
    return jax.shard_map(
        shards,
        mesh=mesh,
        in_specs=(
            rows, P(), columns, P(), P(), P(), P(), first, P(), columns, columns, first,
            rows, P(("narrow", "wide")), P("narrow", None),
        ),
        out_specs=(
            rows, rows, P("wide"), columns, columns, columns, P("wide"), P("wide"),
            first, P("wide"), columns, columns, first,
        ),
        check_vma=False,
    )
```

```python
import numpy as np

import jax
import jax.numpy as jnp
from jax import lax
from jax.experimental import pallas as pl
from jax.experimental.pallas import tpu as pltpu
from jax.sharding import PartitionSpec as P

SEQ = 2048
epsilon = 1e-06
rope_base = 10000.0
BLOCK = 256
NEG = -1e30


def rope_tables(head_size):
    positions = np.arange(SEQ, dtype=np.float32)
    exponents = np.arange(head_size // 2, dtype=np.float32) * np.float32(2.0 / head_size)
    frequency = np.power(np.float32(rope_base), -exponents).astype(np.float32)
    angles = (positions[:, None] * frequency[None, :]).astype(np.float32)
    cosine, sine = np.cos(angles).astype(np.float32), np.sin(angles).astype(np.float32)
    return (
        np.concatenate([cosine, cosine], axis=1),
        np.concatenate([-sine, sine], axis=1),
    )


def dot_nn(left, right):
    return jnp.dot(left, right, preferred_element_type=jnp.float32)


def dot_nt(left, right):
    return lax.dot_general(
        left, right, (((1,), (1,)), ((), ())), preferred_element_type=jnp.float32
    )


def lane_ids(shape):
    return lax.broadcasted_iota(jnp.int32, shape, 1)


def group_ones(width, head_size):
    rows = lax.broadcasted_iota(jnp.int32, (width, width), 0) // head_size
    columns = lax.broadcasted_iota(jnp.int32, (width, width), 1) // head_size
    return jnp.where(rows == columns, 1.0, 0.0).astype(jnp.bfloat16)


def group_sum(values, ones):
    top = values.astype(jnp.bfloat16)
    rest = (values - top.astype(jnp.float32)).astype(jnp.bfloat16)
    return dot_nn(top, ones) + dot_nn(rest, ones)


def swap_halves(values, head_size):
    width, half = values.shape[1], head_size // 2
    if width == head_size:
        return jnp.concatenate([values[:, half:], values[:, :half]], axis=1)
    ahead = pltpu.roll(values, width - half, 1)
    behind = pltpu.roll(values, half, 1)
    return jnp.where(lane_ids(values.shape) % head_size < half, ahead, behind)


def tiled(values, count):
    return jnp.concatenate([values] * count, axis=1) if count > 1 else values


def split_raw(raw, width, head_size, heads):
    query = raw[:, :width]
    key = tiled(raw[:, width : width + head_size], heads)
    value = tiled(raw[:, width + head_size :], heads)
    return query, key, value


def head_masks(block, width, head_size, heads):
    group = lane_ids((block, width)) // head_size
    return [group == h for h in range(heads)]


def attention_forward(raw, query_gain, key_gain, segments, first_block):
    head_size = query_gain.shape[0]
    rows = raw.shape[0]
    heads = raw.shape[1] // head_size - 2
    width = heads * head_size
    seqs, blocks, block = rows // SEQ, SEQ // BLOCK, BLOCK
    scale = head_size ** (-0.5)

    def kernel(
        first_ref, raw_ref, qg_ref, kg_ref, cos_ref, sin_ref, segq_ref, segk_ref,
        mixed_ref, lse_ref, query_ref, key_ref, value_ref, keyt_ref,
        keys, values_t, masked, top, total, acc,
    ):
        s, i = pl.program_id(0), pl.program_id(1)
        cosine, sine = tiled(cos_ref[...], heads), tiled(sin_ref[...], heads)
        ones = group_ones(width, head_size)
        query, key, value = split_raw(raw_ref[...], width, head_size, heads)

        def norm_rope(x, gain):
            x = x * lax.rsqrt(group_sum(x * x, ones) * (1.0 / head_size) + epsilon) * gain
            return x * cosine + swap_halves(x, head_size) * sine

        query_low = norm_rope(query, qg_ref[...]).astype(jnp.bfloat16)
        key_rot = norm_rope(key, kg_ref[...])
        key_low = key_rot.astype(jnp.bfloat16)
        query_ref[...] = query_low
        key_ref[...] = key_low
        value_ref[...] = value.astype(jnp.bfloat16)
        keyt_ref[0] = jnp.transpose(key_rot)[:head_size].astype(jnp.bfloat16)
        keys[pl.ds(pl.multiple_of(i * block, block), block), :] = key_low
        values_t[i] = jnp.transpose(value)[:head_size].astype(jnp.bfloat16)
        scaled = query_low * jnp.bfloat16(scale)
        zero = jnp.zeros_like(scaled)
        for h, mask in enumerate(head_masks(block, width, head_size, heads)):
            masked[h] = jnp.where(mask, scaled, zero)
        top[...] = jnp.full_like(top, NEG)
        total[...] = jnp.zeros_like(total)
        acc[...] = jnp.zeros_like(acc)
        query_pos = i * block + lax.broadcasted_iota(jnp.int32, (block, block), 1)
        segment_query = segq_ref[0]

        def step(j, carry):
            at = pl.multiple_of(j * block, block)
            key_pos = at + lax.broadcasted_iota(jnp.int32, (block, block), 0)
            allowed = (key_pos <= query_pos) & (segk_ref[pl.ds(at, block), :] == segment_query)
            bias = jnp.where(allowed, 0.0, NEG)
            key_block = keys[pl.ds(at, block), :]
            value_t = values_t[j]
            for h in range(heads):
                scores = dot_nt(key_block, masked[h]) + bias
                before = top[h : h + 1, :]
                now = jnp.maximum(before, jnp.max(scores, axis=0, keepdims=True))
                shifted = jnp.exp(scores - now)
                fade = jnp.exp(before - now)
                top[h : h + 1, :] = now
                total[h : h + 1, :] = fade * total[h : h + 1, :] + jnp.sum(
                    shifted, axis=0, keepdims=True
                )
                span = slice(h * head_size, (h + 1) * head_size)
                acc[span, :] = fade * acc[span, :] + dot_nn(value_t, shifted.astype(jnp.bfloat16))
            return carry

        lax.fori_loop(first_ref[s, i], i + 1, step, 0)
        for h in range(heads):
            span = slice(h * head_size, (h + 1) * head_size)
            acc[span, :] = acc[span, :] / total[h : h + 1, :]
        mixed_ref[...] = jnp.transpose(acc[...]).astype(jnp.bfloat16)
        lse_ref[...] = top[...] + jnp.log(jnp.maximum(total[...], 1e-30))

    cosine, sine = rope_tables(head_size)
    at_rows = lambda s, i, first: (s * blocks + i, 0)
    fixed = lambda s, i, first: (0, 0)
    at_lanes = lambda s, i, first: (0, s * blocks + i)
    low = jnp.bfloat16
    pairs = blocks * (blocks + 1) // 2 * seqs * heads
    return pl.pallas_call(
        kernel,
        grid_spec=pltpu.PrefetchScalarGridSpec(
            num_scalar_prefetch=1,
            grid=(seqs, blocks),
            in_specs=[
                pl.BlockSpec((block, raw.shape[1]), at_rows),
                pl.BlockSpec((1, width), fixed),
                pl.BlockSpec((1, width), fixed),
                pl.BlockSpec((block, head_size), lambda s, i, first: (i, 0)),
                pl.BlockSpec((block, head_size), lambda s, i, first: (i, 0)),
                pl.BlockSpec((1, 1, block), lambda s, i, first: (s, 0, i)),
                pl.BlockSpec((SEQ, 1), lambda s, i, first: (s, 0)),
            ],
            out_specs=[
                pl.BlockSpec((block, width), at_rows),
                pl.BlockSpec((8, block), at_lanes),
                pl.BlockSpec((block, width), at_rows),
                pl.BlockSpec((block, width), at_rows),
                pl.BlockSpec((block, width), at_rows),
                pl.BlockSpec((1, head_size, block), lambda s, i, first: (s * blocks + i, 0, 0)),
            ],
            scratch_shapes=[
                pltpu.VMEM((SEQ, width), low),
                pltpu.VMEM((blocks, head_size, block), low),
                pltpu.VMEM((heads, block, width), low),
                pltpu.VMEM((8, block), jnp.float32),
                pltpu.VMEM((8, block), jnp.float32),
                pltpu.VMEM((width, block), jnp.float32),
            ],
        ),
        out_shape=[
            jax.ShapeDtypeStruct((rows, width), low),
            jax.ShapeDtypeStruct((8, rows), jnp.float32),
            jax.ShapeDtypeStruct((rows, width), low),
            jax.ShapeDtypeStruct((rows, width), low),
            jax.ShapeDtypeStruct((rows, width), low),
            jax.ShapeDtypeStruct((rows // block, head_size, block), low),
        ],
        compiler_params=pltpu.CompilerParams(vmem_limit_bytes=40 << 20),
        cost_estimate=pl.CostEstimate(flops=0, bytes_accessed=0, transcendentals=0),
        name="attention_forward",
    )(
        first_block, raw,
        tiled(query_gain.astype(jnp.float32)[None], heads),
        tiled(key_gain.astype(jnp.float32)[None], heads),
        cosine, sine, segments[:, None, :], segments.reshape(rows, 1),
    )


def attention_backward(
    raw, query_gain, key_gain, segments, first_block, saved, mixed_grad
):
    mixed, lse, query_low, key_low, value_low, key_t = saved
    head_size = query_gain.shape[0]
    rows, width = mixed.shape
    heads = width // head_size
    seqs, blocks, block = rows // SEQ, SEQ // BLOCK, BLOCK
    scale = head_size ** (-0.5)

    def kernel(
        first_ref, raw_ref, qg_ref, kg_ref, cos_ref, sin_ref, segq_ref, segk_ref,
        mixed_ref, lse_ref, query_ref, grad_ref, keys_ref, values_ref, keyt_ref,
        out_ref, qgg_ref, kgg_ref,
        masked, masked_grad, key_sums, value_sums, query_sums, deltas,
    ):
        s, i = pl.program_id(0), blocks - 1 - pl.program_id(1)

        @pl.when(pl.program_id(1) == 0)
        def _():
            key_sums[...] = jnp.zeros_like(key_sums)
            value_sums[...] = jnp.zeros_like(value_sums)

        @pl.when((pl.program_id(1) == 0) & (s == 0))
        def _():
            qgg_ref[...] = jnp.zeros_like(qgg_ref)
            kgg_ref[...] = jnp.zeros_like(kgg_ref)

        query_sums[...] = jnp.zeros_like(query_sums)
        grad = grad_ref[...]
        scaled = query_ref[...] * jnp.bfloat16(scale)
        zero = jnp.zeros_like(scaled)
        for h, mask in enumerate(head_masks(block, width, head_size, heads)):
            span = slice(h * block, (h + 1) * block)
            masked[span, :] = jnp.where(mask, scaled, zero)
            masked_grad[span, :] = jnp.where(mask, grad, zero)
        product = jnp.transpose(grad.astype(jnp.float32) * mixed_ref[...].astype(jnp.float32))
        for h in range(heads):
            deltas[h : h + 1, :] = jnp.sum(
                product[h * head_size : (h + 1) * head_size], axis=0, keepdims=True
            )
        query_pos = i * block + lax.broadcasted_iota(jnp.int32, (block, block), 1)
        segment_query = segq_ref[0]

        def step(j, carry):
            at = pl.multiple_of(j * block, block)
            key_pos = at + lax.broadcasted_iota(jnp.int32, (block, block), 0)
            allowed = (key_pos <= query_pos) & (segk_ref[pl.ds(at, block), :] == segment_query)
            bias = jnp.where(allowed, 0.0, NEG)
            key_block = keys_ref[pl.ds(at, block), :]
            value_block = values_ref[pl.ds(at, block), :]
            key_t = keyt_ref[j]
            lows, grads = [], []
            for h in range(heads):
                span = slice(h * block, (h + 1) * block)
                scores = dot_nt(key_block, masked[span, :]) + bias
                probability = jnp.exp(scores - lse_ref[h : h + 1, :])
                prob_grad = dot_nt(value_block, masked_grad[span, :])
                score_grad = (probability * (prob_grad - deltas[h : h + 1, :])).astype(jnp.bfloat16)
                lows.append(probability.astype(jnp.bfloat16))
                grads.append(score_grad)
                rows_h = slice(h * head_size, (h + 1) * head_size)
                query_sums[rows_h, :] += dot_nn(key_t, score_grad)
            value_sums[pl.ds(at, block), :] += dot_nn(
                jnp.concatenate(lows, axis=1), masked_grad[...]
            )
            key_sums[pl.ds(at, block), :] += dot_nn(jnp.concatenate(grads, axis=1), masked[...])
            return carry

        lax.fori_loop(first_ref[s, i], i + 1, step, 0)
        cosine, sine = tiled(cos_ref[...], heads), tiled(sin_ref[...], heads)
        ones = group_ones(width, head_size)
        query, key, _ = split_raw(raw_ref[...], width, head_size, heads)

        def all_heads(x):
            total = x
            for h in range(1, heads):
                total = total + pltpu.roll(x, h * head_size, 1)
            return total

        def norm_rope_back(x, up, gain):
            unrot = up * cosine - swap_halves(up, head_size) * sine
            inverse = lax.rsqrt(group_sum(x * x, ones) * (1.0 / head_size) + epsilon)
            gain_part = jnp.sum(unrot * x * inverse, axis=0, keepdims=True)
            scaled_up = unrot * gain
            mean = group_sum(scaled_up * x, ones) * (1.0 / head_size)
            return scaled_up * inverse - x * (mean * inverse * inverse * inverse), gain_part

        query_up = jnp.transpose(query_sums[...]) * scale
        query_grad, query_part = norm_rope_back(query, query_up, qg_ref[...])
        here = pl.ds(pl.multiple_of(i * block, block), block)
        key_up = all_heads(key_sums[here, :])
        key_grad, key_part = norm_rope_back(key, key_up, kg_ref[...])
        value_grad = all_heads(value_sums[here, :])
        out_ref[...] = jnp.concatenate(
            [query_grad, key_grad[:, :head_size], value_grad[:, :head_size]], axis=1
        ).astype(jnp.bfloat16)
        qgg_ref[...] += query_part
        kgg_ref[...] += key_part

    cosine, sine = rope_tables(head_size)
    at_rows = lambda s, i, first: (s * blocks + blocks - 1 - i, 0)
    fixed = lambda s, i, first: (0, 0)
    at_lanes = lambda s, i, first: (0, s * blocks + blocks - 1 - i)
    at_seq = lambda s, i, first: (s, 0)
    low = jnp.bfloat16
    pairs = blocks * (blocks + 1) // 2 * seqs * heads
    grads, query_part, key_part = pl.pallas_call(
        kernel,
        grid_spec=pltpu.PrefetchScalarGridSpec(
            num_scalar_prefetch=1,
            grid=(seqs, blocks),
            in_specs=[
                pl.BlockSpec((block, raw.shape[1]), at_rows),
                pl.BlockSpec((1, width), fixed),
                pl.BlockSpec((1, width), fixed),
                pl.BlockSpec((block, head_size), lambda s, i, first: (blocks - 1 - i, 0)),
                pl.BlockSpec((block, head_size), lambda s, i, first: (blocks - 1 - i, 0)),
                pl.BlockSpec((1, 1, block), lambda s, i, first: (s, 0, blocks - 1 - i)),
                pl.BlockSpec((SEQ, 1), at_seq),
                pl.BlockSpec((block, width), at_rows),
                pl.BlockSpec((8, block), at_lanes),
                pl.BlockSpec((block, width), at_rows),
                pl.BlockSpec((block, width), at_rows),
                pl.BlockSpec((SEQ, width), at_seq),
                pl.BlockSpec((SEQ, width), at_seq),
                pl.BlockSpec((blocks, head_size, block), lambda s, i, first: (s, 0, 0)),
            ],
            out_specs=[
                pl.BlockSpec((block, raw.shape[1]), at_rows),
                pl.BlockSpec((1, width), fixed),
                pl.BlockSpec((1, width), fixed),
            ],
            scratch_shapes=[
                pltpu.VMEM((heads * block, width), low),
                pltpu.VMEM((heads * block, width), low),
                pltpu.VMEM((SEQ, width), jnp.float32),
                pltpu.VMEM((SEQ, width), jnp.float32),
                pltpu.VMEM((width, block), jnp.float32),
                pltpu.VMEM((8, block), jnp.float32),
            ],
        ),
        out_shape=[
            jax.ShapeDtypeStruct(raw.shape, low),
            jax.ShapeDtypeStruct((1, width), jnp.float32),
            jax.ShapeDtypeStruct((1, width), jnp.float32),
        ],
        compiler_params=pltpu.CompilerParams(vmem_limit_bytes=48 << 20),
        cost_estimate=pl.CostEstimate(flops=0, bytes_accessed=0, transcendentals=0),
        name="attention_backward",
    )(
        first_block, raw,
        tiled(query_gain.astype(jnp.float32)[None], heads),
        tiled(key_gain.astype(jnp.float32)[None], heads),
        cosine, sine, segments[:, None, :], segments.reshape(rows, 1),
        mixed, lse, query_low, mixed_grad, key_low, value_low, key_t,
    )
    return (
        grads,
        jnp.sum(query_part.reshape(heads, head_size), axis=0),
        key_part[0, :head_size],
    )


def first_blocks(segments):
    starts = segments[:, :: BLOCK]
    below = jnp.sum(segments[:, None, :] < starts[:, :, None], axis=-1, dtype=jnp.int32)
    return below // BLOCK

MESH = pl.DeviceIdType.MESH


class Lattice:
    def __init__(self, count):
        self.depth = count // 2
        me = lax.axis_index("wide")
        self.z, self.x = me // 2, me % 2
        self.below = jnp.minimum(self.z, self.depth - 1 - self.z)
        self.low_side = self.z > self.depth - 1 - self.z

    def at(self, z, x):
        return z * 2 + x

    def order(self, m):
        near = m <= 2 * self.below
        r = jnp.where(near, (m + 1) // 2, m - self.below)
        minus = jnp.where(near, m % 2 == 1, self.low_side)
        return jnp.where(minus, self.z - r, self.z + r), r


def greet(lat, partners=()):
    barrier = pltpu.get_barrier_semaphore()
    last = lat.depth - 1
    for partner in partners:
        pl.semaphore_signal(
            barrier, inc=1, device_id={"narrow": partner}, device_id_type=MESH
        )

    def each(act):
        act(lat.at(lat.z, 1 - lat.x))

        @pl.when(lat.z > 0)
        def _():
            act(lat.at(lat.z - 1, lat.x))

        @pl.when(lat.z < last)
        def _():
            act(lat.at(lat.z + 1, lat.x))

    each(lambda who: pl.semaphore_signal(barrier, inc=1, device_id={"wide": who}, device_id_type=MESH))
    own = 1 + len(partners)
    pl.semaphore_wait(barrier, own + jnp.minimum(lat.z, 1) + jnp.minimum(last - lat.z, 1))


def gather_chunks(lat, buffers, send_sems, recv_sems, compute, meanwhile=None, landed=None):
    z, x, depth = lat.z, lat.x, lat.depth
    last = depth - 1
    every = range(len(buffers))

    def copy(k, chunk, way, slot, target):
        return pltpu.make_async_remote_copy(
            src_ref=buffers[k].at[chunk], dst_ref=buffers[k].at[chunk],
            send_sem=send_sems.at[k, way, slot], recv_sem=recv_sems.at[k, chunk],
            device_id={"wide": target}, device_id_type=MESH,
        )

    def up(k, zz):
        return copy(k, lat.at(zz, x), 0, zz, lat.at(z + 1, x))

    def down(k, zz):
        return copy(k, lat.at(zz, x), 1, zz, lat.at(z - 1, x))

    def across(k, zz):
        return copy(k, lat.at(zz, x), 2, zz, lat.at(z, 1 - x))

    def arrived(k, chunk):
        copy(k, chunk, 2, 0, lat.at(z, 1 - x)).wait_recv()
        if landed is not None:
            landed(k, chunk)

    for k in every:
        @pl.when(z < last)
        def _():
            up(k, z).start()

        @pl.when(z > 0)
        def _():
            down(k, z).start()

        across(k, z).start()
    if meanwhile is not None:
        meanwhile()

    def step(m, carry):
        zz, r = lat.order(m)
        _, before = lat.order(m - 1)

        @pl.when((m >= 1) & (m < depth) & (r != before))
        def _():
            for k in every:
                @pl.when(z - r >= 0)
                def _():
                    arrived(k, lat.at(z - r, x))

                    @pl.when(z < last)
                    def _():
                        up(k, z - r).start()

                    across(k, z - r).start()

                @pl.when(z + r <= last)
                def _():
                    arrived(k, lat.at(z + r, x))

                    @pl.when(z > 0)
                    def _():
                        down(k, z + r).start()

                    across(k, z + r).start()

        mirror = lat.order(jnp.maximum(m - 1, 0))[0]

        def part(p, carry):
            @pl.when((p == 1) & (m >= 1))
            def _():
                for k in every:
                    arrived(k, lat.at(mirror, 1 - x))

            @pl.when(((p == 0) & (m < depth)) | ((p == 1) & (m >= 1)))
            def _():
                compute(jnp.where(p == 0, lat.at(zz, x), lat.at(mirror, 1 - x)))

            return carry

        return lax.fori_loop(0, 2, part, carry)

    lax.fori_loop(0, depth + 1, step, 0)

    def settle(zz, carry):
        for k in every:
            @pl.when((z < last) & (zz <= z))
            def _():
                up(k, zz).wait_send()

            @pl.when((z > 0) & (zz >= z))
            def _():
                down(k, zz).wait_send()

            across(k, zz).wait_send()
        return carry

    lax.fori_loop(0, depth, settle, 0)


def project_gathered(local, weights, values, strips, counts, collective_id):
    rows, model = local.shape
    columns = weights.shape[1]
    narrow_count, wide_count = counts
    depth = wide_count // 2
    strip = strips[0].shape[0]
    tall = strip * len(strips)

    def kernel(
        local_ref, weights_ref, values_ref, *refs
    ):
        strip_refs, refs = refs[: len(strips)], refs[len(strips) :]
        full_ref, out_ref, sum_ref, refs = refs[0], refs[1], refs[2], refs[3:]
        spread_refs, refs = refs[: len(strips)], refs[len(strips) :]
        (full, spread, send_sems, recv_sems, own_sems, store_sems, spread_sems, y_send, core_send, spread_recv,
         mine, held, total, load_sem, *sems) = refs
        lat = Lattice(wide_count)
        me = lat.at(lat.z, lat.x)
        narrow_me = lax.axis_index("narrow")
        core_side, y_side = narrow_me + 1 - 2 * (narrow_me % 2), (narrow_me + 2) % 4
        corner = y_side + 1 - 2 * (y_side % 2)
        loads = [
            pltpu.make_async_copy(local_ref, full.at[me], own_sems.at[0]),
            pltpu.make_async_copy(values_ref, mine, load_sem),
        ] + [
            pltpu.make_async_copy(
                ref, spread.at[narrow_me, me, pl.ds(k * strip, strip)], own_sems.at[1 + k]
            )
            for k, ref in enumerate(strip_refs)
        ]
        for load in loads:
            load.start()
        arrive = greet_all(counts)
        for load in loads:
            load.wait()
        arrive()
        narrow, wide = exchange_pair(counts, mine, held, total, *sems)

        def to_side(n, chunk, target, send_sem):
            return pltpu.make_async_remote_copy(
                src_ref=spread.at[n, chunk], dst_ref=spread.at[n, chunk],
                send_sem=send_sem, recv_sem=spread_recv.at[n, chunk],
                device_id={"narrow": target}, device_id_type=MESH,
            )

        def to_y(chunk):
            return to_side(narrow_me, chunk, y_side, y_send.at[chunk])

        def to_core(n, chunk):
            return to_side(n, chunk, core_side, core_send.at[n // 2, chunk])

        def spread_out(chunk):
            to_y(chunk).start()
            to_core(narrow_me, chunk).start()

        def landed(k, chunk):
            if k == 0:
                spread_out(chunk)

        def meanwhile():
            spread_out(me)
            narrow.start()
            total[...] = narrow.total()
            wide.start()

        def keep(chunk):
            return pltpu.make_async_copy(full.at[chunk], full_ref.at[chunk], store_sems.at[chunk])

        def keep_strip(n, chunk, k):
            return pltpu.make_async_copy(
                spread.at[n, chunk, pl.ds(k * strip, strip)], spread_refs[k].at[chunk, n],
                spread_sems.at[k, n, chunk],
            )

        def keep_strips(n, chunk):
            for k in range(len(strips)):
                keep_strip(n, chunk, k).start()

        def compute(chunk):
            keep(chunk).start()
            keep_strips(narrow_me, chunk)
            at = pl.multiple_of(chunk * rows, rows)
            out_ref[pl.ds(at, rows), :] = jnp.dot(
                full[chunk], weights_ref[...], preferred_element_type=jnp.float32
            )

        gather_chunks(
            lat, [spread.at[narrow_me], full], send_sems, recv_sems, compute, meanwhile, landed
        )

        def event(e):
            zz = lat.order(e // 2)[0]
            return lat.at(zz, jnp.where(e % 2 == 0, lat.x, 1 - lat.x))

        def pass_on(e, carry):
            chunk = event(e)
            to_side(y_side, chunk, y_side, y_send.at[chunk]).wait_recv()
            to_core(y_side, chunk).start()
            keep_strips(y_side, chunk)
            return carry

        def take(e, carry):
            chunk = event(e)
            for n in (core_side, corner):
                to_side(n, chunk, core_side, core_send.at[0, chunk]).wait_recv()
                keep_strips(n, chunk)
            return carry

        lax.fori_loop(0, wide_count, pass_on, 0)
        lax.fori_loop(0, wide_count, take, 0)
        sum_ref[...] = wide.total()
        narrow.settle()
        wide.settle()

        def settle(c, carry):
            keep(c).wait()
            to_y(c).wait_send()
            to_core(narrow_me, c).wait_send()
            to_core(y_side, c).wait_send()
            for k in range(len(strips)):
                for n in range(narrow_count):
                    keep_strip(n, c, k).wait()
            return carry

        lax.fori_loop(0, wide_count, settle, 0)

    vmem = pl.BlockSpec(memory_space=pltpu.VMEM)
    hbm = pl.BlockSpec(memory_space=pl.ANY)
    low = local.dtype
    full, out, sums, *gathered = pl.pallas_call(
        kernel,
        in_specs=[hbm, vmem, hbm] + [hbm] * len(strips),
        out_specs=[hbm, vmem, vmem] + [hbm] * len(strips),
        out_shape=[
            jax.ShapeDtypeStruct((wide_count, rows, model), low),
            jax.ShapeDtypeStruct((wide_count * rows, columns), jnp.float32),
            jax.ShapeDtypeStruct(values.shape, jnp.float32),
        ]
        + [jax.ShapeDtypeStruct((wide_count, narrow_count, strip, model), low)] * len(strips),
        scratch_shapes=[
            pltpu.VMEM((wide_count, rows, model), low),
            pltpu.VMEM((narrow_count, wide_count, tall, model), low),
            pltpu.SemaphoreType.DMA((2, 3, depth)),
            pltpu.SemaphoreType.DMA((2, wide_count)),
            pltpu.SemaphoreType.DMA((1 + len(strips),)),
            pltpu.SemaphoreType.DMA((wide_count,)),
            pltpu.SemaphoreType.DMA((len(strips), narrow_count, wide_count)),
            pltpu.SemaphoreType.DMA((wide_count,)),
            pltpu.SemaphoreType.DMA((2, wide_count)),
            pltpu.SemaphoreType.DMA((narrow_count, wide_count)),
        ]
        + exchange_scratch(values.shape, counts),
        compiler_params=pltpu.CompilerParams(
            collective_id=collective_id, has_side_effects=True, vmem_limit_bytes=48 << 20
        ),
        name="project_gathered",
    )(local, weights, values, *strips)
    flat = narrow_count * wide_count * strip
    return full.reshape(wide_count * rows, model), out, sums, [g.reshape(flat, model) for g in gathered]


def nt(left, right):
    return lax.dot_general(
        left, right, (((1,), (1,)), ((), ())), preferred_element_type=jnp.float32
    )


def forward_gathered(local, gate_weight, up_weight, down_weight, wide_count, collective_id):
    rows, model = local.shape
    hidden = gate_weight.shape[1]
    depth = wide_count // 2
    tile = min(256, hidden)
    wide_tile = min(512, model)

    def kernel(
        local_ref, gate_ref, up_ref, down_ref, full_ref, gates_ref, ups_ref, acts_ref, downs_ref,
        full, gates, ups, acts, downs, send_sems, recv_sems, load_sem, store_sems,
    ):
        lat = Lattice(wide_count)
        me = lat.at(lat.z, lat.x)
        load = pltpu.make_async_copy(local_ref, full.at[me], load_sem)
        load.start()
        greet(lat)
        load.wait()
        kept = ((full, full_ref), (gates, gates_ref), (ups, ups_ref), (acts, acts_ref), (downs, downs_ref))

        def keep(which, chunk):
            source, target = kept[which]
            return pltpu.make_async_copy(source.at[chunk], target.at[chunk], store_sems.at[which, chunk])

        def compute(chunk):
            keep(0, chunk).start()
            rows_in = full[chunk]

            def inner(t, carry):
                at = pl.ds(pl.multiple_of(t * tile, tile), tile)
                gate = jnp.dot(rows_in, gate_ref[:, at], preferred_element_type=jnp.float32)
                up = jnp.dot(rows_in, up_ref[:, at], preferred_element_type=jnp.float32)
                gates[chunk, :, at] = gate
                ups[chunk, :, at] = up
                acts[chunk, :, at] = (gate * lax.logistic(gate) * up).astype(jnp.bfloat16)
                return carry

            lax.fori_loop(0, hidden // tile, inner, 0)
            for which in (1, 2, 3):
                keep(which, chunk).start()
            act = acts[chunk]

            def outer(t, carry):
                at = pl.ds(pl.multiple_of(t * wide_tile, wide_tile), wide_tile)
                downs[chunk, :, at] = jnp.dot(
                    act, down_ref[:, at], preferred_element_type=jnp.float32
                ).astype(jnp.bfloat16)
                return carry

            lax.fori_loop(0, model // wide_tile, outer, 0)
            keep(4, chunk).start()

        gather_chunks(lat, [full], send_sems, recv_sems, compute)
        for which in range(5):
            lax.fori_loop(0, wide_count, lambda c, carry: (keep(which, c).wait(), carry)[1], 0)

    low = jnp.bfloat16
    outs = [
        ((wide_count, rows, model), low),
        ((wide_count, rows, hidden), jnp.float32),
        ((wide_count, rows, hidden), jnp.float32),
        ((wide_count, rows, hidden), low),
        ((wide_count, rows, model), low),
    ]
    vmem = pl.BlockSpec(memory_space=pltpu.VMEM)
    hbm = pl.BlockSpec(memory_space=pl.ANY)
    results = pl.pallas_call(
        kernel,
        in_specs=[hbm, vmem, vmem, vmem],
        out_specs=[hbm] * 5,
        out_shape=[jax.ShapeDtypeStruct(*o) for o in outs],
        scratch_shapes=[pltpu.VMEM(*o) for o in outs]
        + [
            pltpu.SemaphoreType.DMA((1, 3, depth)),
            pltpu.SemaphoreType.DMA((1, wide_count)),
            pltpu.SemaphoreType.DMA,
            pltpu.SemaphoreType.DMA((5, wide_count)),
        ],
        compiler_params=pltpu.CompilerParams(
            collective_id=collective_id, has_side_effects=True, vmem_limit_bytes=60 << 20
        ),
        name="forward_gathered",
    )(local, gate_weight, up_weight, down_weight)
    return [r.reshape(wide_count * rows, r.shape[2]) for r in results]


def tn(left, right):
    return lax.dot_general(
        left, right, (((0,), (0,)), ((), ())), preferred_element_type=jnp.float32
    )


def backward_scattered(
    cot, gates, ups, hidden_rows, gate_weight, up_weight, down_weight, wide_count, collective_id
):
    model = cot.shape[1]
    rows = cot.shape[0] // wide_count
    hidden = gate_weight.shape[1]
    depth = wide_count // 2
    tile = min(256, hidden)
    wide_tile = min(512, model)
    low = jnp.bfloat16

    half = model // 2
    slab = min(256, half)
    per = half // slab

    def kernel(
        cot_ref, gates_ref, ups_ref, hidden_ref, gate_ref, up_ref, down_ref,
        sum_ref, gate_half_ref, up_half_ref,
        cots, gate_in, up_in, gate_low, up_low, foreign, own, crossed, from_low, from_high,
        columns, given, taken, kept,
        in_sems, cross_send, cross_recv, chain_send, low_recv, high_recv,
        column_sems, give_send, give_recv, kept_sems,
    ):
        lat = Lattice(wide_count)
        z, x, last = lat.z, lat.x, depth - 1
        narrow = lax.axis_index("narrow")
        core = narrow % 2
        partner = narrow + 1 - 2 * core

        def place(e):
            zz = lat.order(depth - 1 - e % depth)[0]
            return zz, lat.at(zz, jnp.where(e < depth, 1 - x, x))

        def loads(e):
            slot = e % 2
            chunk = place(e)[1]
            return [
                pltpu.make_async_copy(source.at[chunk], target.at[slot], in_sems.at[k, slot])
                for k, (source, target) in enumerate(
                    ((cot_ref, cots), (gates_ref, gate_in), (ups_ref, up_in))
                )
            ]

        def cross(zz):
            return pltpu.make_async_remote_copy(
                src_ref=foreign.at[zz], dst_ref=crossed.at[zz],
                send_sem=cross_send.at[zz], recv_sem=cross_recv.at[zz],
                device_id={"wide": lat.at(z, 1 - x)}, device_id_type=MESH,
            )

        def rise(zz):
            return pltpu.make_async_remote_copy(
                src_ref=own.at[zz], dst_ref=from_low.at[zz],
                send_sem=chain_send.at[zz], recv_sem=low_recv.at[zz],
                device_id={"wide": lat.at(z + 1, x)}, device_id_type=MESH,
            )

        def sink(zz):
            return pltpu.make_async_remote_copy(
                src_ref=own.at[zz], dst_ref=from_high.at[zz],
                send_sem=chain_send.at[zz], recv_sem=high_recv.at[zz],
                device_id={"wide": lat.at(z - 1, x)}, device_id_type=MESH,
            )

        def slab_of(e):
            side = jnp.where(e < 2 * per, 1 - core, core)
            return e // per % 2, e % per, side * per + e % per

        def column_load(e):
            at = pl.ds(pl.multiple_of(slab_of(e)[2] * slab, slab), slab)
            return pltpu.make_async_copy(
                hidden_ref.at[:, :, at], columns.at[e % 2], column_sems.at[e % 2]
            )

        def give(e):
            which, n, _ = slab_of(e)
            return pltpu.make_async_remote_copy(
                src_ref=given.at[e % 2], dst_ref=taken.at[which, n],
                send_sem=give_send.at[e % 2], recv_sem=give_recv.at[which, n],
                device_id={"narrow": partner}, device_id_type=MESH,
            )

        def keep(e, k):
            target = (gate_half_ref, up_half_ref)[k]
            return pltpu.make_async_copy(kept.at[e % 2], target.at[slab_of(e)[1]], kept_sems.at[e % 2])

        def weight_slab(e):
            which, n, _ = slab_of(e)
            column_load(e).wait()

            @pl.when(e + 1 < 4 * per)
            def _():
                column_load(e + 1).start()

            tokens = columns[e % 2].reshape(wide_count * rows, slab)

            @pl.when((e >= 2) & (e < 2 * per + 2))
            def _():
                give(e - 2).wait_send()

            @pl.when(e >= 2 * per + 2)
            def _():
                keep(e - 2, 0).wait()

            def product(k):
                source = (gate_low, up_low)[k]
                value = tn(tokens, source[...].reshape(wide_count * rows, hidden))

                @pl.when(e < 2 * per)
                def _():
                    given[e % 2] = value.astype(low)
                    give(e).start()

                @pl.when(e >= 2 * per)
                def _():
                    give(e).wait_recv()
                    kept[e % 2] = (value + taken[k, n].astype(jnp.float32)).astype(low)
                    keep(e, k).start()

            @pl.when(which == 0)
            def _():
                product(0)

            @pl.when(which == 1)
            def _():
                product(1)

        for copy in loads(0):
            copy.start()
        column_load(0).start()
        greet(lat, (partner,))

        def partial(e, target, zz):
            slot = e % 2
            for copy in loads(e):
                copy.wait()

            @pl.when(e + 1 < 2 * depth)
            def _():
                for copy in loads(e + 1):
                    copy.start()

            cot_rows = cots[slot]
            chunk = place(e)[1]

            def inner(t, carry):
                at = pl.ds(pl.multiple_of(t * tile, tile), tile)
                act_grad = nt(cot_rows, down_ref[at, :])
                gate, up = gate_in[slot, :, at], up_in[slot, :, at]
                sigmoid = lax.logistic(gate)
                gate_low[chunk, :, at] = (
                    act_grad * up * sigmoid * (1.0 + gate * (1.0 - sigmoid))
                ).astype(low)
                up_low[chunk, :, at] = (act_grad * gate * sigmoid).astype(low)
                return carry

            lax.fori_loop(0, hidden // tile, inner, 0)
            gate_rows, up_rows = gate_low[chunk], up_low[chunk]

            def outer(t, carry):
                at = pl.ds(pl.multiple_of(t * wide_tile, wide_tile), wide_tile)
                target[zz, :, at] = (
                    nt(gate_rows, gate_ref[at, :]) + nt(up_rows, up_ref[at, :])
                ).astype(low)
                return carry

            lax.fori_loop(0, model // wide_tile, outer, 0)

        def send_step(e, carry):
            zz, _ = place(e)
            partial(e, foreign, zz)
            cross(zz).start()
            return carry

        lax.fori_loop(0, depth, send_step, 0)

        def own_step(e, carry):
            zz, _ = place(e)
            partial(e, own, zz)

            @pl.when(e == depth)
            def _():
                chain(zz)

            return carry

        def chain(zz):
            cross(zz).wait_recv()
            wide = jnp.float32

            @pl.when((zz > z) & (z > 0))
            def _():
                rise(zz).wait_recv()
                own[zz] = (own[zz].astype(wide) + crossed[zz].astype(wide) + from_low[zz].astype(wide)).astype(low)

            @pl.when((zz < z) & (z < last))
            def _():
                sink(zz).wait_recv()
                own[zz] = (own[zz].astype(wide) + crossed[zz].astype(wide) + from_high[zz].astype(wide)).astype(low)

            @pl.when(((zz > z) & (z == 0)) | ((zz < z) & (z == last)))
            def _():
                own[zz] = (own[zz].astype(wide) + crossed[zz].astype(wide)).astype(low)

            @pl.when(zz > z)
            def _():
                rise(zz).start()

            @pl.when(zz < z)
            def _():
                sink(zz).start()

            @pl.when(zz == z)
            def _():
                sum_ref[...] = own[zz].astype(wide) + crossed[zz].astype(wide)

                @pl.when(z > 0)
                def _():
                    rise(zz).wait_recv()
                    sum_ref[...] += from_low[zz].astype(wide)

                @pl.when(z < last)
                def _():
                    sink(zz).wait_recv()
                    sum_ref[...] += from_high[zz].astype(wide)

        lax.fori_loop(depth, 2 * depth, own_step, 0)

        def slab_step(e, carry):
            for k in range(1, depth):
                @pl.when(e == 4 * per * (k - 1) // (depth - 2))
                def _():
                    chain(place(depth + k)[0])

            @pl.when(e < 4 * per)
            def _():
                weight_slab(e)

            return carry

        lax.fori_loop(0, 4 * per + 1, slab_step, 0)
        for e in (4 * per - 2, 4 * per - 1):
            keep(e, 1).wait()

        def settle(zz, carry):
            cross(zz).wait_send()

            @pl.when(zz > z)
            def _():
                rise(zz).wait_send()

            @pl.when(zz < z)
            def _():
                sink(zz).wait_send()

            return carry

        lax.fori_loop(0, depth, settle, 0)

    vmem = pl.BlockSpec(memory_space=pltpu.VMEM)
    hbm = pl.BlockSpec(memory_space=pl.ANY)
    total, gate_half, up_half = pl.pallas_call(
        kernel,
        in_specs=[hbm, hbm, hbm, hbm, vmem, vmem, vmem],
        out_specs=[vmem] + [hbm] * 2,
        out_shape=[
            jax.ShapeDtypeStruct((rows, model), jnp.float32),
            jax.ShapeDtypeStruct((per, slab, hidden), low),
            jax.ShapeDtypeStruct((per, slab, hidden), low),
        ],
        scratch_shapes=[
            pltpu.VMEM((2, rows, model), low),
            pltpu.VMEM((2, rows, hidden), jnp.float32),
            pltpu.VMEM((2, rows, hidden), jnp.float32),
            pltpu.VMEM((wide_count, rows, hidden), low),
            pltpu.VMEM((wide_count, rows, hidden), low),
        ]
        + [pltpu.VMEM((depth, rows, model), low)] * 5
        + [
            pltpu.VMEM((2, wide_count, rows, slab), low),
            pltpu.VMEM((2, slab, hidden), low),
            pltpu.VMEM((2, per, slab, hidden), low),
            pltpu.VMEM((2, slab, hidden), low),
            pltpu.SemaphoreType.DMA((3, 2)),
        ]
        + [pltpu.SemaphoreType.DMA((depth,))] * 5
        + [
            pltpu.SemaphoreType.DMA((2,)),
            pltpu.SemaphoreType.DMA((2,)),
            pltpu.SemaphoreType.DMA((2, per)),
            pltpu.SemaphoreType.DMA((2,)),
        ],
        compiler_params=pltpu.CompilerParams(
            collective_id=collective_id, has_side_effects=True, vmem_limit_bytes=67043328
        ),
        name="backward_scattered",
    )(
        cot.reshape(wide_count, rows, model),
        gates.reshape(wide_count, rows, hidden),
        ups.reshape(wide_count, rows, hidden),
        hidden_rows.reshape(wide_count, rows, model),
        gate_weight, up_weight, down_weight,
    )
    return total, gate_half.reshape(half, hidden), up_half.reshape(half, hidden)


AXES = ("narrow", "wide")


def peers(k, counts, act):
    here = lax.axis_index(AXES[k])

    def one(step, carry):
        act((here + step) % counts[k])
        return carry

    lax.fori_loop(1, counts[k], one, 0)


def greet_all(counts):
    barrier = pltpu.get_barrier_semaphore()
    for k, axis in enumerate(AXES):
        peers(k, counts, lambda who: pl.semaphore_signal(
            barrier, inc=1, device_id={axis: who}, device_id_type=MESH))
    return lambda: pl.semaphore_wait(barrier, counts[0] + counts[1] - 2)


class Exchange:
    def __init__(self, k, counts, source, slots, sends, recvs):
        self.k, self.counts, self.source = k, counts, source
        self.slots, self.sends, self.recvs = slots, sends, recvs
        self.here = lax.axis_index(AXES[k])

    def copy(self, who, slot):
        return pltpu.make_async_remote_copy(
            src_ref=self.source, dst_ref=self.slots.at[slot],
            send_sem=self.sends.at[who], recv_sem=self.recvs.at[slot],
            device_id={AXES[self.k]: who}, device_id_type=MESH,
        )

    def start(self):
        peers(self.k, self.counts, lambda who: self.copy(who, self.here).start())
        self.slots[self.here] = self.source[...]

    def total(self):
        peers(self.k, self.counts, lambda who: self.copy(who, who).wait_recv())
        sums = self.slots[0]
        for n in range(1, self.counts[self.k]):
            sums = sums + self.slots[n]
        return sums

    def settle(self):
        peers(self.k, self.counts, lambda who: self.copy(who, self.here).wait_send())


def exchange_scratch(shape, counts):
    return [
        pltpu.VMEM(shape, jnp.float32),
        pltpu.VMEM((2, max(counts)) + shape, jnp.float32),
        pltpu.VMEM(shape, jnp.float32),
        pltpu.SemaphoreType.DMA,
        pltpu.SemaphoreType.DMA((counts[0],)),
        pltpu.SemaphoreType.DMA((counts[0],)),
        pltpu.SemaphoreType.DMA((counts[1],)),
        pltpu.SemaphoreType.DMA((counts[1],)),
    ]


def exchange_pair(counts, mine, held, total, narrow_send, narrow_recv, wide_send, wide_recv):
    return (
        Exchange(0, counts, mine, held.at[0], narrow_send, narrow_recv),
        Exchange(1, counts, total, held.at[1], wide_send, wide_recv),
    )


def sum_everywhere(values, counts, collective_id, strip=None):
    extra = [] if strip is None else [strip]

    def kernel(in_ref, *refs):
        strip_refs, refs = refs[: len(extra)], refs[len(extra) :]
        out_ref, refs = refs[0], refs[1:]
        gathered_refs, refs = refs[: len(extra)], refs[len(extra) :]
        mine, held, total, load_sem, narrow_send, narrow_recv, wide_send, wide_recv, *rest = refs
        load = pltpu.make_async_copy(in_ref, mine, load_sem)
        load.start()
        arrive = greet_all(counts)
        me = lax.axis_index("narrow")
        if extra:
            strips, strip_sem, strip_send, strip_recv = rest
            own = pltpu.make_async_copy(strip_refs[0], strips.at[me], strip_sem)
            own.start()
            own.wait()

        def strip_copy(who, slot):
            return pltpu.make_async_remote_copy(
                src_ref=strips.at[me], dst_ref=strips.at[slot],
                send_sem=strip_send.at[who], recv_sem=strip_recv.at[slot],
                device_id={"narrow": who}, device_id_type=MESH,
            )

        load.wait()
        arrive()
        narrow, wide = exchange_pair(
            counts, mine, held, total, narrow_send, narrow_recv, wide_send, wide_recv
        )
        narrow.start()
        if extra:
            peers(0, counts, lambda who: strip_copy(who, me).start())
        total[...] = narrow.total()
        wide.start()
        out_ref[...] = wide.total()
        narrow.settle()
        wide.settle()
        if extra:
            peers(0, counts, lambda who: strip_copy(who, who).wait_recv())
            gathered_refs[0][...] = strips[...]
            peers(0, counts, lambda who: strip_copy(who, me).wait_send())

    vmem, hbm = pl.BlockSpec(memory_space=pltpu.VMEM), pl.BlockSpec(memory_space=pl.ANY)
    out_shape = [jax.ShapeDtypeStruct(values.shape, jnp.float32)]
    scratch = exchange_scratch(values.shape, counts)
    if extra:
        whole = (counts[0],) + strip.shape
        out_shape += [jax.ShapeDtypeStruct(whole, strip.dtype)]
        scratch += [
            pltpu.VMEM(whole, strip.dtype),
            pltpu.SemaphoreType.DMA,
            pltpu.SemaphoreType.DMA((counts[0],)),
            pltpu.SemaphoreType.DMA((counts[0],)),
        ]
    results = pl.pallas_call(
        kernel,
        in_specs=[hbm] * (1 + len(extra)),
        out_specs=[vmem] * (1 + len(extra)),
        out_shape=out_shape,
        scratch_shapes=scratch,
        compiler_params=pltpu.CompilerParams(collective_id=collective_id, has_side_effects=True),
        name="sum_everywhere",
    )(values, *extra)
    if not extra:
        return results[0]
    return results[0], results[1].reshape(-1, strip.shape[1])


def greet_wide(counts, partners=()):
    barrier = pltpu.get_barrier_semaphore()
    peers(1, counts, lambda who: pl.semaphore_signal(
        barrier, inc=1, device_id={"wide": who}, device_id_type=MESH))
    for partner in partners:
        pl.semaphore_signal(
            barrier, inc=1, device_id={"narrow": partner}, device_id_type=MESH
        )
    pl.semaphore_wait(barrier, counts[1] - 1 + len(partners))


class Blocks:
    def __init__(self, counts, blocks, held, sends, recvs):
        self.counts, self.blocks, self.held = counts, blocks, held
        self.sends, self.recvs = sends, recvs
        self.me = lax.axis_index("wide")

    def copy(self, who, slot):
        return pltpu.make_async_remote_copy(
            src_ref=self.blocks.at[who], dst_ref=self.held.at[slot],
            send_sem=self.sends.at[who], recv_sem=self.recvs.at[slot],
            device_id={"wide": who}, device_id_type=MESH,
        )

    def start(self, who):
        self.copy(who, self.me).start()

    def each(self, act):
        peers(1, self.counts, act)

    def arrived(self, who):
        self.copy(who, who).wait_recv()

    def settle(self):
        self.each(lambda who: self.copy(who, self.me).wait_send())


def carry_over(source, target, sems):
    across = (lax.axis_index("narrow") + 2) % 4
    return pltpu.make_async_remote_copy(
        src_ref=source, dst_ref=target, send_sem=sems.at[0], recv_sem=sems.at[1],
        device_id={"narrow": across}, device_id_type=MESH,
    )


VMEM_SPEC = pl.BlockSpec(memory_space=pltpu.VMEM)
HBM_SPEC = pl.BlockSpec(memory_space=pl.ANY)


def mix_and_project(mixed, output_full, counts, collective_id):
    wide_count = counts[1]
    rows, width = mixed.shape[0] // wide_count, mixed.shape[1]
    model = output_full.shape[1]
    tile = min(512, model)

    def kernel(mixed_ref, weight_ref, out_ref, held_ref, sends, recvs):
        blocks = Blocks(counts, mixed_ref, held_ref, sends, recvs)
        greet_wide(counts)
        blocks.each(blocks.start)
        held_ref[blocks.me] = mixed_ref[blocks.me]

        def add(who, first):
            rows_in = held_ref[who]

            def one(t, carry):
                at = pl.ds(pl.multiple_of(t * tile, tile), tile)
                part = jnp.dot(
                    rows_in, weight_ref[pl.ds(pl.multiple_of(who * width, width), width), at],
                    preferred_element_type=jnp.float32,
                )
                out_ref[:, at] = part if first else out_ref[:, at] + part
                return carry

            lax.fori_loop(0, model // tile, one, 0)

        add(blocks.me, True)

        def later(who):
            blocks.arrived(who)
            add(who, False)

        blocks.each(later)
        blocks.settle()

    return pl.pallas_call(
        kernel,
        in_specs=[VMEM_SPEC, VMEM_SPEC],
        out_specs=[VMEM_SPEC, VMEM_SPEC],
        out_shape=[
            jax.ShapeDtypeStruct((rows, model), jnp.float32),
            jax.ShapeDtypeStruct((wide_count, rows, width), mixed.dtype),
        ],
        scratch_shapes=[pltpu.SemaphoreType.DMA((wide_count,))] * 2,
        compiler_params=pltpu.CompilerParams(
            collective_id=collective_id, has_side_effects=True, vmem_limit_bytes=32 << 20
        ),
        name="mix_and_project",
    )(mixed.reshape(wide_count, rows, width), output_full)


def unmix(middle_low, output_full, mixed_blocks, carried, counts, collective_id):
    wide_count = counts[1]
    rows, model = middle_low.shape
    width = mixed_blocks.shape[2]
    strip = width // 4
    low = jnp.bfloat16

    def kernel(
        middle_ref, weight_ref, mixed_ref, carried_ref, held_ref, half_ref, swapped_ref,
        made, product, own, given, taken, sends, recvs, give_send, give_recv, carry_sems,
    ):
        blocks = Blocks(counts, made, held_ref, sends, recvs)
        narrow = lax.axis_index("narrow")
        core = narrow % 2
        partner = narrow + 1 - 2 * core
        greet_wide(counts, (partner, (narrow + 2) % 4))
        carry = carry_over(carried_ref, swapped_ref, carry_sems)
        carry.start()

        def make(who):
            made[who] = nt(
                middle_ref[...], weight_ref[pl.ds(pl.multiple_of(who * width, width), width), :]
            ).astype(low)

        def make_and_start(who):
            make(who)
            blocks.start(who)

        blocks.each(make_and_start)
        make(blocks.me)
        held_ref[blocks.me] = made[blocks.me]

        def give(w):
            return pltpu.make_async_remote_copy(
                src_ref=given.at[w], dst_ref=taken.at[w],
                send_sem=give_send.at[w], recv_sem=give_recv.at[w],
                device_id={"narrow": partner}, device_id_type=MESH,
            )

        def multiply(w, state):
            product[...] = tn(mixed_ref[w], middle_ref[...])
            for y in range(2):
                at = pl.multiple_of((2 * y + 1 - core) * strip, strip)
                given[w, y] = product[pl.ds(at, strip), :].astype(low)
                at = pl.multiple_of((2 * y + core) * strip, strip)
                own[w, y] = product[pl.ds(at, strip), :]
            give(w).start()
            return state

        def collect(w, state):
            give(w).wait_recv()
            for y in range(2):
                half_ref[y, w] = (own[w, y] + taken[w, y].astype(jnp.float32)).astype(low)
            return state

        lax.fori_loop(0, wide_count, multiply, 0)
        lax.fori_loop(0, wide_count, collect, 0)
        blocks.each(blocks.arrived)
        blocks.settle()
        lax.fori_loop(0, wide_count, lambda w, state: (give(w).wait_send(), state)[1], 0)
        carry.wait()

    held, half, swapped = pl.pallas_call(
        kernel,
        in_specs=[VMEM_SPEC] * 3 + [HBM_SPEC],
        out_specs=[VMEM_SPEC] * 2 + [HBM_SPEC],
        out_shape=[
            jax.ShapeDtypeStruct((wide_count, rows, width), low),
            jax.ShapeDtypeStruct((2, wide_count, strip, model), low),
            jax.ShapeDtypeStruct(carried.shape, low),
        ],
        scratch_shapes=[
            pltpu.VMEM((wide_count, rows, width), low),
            pltpu.VMEM((width, model), jnp.float32),
            pltpu.VMEM((wide_count, 2, strip, model), jnp.float32),
            pltpu.VMEM((wide_count, 2, strip, model), low),
            pltpu.VMEM((wide_count, 2, strip, model), low),
        ]
        + [pltpu.SemaphoreType.DMA((wide_count,))] * 4
        + [pltpu.SemaphoreType.DMA((2,))],
        compiler_params=pltpu.CompilerParams(
            collective_id=collective_id, has_side_effects=True, vmem_limit_bytes=48 << 20
        ),
        name="unmix",
    )(middle_low, output_full, mixed_blocks, carried)
    return (
        held.reshape(wide_count * rows, width),
        half.reshape(2, wide_count * strip, model),
        swapped,
    )


def return_and_project(
    grads, hidden_rows, query_turned, key_weight, value_weight, carried, counts, collective_id
):
    wide_count = counts[1]
    rows, columns = grads.shape[0] // wide_count, grads.shape[1]
    model = query_turned.shape[1]
    width = query_turned.shape[0] // wide_count
    head = (columns - width) // 2
    tile = min(512, model)
    slab = min(256, model // 2)
    per = model // 2 // slab
    low = jnp.bfloat16

    def kernel(
        grads_ref, hidden_ref, query_ref, key_ref, value_ref, carried_ref,
        out_ref, weight_ref, swapped_ref,
        held, slabs, query_all, key_all, value_all, given, taken, halves, whole,
        sends, recvs, slab_sems, give_send, give_recv, half_sems, carry_sems,
    ):
        blocks = Blocks(counts, grads_ref, held, sends, recvs)
        narrow = lax.axis_index("narrow")
        core = narrow % 2
        partner, across = narrow + 1 - 2 * core, (narrow + 2) % 4

        def row_of(t):
            return pl.multiple_of((jnp.where(t < per, 1 - core, core) * per + t % per) * slab, slab)

        def load(t):
            at = pl.ds(row_of(t), slab)
            return pltpu.make_async_copy(hidden_ref.at[:, :, at], slabs.at[t % 2], slab_sems.at[t % 2])

        load(0).start()
        greet_wide(counts, (partner, across))
        blocks.each(blocks.start)
        carry = carry_over(carried_ref, swapped_ref, carry_sems)
        held[blocks.me] = grads_ref[blocks.me]

        def give(n):
            return pltpu.make_async_remote_copy(
                src_ref=given.at[n], dst_ref=taken.at[n],
                send_sem=give_send.at[n], recv_sem=give_recv.at[n],
                device_id={"narrow": partner}, device_id_type=MESH,
            )

        exchange = pltpu.make_async_remote_copy(
            src_ref=halves.at[0], dst_ref=halves.at[1],
            send_sem=half_sems.at[0], recv_sem=half_sems.at[1],
            device_id={"narrow": across}, device_id_type=MESH,
        )
        hand_over = pltpu.make_async_remote_copy(
            src_ref=whole.at[core], dst_ref=whole.at[core],
            send_sem=half_sems.at[2], recv_sem=half_sems.at[3],
            device_id={"narrow": partner}, device_id_type=MESH,
        )

        def weigh(t, state):
            load(t).wait()

            @pl.when(t + 1 < 2 * per)
            def _():
                load(t + 1).start()

            value = tn(
                slabs[t % 2].reshape(wide_count * rows, slab),
                grads_ref[...].reshape(wide_count * rows, columns),
            )
            n = t % per

            @pl.when(t < per)
            def _():
                given[n] = value.astype(low)
                give(n).start()

            @pl.when(t >= per)
            def _():
                give(n).wait_recv()
                halves[0, n] = (value + taken[n].astype(jnp.float32)).astype(low)

            return state

        lax.fori_loop(0, 2 * per, weigh, 0)
        exchange.start()
        carry.start()
        blocks.each(blocks.arrived)
        exchange.wait()
        whole[core] = (halves[0].astype(jnp.float32) + halves[1].astype(jnp.float32)).astype(low)
        hand_over.start()
        for w in range(wide_count):
            query_all[:, w * width : (w + 1) * width] = held[w, :, :width]
        key_all[...] = jnp.concatenate(
            [held[w, :, width : width + head] for w in range(wide_count)], axis=1
        )
        value_all[...] = jnp.concatenate(
            [held[w, :, width + head :] for w in range(wide_count)], axis=1
        )

        def one(t, state):
            at = pl.ds(pl.multiple_of(t * tile, tile), tile)
            out_ref[:, at] = (
                jnp.dot(query_all[...], query_ref[:, at], preferred_element_type=jnp.float32)
                + nt(key_all[...], key_ref[at, :])
                + nt(value_all[...], value_ref[at, :])
            )
            return state

        lax.fori_loop(0, model // tile, one, 0)
        hand_over.wait()
        weight_ref[...] = whole[...].reshape(model, columns).astype(jnp.float32)
        blocks.settle()
        lax.fori_loop(0, per, lambda n, state: (give(n).wait_send(), state)[1], 0)
        carry.wait()

    return pl.pallas_call(
        kernel,
        in_specs=[VMEM_SPEC, HBM_SPEC] + [VMEM_SPEC] * 3 + [HBM_SPEC],
        out_specs=[VMEM_SPEC] * 2 + [HBM_SPEC],
        out_shape=[
            jax.ShapeDtypeStruct((rows, model), jnp.float32),
            jax.ShapeDtypeStruct((model, columns), jnp.float32),
            jax.ShapeDtypeStruct(carried.shape, low),
        ],
        scratch_shapes=[
            pltpu.VMEM((wide_count, rows, columns), low),
            pltpu.VMEM((2, wide_count, rows, slab), low),
            pltpu.VMEM((rows, wide_count * width), low),
            pltpu.VMEM((rows, wide_count * head), low),
            pltpu.VMEM((rows, wide_count * head), low),
            pltpu.VMEM((per, slab, columns), low),
            pltpu.VMEM((per, slab, columns), low),
            pltpu.VMEM((2, per, slab, columns), low),
            pltpu.VMEM((2, per, slab, columns), low),
            pltpu.SemaphoreType.DMA((wide_count,)),
            pltpu.SemaphoreType.DMA((wide_count,)),
            pltpu.SemaphoreType.DMA((2,)),
            pltpu.SemaphoreType.DMA((per,)),
            pltpu.SemaphoreType.DMA((per,)),
            pltpu.SemaphoreType.DMA((4,)),
            pltpu.SemaphoreType.DMA((2,)),
        ],
        compiler_params=pltpu.CompilerParams(
            collective_id=collective_id, has_side_effects=True, vmem_limit_bytes=48 << 20
        ),
        name="return_and_project",
    )(
        grads.reshape(wide_count, rows, columns),
        hidden_rows.reshape(wide_count, rows, model),
        query_turned, key_weight, value_weight,
        carried,
    )

CORPORA = 8
GATHER_BYTES = 8 << 20


def norm_scale(values, scale_gain):
    return (
        values * lax.rsqrt(jnp.mean(values * values, axis=-1, keepdims=True) + epsilon) * scale_gain
    )


def contract_first(left, right):
    return lax.dot_general(
        left, right, (((0,), (0,)), ((), ())), preferred_element_type=jnp.float32
    )


def gather_wide(values):
    return lax.all_gather(values, "wide", axis=0, tiled=True)


def scatter_wide(values):
    return lax.psum_scatter(
        values.astype(jnp.bfloat16), "wide", scatter_dimension=0, tiled=True
    ).astype(jnp.float32)


def own_part(values, axis, index, count):
    size = values.shape[axis] // count
    return lax.dynamic_slice_in_dim(values, index * size, size, axis)


def swap_narrow(values, bit):
    count = lax.axis_size("narrow")
    return lax.ppermute(values, "narrow", [(i, i ^ bit) for i in range(count)])


def keep_half(values, axis, bit):
    side = lax.axis_index("narrow") // bit % 2
    mine = lax.dynamic_index_in_dim(values, side, axis, keepdims=False)
    other = lax.dynamic_index_in_dim(values, 1 - side, axis, keepdims=False)
    return add_low(mine, swap_narrow(other, bit))


def add_low(left, right):
    return (left.astype(jnp.float32) + right.astype(jnp.float32)).astype(jnp.bfloat16)


def core_half(values):
    rows, columns = values.shape
    return keep_half(values.astype(jnp.bfloat16).reshape(2, rows // 2, columns), 0, 1)


def sum_narrow(values):
    half = core_half(values)
    return hand_back(add_low(half, swap_narrow(half, 2)))


def hand_back(half):
    other = swap_narrow(half, 1)
    first = lax.axis_index("narrow") % 2 == 0
    return jnp.concatenate(
        [jnp.where(first, half, other), jnp.where(first, other, half)], axis=0
    ).astype(jnp.float32)


def swiglu_back(act_grad, gate_values, up_values):
    sigmoid_gate = lax.logistic(gate_values)
    gate_part = act_grad * up_values * sigmoid_gate * (1.0 + gate_values * (1.0 - sigmoid_gate))
    up_part = act_grad * gate_values * sigmoid_gate
    return (gate_part.astype(jnp.bfloat16), up_part.astype(jnp.bfloat16))


def shards(
    tokens,
    attention_gain,
    query_weight,
    key_weight,
    value_weight,
    query_gain,
    key_gain,
    output_weight,
    feedforward_gain,
    gate_weight,
    up_weight,
    down_weight,
    cotangent,
    corpus_tags,
    segments,
):
    low, wide_type = jnp.bfloat16, jnp.float32
    head_size = query_gain.shape[0]
    own_rows, model_width = tokens.shape
    wide_count, narrow_count = lax.axis_size("wide"), lax.axis_size("narrow")
    counts = (narrow_count, wide_count)
    wide_index, narrow_index = lax.axis_index("wide"), lax.axis_index("narrow")
    key_total = key_weight.shape[1] // head_size
    width = query_weight.shape[1]
    key_head = wide_index * key_total // wide_count
    all_rows = own_rows * wide_count
    chained = wide_count == key_total and narrow_count == 4 and all_rows * model_width * 2 <= GATHER_BYTES

    tag_hits = corpus_tags[:, None] == jnp.arange(CORPORA, dtype=jnp.int32)[None, :]
    local_counts = jnp.sum(tag_hits.astype(wide_type), axis=0)
    local_counts = jnp.pad(local_counts[None], ((0, 7), (0, 128 - CORPORA)))
    token_values = tokens.astype(wide_type)
    first_gain = attention_gain.astype(wide_type)
    second_gain = feedforward_gain.astype(wide_type)

    key_columns = lax.dynamic_slice_in_dim(key_weight, key_head * head_size, head_size, 1)
    value_columns = lax.dynamic_slice_in_dim(value_weight, key_head * head_size, head_size, 1)
    own_weights = jnp.concatenate([query_weight, key_columns, value_columns], axis=1)
    strip = width // narrow_count
    strips = [
        own_part(output_weight, 0, narrow_index, narrow_count),
        jnp.transpose(own_part(query_weight, 1, narrow_index, narrow_count)),
    ]
    hidden_local = norm_scale(token_values, first_gain).astype(low)
    if chained:
        hidden_one, raw, corpus_counts, gathered = project_gathered(
            hidden_local, own_weights, local_counts, strips, counts, 2
        )
    else:
        hidden_one = gather_wide(hidden_local)
        raw = dot_nn(hidden_one, own_weights)
        corpus_counts = sum_everywhere(local_counts, counts, 1)
        gathered = [lax.all_gather(part, ("wide", "narrow"), axis=0, tiled=True) for part in strips]
    output_full, query_turned = gathered
    corpus_counts = corpus_counts[0, :CORPORA]
    corpus_scale = jnp.sqrt(jnp.sum(corpus_counts) / (CORPORA * corpus_counts))
    row_weight = jnp.sum(jnp.where(tag_hits, corpus_scale[None, :], 0.0), axis=1)
    out_cot = cotangent.astype(wide_type) * row_weight[:, None]
    cot_low, raw = lax.optimization_barrier((out_cot.astype(low), raw))
    cot_low = gather_wide(cot_low)

    first_block = first_blocks(segments)
    saved = attention_forward(raw, query_gain, key_gain, segments, first_block)
    if chained:
        branch, mixed = mix_and_project(saved[0], output_full, counts, 6)
        middle = token_values + branch
    else:
        mixed = lax.all_to_all(saved[0], "wide", split_axis=0, concat_axis=1, tiled=True)
        middle = token_values + dot_nn(mixed, output_full)

    together = lax.optimization_barrier
    hidden_two_local = norm_scale(middle, second_gain).astype(low)
    if chained:
        hidden_two, gate_values, up_values, activated, down_part = forward_gathered(
            hidden_two_local, gate_weight, up_weight, down_weight, wide_count, 3
        )
        hidden_two_grad, gate_half, up_half = backward_scattered(
            cot_low, gate_values, up_values, hidden_two, gate_weight, up_weight, down_weight,
            wide_count, 4,
        )
        down_part, hidden_two_grad = together((down_part, hidden_two_grad))
    else:
        hidden_two = gather_wide(hidden_two_local)
        gate_values = dot_nn(hidden_two, gate_weight)
        up_values = dot_nn(hidden_two, up_weight)
        activated = (gate_values * lax.logistic(gate_values) * up_values).astype(low)
        down_part = dot_nn(activated, down_weight)
        gate_low, up_low = swiglu_back(dot_nt(cot_low, down_weight), gate_values, up_values)
        hidden_two_grad = scatter_wide(dot_nt(gate_low, gate_weight) + dot_nt(up_low, up_weight))
        gate_half = core_half(contract_first(hidden_two, gate_low))
        up_half = core_half(contract_first(hidden_two, up_low))
        gate_other = swap_narrow(gate_half, 2)
    down_sum = scatter_wide(down_part)

    _, second_pull = jax.vjp(norm_scale, middle, second_gain)
    middle_part, second_gain_grad = second_pull(hidden_two_grad)
    middle_grad = out_cot + middle_part
    middle_low = middle_grad.astype(low)
    if chained:
        mixed_grad, output_part, gate_other = unmix(
            middle_low, output_full, mixed, gate_half, counts, 7
        )
    else:
        mixed_grad = lax.all_to_all(
            dot_nt(middle_low, output_full).astype(low), "wide", split_axis=1, concat_axis=0, tiled=True
        )
        mixed = mixed.reshape(own_rows, wide_count, narrow_count, strip).transpose(0, 2, 1, 3)
        output_part = contract_first(mixed.reshape(own_rows, wide_count * width), middle_low)
        output_part = output_part.astype(low).reshape(2, 2, wide_count * strip, model_width)
        output_part = keep_half(output_part, 1, 1)
    mixed_grad, output_part, activated, up_half = together(
        (mixed_grad, output_part, activated, up_half)
    )
    output_part = keep_half(output_part, 0, 2)
    down_half = core_half(contract_first(activated, cot_low))
    mixed_grad, down_half = together((mixed_grad, down_half))
    up_half = add_low(up_half, swap_narrow(up_half, 2))
    gate_grad = hand_back(add_low(gate_half, gate_other))
    grads, query_gain_grad, key_gain_grad = attention_backward(
        raw, query_gain, key_gain, segments, first_block, saved, mixed_grad
    )
    grads, up_half, gate_grad = together((grads, up_half, gate_grad))
    grads, output_part, up_grad, down_sum = together(
        (grads, output_part, hand_back(up_half), down_sum)
    )
    output_part = lax.psum_scatter(output_part, "wide", scatter_dimension=0, tiled=True)
    shared = wide_count // key_total
    if chained:
        hidden_one_grad, weight_sums, down_other = return_and_project(
            grads, hidden_one, query_turned, key_weight, value_weight, down_half, counts, 8
        )
    else:
        down_other = swap_narrow(down_half, 2)
        weight_grads = contract_first(hidden_one, grads)
        sent = lax.all_to_all(grads, "wide", split_axis=0, concat_axis=1, tiled=True).reshape(
            own_rows, wide_count, width + 2 * head_size
        )

        def key_side(start):
            part = sent[:, :, start : start + head_size]
            if shared > 1:
                part = jnp.sum(
                    part.astype(wide_type).reshape(own_rows, key_total, shared, head_size), axis=2
                ).astype(low)
            return part.reshape(own_rows, key_total * head_size)

        hidden_one_grad = (
            dot_nn(sent[:, :, :width].reshape(own_rows, wide_count * width), query_turned)
            + dot_nt(key_side(width), key_weight)
            + dot_nt(key_side(width + head_size), value_weight)
        )
    hidden_one_grad, output_part = together((hidden_one_grad, output_part))
    down_grad = hand_back(add_low(down_half, down_other))
    _, first_pull = jax.vjp(norm_scale, token_values, first_gain)
    token_part, first_gain_grad = first_pull(hidden_one_grad)
    tokens_gradient = (middle_grad + token_part).astype(low)
    tokens_gradient, down_sum = lax.optimization_barrier((tokens_gradient, down_sum))
    result = (middle + down_sum).astype(low)

    if shared == 1:
        if not chained:
            weight_sums = sum_narrow(weight_grads)
        key_weight_grad = weight_sums[:, width : width + head_size]
        value_weight_grad = weight_sums[:, width + head_size :]
    else:
        weight_sums = sum_narrow(weight_grads[:, :width])

        def spread(part):
            whole = jnp.zeros((model_width, key_total * head_size), wide_type)
            whole = lax.dynamic_update_slice_in_dim(whole, part, key_head * head_size, 1)
            share = lax.psum_scatter(whole.astype(low), "wide", scatter_dimension=1, tiled=True)
            return lax.psum(share, "narrow").astype(wide_type)

        key_weight_grad = spread(weight_grads[:, width : width + head_size])
        value_weight_grad = spread(weight_grads[:, width + head_size :])

    gain_parts = jnp.concatenate([first_gain_grad, second_gain_grad, query_gain_grad, key_gain_grad])
    lines = -(-gain_parts.shape[0] // 1024) * 8
    gain_parts = jnp.pad(gain_parts, (0, lines * 128 - gain_parts.shape[0])).reshape(lines, 128)
    gains, output_grad = sum_everywhere(gain_parts, counts, 5, output_part)
    gains, output_grad = gains.reshape(-1), output_grad.astype(wide_type)
    starts = (0, model_width, 2 * model_width, 2 * model_width + head_size)
    sizes = (model_width, model_width, head_size, head_size)
    first_out, second_out, query_gain_out, key_gain_out = (
        own_part(gains[start : start + size], 0, wide_index, wide_count)
        for start, size in zip(starts, sizes)
    )
    return (
        result,
        tokens_gradient,
        first_out,
        weight_sums[:, :width],
        key_weight_grad,
        value_weight_grad,
        query_gain_out,
        key_gain_out,
        output_grad,
        second_out,
        gate_grad,
        up_grad,
        down_grad,
    )


def solution(mesh):
    rows = P(("narrow", "wide"), None)
    columns, first = P(None, "wide"), P("wide", None)
    return jax.shard_map(
        shards,
        mesh=mesh,
        in_specs=(
            rows, P(), columns, P(), P(), P(), P(), first, P(), columns, columns, first,
            rows, P(("narrow", "wide")), P("narrow", None),
        ),
        out_specs=(
            rows, rows, P("wide"), columns, columns, columns, P("wide"), P("wide"),
            first, P("wide"), columns, columns, first,
        ),
        check_vma=False,
    )
```
